256 devices in a mesh: out: 32 (over z, x_hi, core), in: 8 (over y, x_lo).
Axes of the slice: x: 4 (x_hi: 2, x_lo: 2; x = x_hi * 2 + x_lo), y: 4, z: 8, core: 2. Of those that a mesh axis runs over, the one named last changes fastest.
Arguments:
- basis_out: bfloat16 [16384, 16384], P('in', 'out'), may hold values from -0.046875 to 0.046875
- corrected: float32 [16384, 26624], P('out', 'in'), may hold values from 0.5 to 2
- factor_table: float32 [32, 1664], replicated, may hold values from 0.5 to 2
- block_ids: int32 [16], replicated, may hold values from 0 to 31, as said below
- basis_in: bfloat16 [16, 1664, 1664], P('in', 'out'), may hold values from -0.15625 to 0.15625
- query_ids: int32 [4], replicated, may hold values from 0 to 5
- u_pool: bfloat16 [6, 16384, 64], P(None, 'in'), may hold values from -0.75 to 0.75
- v_pool: bfloat16 [6, 26624, 64], P(None, 'in'), may hold values from -6 to 6
- train_ids: int32 [4], replicated, may hold values from 0 to 7
- x_pool: bfloat16 [8, 32, 26624], P(None, 'out', 'in'), may hold values from -0.0390625 to 0.0390625
- delta_pool: bfloat16 [8, 32, 128], P(None, 'out'), may hold values from -0.09375 to 0.09375
Outputs:
- tiles: bfloat16 [4, 128, 26624], P(None, 'out', 'in')
- scores: float32 [4, 4], replicated
The draws below stay inside these ranges and needn't reach their ends.
Inputs may be any that keep to these rules, and one draw needn't show every extreme that they name: `block_ids`: the 16 entries are distinct.
All inputs are finite; a program needn't handle non-finite values.
Results may differ from the reference program's by a relative error of at most 0.023.
Values may be sent and summed in bfloat16 or wider, within the bound.
No kernel may reach another device: no remote copies, remote signals or barrier semaphores. Data moves between devices by JAX's collectives and lax.ppermute only.
A program may use at most 128 MiB of HBM per device.

```python
import math
import jax
import jax.numpy as jnp
from jax import lax

OUT = 16384
EB = 1664
NB = 16
POOL_BLOCKS = 32
RANK = 64
QUERIES = 4
QPOOL = 6
TRAIN = 4
TPOOL = 8
BLOCK_ROWS = 32
WIN_ROWS = 16
IN_SEL = 26624
OUT_WIN = 128
N_IN = 8


def draw_block_ids(key, part):
    order = jax.random.permutation(jax.random.fold_in(key, 17), POOL_BLOCKS)
    return order[:NB].astype(jnp.int32)


def touch_ends(entries, stream_key, low, high):
    extent = entries.shape
    spot = [jax.random.randint(jax.random.fold_in(stream_key, axis), (), 0, extent[axis]) for axis in range(len(extent))]
    entries = entries.at[tuple(spot)].set(low)
    longest = extent.index(max(extent))
    spot[longest] = (spot[longest] + 1) % extent[longest]
    return entries.at[tuple(spot)].set(high)


def block_scale(key, dims, pieces, low, largest):
    loudness = 1.0
    for axis_at, shards_of in pieces:
        heights = jax.random.uniform(jax.random.fold_in(jax.random.fold_in(key, 6), axis_at), (shards_of,), jnp.float32, low / len(pieces), largest / len(pieces))
        loudness = loudness * jnp.repeat(jnp.exp(heights), dims[axis_at] // shards_of).reshape((-1,) + (1,) * (len(dims) - 1 - axis_at))
    return loudness


def noise(rng, shape, deviation, most, cuts=(), kind=jnp.bfloat16):
    result = jax.random.normal(rng, shape, jnp.float32) * deviation
    if len(cuts) > 0:
        result = block_scale(rng, shape, cuts, -0.22, 0.18) * result
    return jnp.clip(result, min=-most, max=most).astype(kind)


def setup_inputs(seed: int = 0) -> dict:
    arg_keys = jax.random.split(jax.random.key(seed), 12)
    basis_out = noise(arg_keys[0], (OUT, OUT), OUT ** -0.5, 0.046875, ((0, 8), (1, 32)))
    corrected = jnp.clip(jnp.exp(math.log(2.0) - 1.3862944 * jax.random.uniform(arg_keys[1], (OUT, IN_SEL), jnp.float32) ** block_scale(arg_keys[1], (OUT, IN_SEL), ((0, 32), (1, 8)), -0.2, 0.2)), 0.5, 2.0)
    factor_table = jnp.clip(jnp.exp(jax.random.uniform(arg_keys[2], (POOL_BLOCKS, EB), jnp.float32, math.log(0.5), math.log(2.0))), 0.5, 2.0)
    block_ids = draw_block_ids(jax.random.fold_in(arg_keys[11], 71), 0)
    basis_in = noise(arg_keys[4], (NB, EB, EB), EB ** -0.5, 0.15625, ((0, 8), (1, 32)))
    query_ids = touch_ends(jax.random.randint(arg_keys[5], (QUERIES,), 0, QPOOL), jax.random.fold_in(arg_keys[5], 1), 0, QPOOL - 1).astype(jnp.int32)
    u_pool = noise(arg_keys[6], (QPOOL, OUT, RANK), RANK ** -0.5, 0.75, ((1, 8),))
    v_pool = noise(arg_keys[7], (QPOOL, IN_SEL, RANK), 1.0, 6.0, ((1, 8),))
    train_ids = touch_ends(jax.random.randint(arg_keys[8], (TRAIN,), 0, TPOOL), jax.random.fold_in(arg_keys[8], 1), 0, TPOOL - 1).astype(jnp.int32)
    x_pool = noise(arg_keys[9], (TPOOL, BLOCK_ROWS, IN_SEL), IN_SEL ** -0.5, 0.0390625, ((1, 32), (2, 8)))
    delta_pool = noise(arg_keys[10], (TPOOL, BLOCK_ROWS, OUT_WIN), (BLOCK_ROWS * OUT_WIN) ** -0.5, 0.09375, ((1, 32),))
    return {"basis_out": basis_out, "corrected": corrected, "factor_table": factor_table, "block_ids": block_ids, "basis_in": basis_in, "query_ids": query_ids, "u_pool": u_pool, "v_pool": v_pool, "train_ids": train_ids, "x_pool": x_pool, "delta_pool": delta_pool}


def reference(basis_out, corrected, factor_table, block_ids, basis_in, query_ids, u_pool, v_pool, train_ids, x_pool, delta_pool):
    queries = query_ids.shape[0]
    query_left = jnp.take(u_pool, query_ids, axis=0)
    left_flat = jnp.transpose(query_left, (1, 0, 2)).reshape(OUT, queries * RANK)
    rotated_left = jnp.dot(basis_out.T, left_flat, preferred_element_type=jnp.float32).astype(jnp.bfloat16)
    query_right = jnp.take(v_pool, query_ids, axis=0)
    right_blocks = jnp.transpose(query_right, (1, 0, 2)).reshape(NB, EB, queries * RANK)
    rotated_right = jnp.einsum("cij,cir->cjr", basis_in.astype(jnp.float32), right_blocks.astype(jnp.float32))
    rotated_right = rotated_right.astype(jnp.bfloat16).reshape(IN_SEL, queries, RANK)
    scale_row = jnp.take(factor_table, block_ids, axis=0).reshape(IN_SEL)
    divisor = corrected * scale_row[None, :]
    positions = jnp.arange(OUT_WIN, dtype=jnp.int32)
    window_index = (positions // WIN_ROWS) * (OUT // N_IN) + positions % WIN_ROWS
    window = jnp.take(basis_out, window_index, axis=0)
    left_three = rotated_left.reshape(OUT, queries, RANK)
    block_rows = math.gcd(OUT, 512)

    def add_block(running, step_index):
        offset = (step_index * block_rows).astype(jnp.int32)
        left_part = lax.dynamic_slice_in_dim(left_three, offset, block_rows, 0)
        divisor_part = lax.dynamic_slice_in_dim(divisor, offset, block_rows, 0)
        product = jnp.einsum("kqr,jqr->kqj", left_part.astype(jnp.float32), rotated_right.astype(jnp.float32))
        precond = (product / divisor_part[:, None, :]).astype(jnp.bfloat16)
        window_part = lax.dynamic_slice_in_dim(window, offset, block_rows, 1)
        window_term = jnp.dot(window_part, precond.reshape(block_rows, queries * IN_SEL), preferred_element_type=jnp.float32)
        return running + window_term, None

    start_sum = jnp.zeros((OUT_WIN, queries * IN_SEL), jnp.float32)
    half_back, _ = lax.scan(add_block, start_sum, jnp.arange(OUT // block_rows, dtype=jnp.int32))
    half_back = half_back.astype(jnp.bfloat16).reshape(OUT_WIN, queries, NB, EB)
    tiles = jnp.einsum("oqcj,cij->qoci", half_back.astype(jnp.float32), basis_in.astype(jnp.float32))
    tiles = tiles.astype(jnp.bfloat16).reshape(queries, OUT_WIN, IN_SEL)
    train_inputs = jnp.take(x_pool, train_ids, axis=0).astype(jnp.float32)
    train_deltas = jnp.take(delta_pool, train_ids, axis=0).astype(jnp.float32)
    projected = jnp.einsum("bsj,qoj->bsqo", train_inputs, tiles.astype(jnp.float32))
    scores = jnp.einsum("bsqo,bso->qb", projected, train_deltas, precision=lax.Precision.HIGHEST)
    return tiles, scores
```

```python
import functools

import jax
import jax.numpy as jnp
from jax import lax
from jax.experimental import pallas as pl
from jax.experimental.pallas import tpu as pltpu
from jax.sharding import Mesh
from jax.sharding import PartitionSpec as P

WIN_ROWS = 16
OUT = ("z", "xh", "c")
IN = ("y", "xl")
QUAD = ("xh", "c")
PLANE = ("xh", "c", "y", "xl")
BF = jnp.bfloat16
F32 = jnp.float32
LANES = 128
VMEM_LIMIT = 56 * 2**20

VMEM_SPEC = pl.BlockSpec(memory_space=pltpu.VMEM)
SMEM_SPEC = pl.BlockSpec(memory_space=pltpu.SMEM)


def params():
    return pltpu.CompilerParams(vmem_limit_bytes=VMEM_LIMIT)


def dot(a, b, ca, cb):
    return lax.dot_general(a, b, (((ca,), (cb,)), ((), ())), preferred_element_type=F32)


def exchange(value, axis):
    return lax.all_to_all(value, axis, split_axis=0, concat_axis=0, tiled=True)


def copies(value, axis):
    return exchange(jnp.broadcast_to(value, (lax.axis_size(axis), *value.shape)), axis)


def swap(value, axis, mask=1):
    size = lax.axis_size(axis)
    return lax.ppermute(value, axis, [(i, i ^ mask) for i in range(size)])


def shift(value, step):
    size = lax.axis_size("z")
    return lax.ppermute(value, "z", [(i, (i + step) % size) for i in range(size)])


def left_body(ids, u0, u1, u2, u3, basis, out):
    left = jnp.concatenate([u[0] for u in (u0, u1, u2, u3)], axis=0)
    n_in, rows, width = out.shape
    part = dot(left, basis[...], 1, 0).astype(BF)
    out[:, : rows - WIN_ROWS, :] = part.reshape(n_in, rows - WIN_ROWS, width)
    out[:, rows - WIN_ROWS :, :] = jnp.broadcast_to(
        basis[:WIN_ROWS, :][None], (n_in, WIN_ROWS, width)
    )


def left_part(query_ids, u_t, basis_out, n_in):
    queries = query_ids.shape[0]
    _, rank, depth = u_t.shape
    eigen = basis_out.shape[1]
    rows = queries * rank // n_in + WIN_ROWS
    tile = 256
    specs = [
        pl.BlockSpec((1, rank, depth), functools.partial(lambda q, n, ids: (ids[q], 0, 0), q))
        for q in range(queries)
    ]
    return pl.pallas_call(
        left_body,
        out_shape=jax.ShapeDtypeStruct((n_in, rows, eigen), BF),
        grid_spec=pltpu.PrefetchScalarGridSpec(
            num_scalar_prefetch=1,
            grid=(eigen // tile,),
            in_specs=[*specs, pl.BlockSpec((depth, tile), lambda n, ids: (0, n))],
            out_specs=pl.BlockSpec((n_in, rows, tile), lambda n, ids: (0, 0, n)),
        ),
        compiler_params=params(),
        name="left",
    )(query_ids, u_t, u_t, u_t, u_t, basis_out)


def left_sum_body(parts, out, window):
    n_in, rows, _ = parts.shape
    own = rows - WIN_ROWS
    total = parts[0, :own, :].astype(F32)
    for i in range(1, n_in):
        total += parts[i, :own, :].astype(F32)
    total = total.astype(BF)
    for i in range(n_in):
        out[i] = total
        window[i * WIN_ROWS : (i + 1) * WIN_ROWS, :] = parts[i, own:, :]


def left_sum(parts):
    n_in, rows, eigen = parts.shape
    return pl.pallas_call(
        left_sum_body,
        out_shape=(
            jax.ShapeDtypeStruct((n_in, rows - WIN_ROWS, eigen), BF),
            jax.ShapeDtypeStruct((n_in * WIN_ROWS, eigen), BF),
        ),
        in_specs=[VMEM_SPEC],
        out_specs=(VMEM_SPEC, VMEM_SPEC),
        compiler_params=params(),
        name="left_sum",
    )(parts)


def inverse_body(offsets, corrected, *outs):
    for r, out in enumerate(outs):
        at = pl.multiple_of(offsets[r], LANES)
        out[...] = (1.0 / corrected[:, pl.ds(at, out.shape[1])]).astype(BF)


def inverse_quarters(offsets, corrected, width):
    rows, columns = corrected.shape
    tile = 64
    return pl.pallas_call(
        inverse_body,
        out_shape=tuple(jax.ShapeDtypeStruct((rows, width), BF) for _ in range(4)),
        grid_spec=pltpu.PrefetchScalarGridSpec(
            num_scalar_prefetch=1,
            grid=(rows // tile,),
            in_specs=[pl.BlockSpec((tile, columns), lambda n, o: (n, 0))],
            out_specs=tuple(pl.BlockSpec((tile, width), lambda n, o: (n, 0)) for _ in range(4)),
        ),
        compiler_params=params(),
        name="inverse",
    )(offsets, corrected)


def rotate_body(where, ids, v0, v1, v2, v3, *refs):
    chunks, (basis, right, tokens, delta) = refs[:-4], refs[-4:]
    n_z = len(chunks)
    slab = basis.shape[0] // n_z
    extra = (chunks[0].shape[0] - slab) // 2
    for k, chunk in enumerate(chunks):
        step = k if k <= n_z // 2 else k - n_z
        at = lax.rem(where[0] - step + n_z, n_z) * slab
        basis[pl.ds(pl.multiple_of(at, 16), slab), :] = chunk[:slab, :]
    factors = jnp.concatenate([v[0] for v in (v0, v1, v2, v3)], axis=0)
    whole = basis[...]
    right[...] = dot(factors, whole, 1, 0).astype(BF)
    width = whole.shape[1]
    rest = whole.shape[0] - width
    head = jnp.concatenate([c[slab : slab + extra, :] for c in chunks], axis=0)
    tail = jnp.concatenate([c[slab + extra :, :] for c in chunks], axis=0)
    rotated = dot(head, whole[:width, :], 1, 0) + dot(tail[:, :rest], whole[width:, :], 1, 0)
    tokens[...] = rotated.astype(BF)
    delta[...] = tail[:, rest:]


def rotate(where, query_ids, v_t, chunks, block_width):
    queries = query_ids.shape[0]
    rank = v_t.shape[1]
    rows, width = chunks[0].shape
    extra = (rows - block_width // len(chunks)) // 2
    specs = [
        pl.BlockSpec(
            (1, rank, block_width),
            functools.partial(lambda q, n, w, ids: (ids[q], 0, w[1]), q),
        )
        for q in range(queries)
    ]

    def full(shape):
        return pl.BlockSpec(shape, lambda n, w, ids: (0, 0))

    shapes = (
        (block_width, width),
        (queries * rank, width),
        (len(chunks) * extra, width),
        (len(chunks) * extra, 2 * width - block_width),
    )
    return pl.pallas_call(
        rotate_body,
        out_shape=tuple(jax.ShapeDtypeStruct(s, BF) for s in shapes),
        grid_spec=pltpu.PrefetchScalarGridSpec(
            num_scalar_prefetch=2,
            grid=(1,),
            in_specs=[*specs, *(full((rows, width)) for _ in chunks)],
            out_specs=tuple(full(s) for s in shapes),
        ),
        compiler_params=params(),
        name="rotate",
    )(where, query_ids, v_t, v_t, v_t, v_t, *chunks)


def back_body(where, factors, right, tokens, delta, *refs):
    lefts, windows, inverses, (out, score) = refs[:4], refs[4:8], refs[8:12], refs[12:]
    n_z, queries, rows, width = out.shape
    rank = right.shape[0] // queries
    valid = factors.shape[1] // 2
    skip = factors.shape[1] - width
    row = factors[pl.ds(where[2], 1), pl.ds(pl.multiple_of(where[3] * skip, LANES), width)]
    lane = lax.broadcasted_iota(jnp.int32, (1, width), 1)
    first = where[3] * (width - valid)
    mine = jnp.logical_and(lane >= first, lane < first + valid)
    scale = jnp.where(mine, 1.0 / row, 0.0)
    train = 4
    which = lax.rem(lax.broadcasted_iota(jnp.int32, (tokens.shape[0], 1), 0), train)
    for q in range(queries):
        at = slice(q * rank, (q + 1) * rank)
        total = None
        for left, window, inverse in zip(lefts, windows, inverses):
            product = dot(left[at, :], right[at, :], 0, 0)
            precond = (product * inverse[...].astype(F32)).astype(BF)
            term = dot(window[...], precond, 1, 0)
            total = term if total is None else total + term
        total = (total * scale).astype(BF)
        out[:, q] = total.reshape(n_z, rows, width)
        projected = dot(tokens[...], total, 1, 1) * delta[...].astype(F32)
        for b in range(train):
            part = jnp.where(which == b, projected, 0.0)
            score[q * train + b : q * train + b + 1, :] = jnp.sum(part, axis=0, keepdims=True)


def back(where, factors, right, tokens, delta, lefts, windows, inverses, n_z, queries):
    width = right.shape[1]
    win = windows[0].shape[0]
    return pl.pallas_call(
        back_body,
        out_shape=(
            jax.ShapeDtypeStruct((n_z, queries, win // n_z, width), BF),
            jax.ShapeDtypeStruct((queries * 4, win), F32),
        ),
        in_specs=[SMEM_SPEC, *([VMEM_SPEC] * (4 + 12))],
        out_specs=(VMEM_SPEC, VMEM_SPEC),
        compiler_params=params(),
        name="back",
    )(where, factors, right, tokens, delta, *lefts, *windows, *inverses)


def tile_body(parts, basis, out):
    n_z, rows, width = parts.shape
    owners, own, _ = out.shape
    queries = 4
    per = own // queries
    to = lax.broadcasted_iota(jnp.int32, (rows, n_z * rows), 0)
    at = lax.rem(lax.broadcasted_iota(jnp.int32, (rows, n_z * rows), 1), rows)
    query = at // (owners * per)
    owner = lax.rem(at // per, owners)
    goal = owner * own + query * per + lax.rem(at, per)
    select = jnp.where(goal == to, 1.0, 0.0).astype(BF)
    half = dot(select, parts[...].reshape(n_z * rows, width), 1, 0).astype(BF)
    tiles = dot(half, basis[...], 1, 1).astype(BF)
    out[...] = tiles.reshape(owners, own, tiles.shape[1])


def tile_part(parts, basis, owners):
    rows = parts.shape[1]
    return pl.pallas_call(
        tile_body,
        out_shape=jax.ShapeDtypeStruct((owners, rows // owners, basis.shape[0]), BF),
        in_specs=[VMEM_SPEC, VMEM_SPEC],
        out_specs=VMEM_SPEC,
        compiler_params=params(),
        name="tile",
    )(parts, basis)


def shards(
    basis_out,
    corrected,
    factor_table,
    block_ids,
    basis_in,
    query_ids,
    u_pool,
    v_pool,
    train_ids,
    x_pool,
    delta_pool,
):
    n_z, n_in = lax.axis_size("z"), lax.axis_size(IN)
    z, xh, c = lax.axis_index("z"), lax.axis_index("xh"), lax.axis_index("c")
    in_pos = lax.axis_index(IN)
    queries, train = query_ids.shape[0], train_ids.shape[0]
    _, local_rows, block = basis_in.shape
    width = -(-(block // 2) // LANES) * LANES
    skip = block - width
    me = 2 * xh + c

    parts = left_part(query_ids, jnp.transpose(u_pool, (0, 2, 1)), basis_out, n_in)
    spread, window = left_sum(exchange(parts, IN))
    left = exchange(spread, IN).reshape(-1, basis_out.shape[1])
    left_x, window_x = swap(left, "xh"), swap(window, "xh")
    lefts = (left, swap(left, "c"), left_x, swap(left_x, "c"))
    windows = (window, swap(window, "c"), window_x, swap(window_x, "c"))

    others = me ^ jnp.arange(4, dtype=jnp.int32)
    offsets = (others // 2) * block + (others % 2) * skip
    quarters = inverse_quarters(offsets, corrected, width)
    inverses = (
        quarters[0],
        swap(quarters[1], "c"),
        swap(quarters[2], "xh"),
        swap(quarters[3], QUAD, 3),
    )

    chosen = (train_ids[:, None] == jnp.arange(x_pool.shape[0])[None, :]).astype(BF)
    rows = jnp.concatenate([x_pool[:, 0], delta_pool[:, 0]], axis=1)
    rows = jnp.dot(chosen, rows, preferred_element_type=F32).astype(BF)
    deltas = rows[:, 2 * block :]
    send = []
    for p in range(4):
        blk, half = divmod(p, 2)
        cut = basis_in[blk, :, half * skip : half * skip + width]
        own = rows[:, blk * block : (blk + 1) * block]
        send.append(
            jnp.concatenate(
                [cut, own[:, :width], jnp.concatenate([own[:, width:], deltas], axis=1)], axis=0
            )
        )
    got = exchange(jnp.stack(send), QUAD)
    ends = (0, local_rows, local_rows + train, local_rows + 2 * train)
    own = jnp.concatenate(
        [got[:, a:b].reshape(-1, width) for a, b in zip(ends[:-1], ends[1:])], axis=0
    )
    ahead, behind = [own], []
    for step in range(n_z // 2):
        ahead.append(shift(ahead[-1], 1))
        if step < n_z // 2 - 1:
            behind.append(shift(behind[-1] if behind else own, -1))
    chunks = ahead + behind[::-1]

    block_id = lax.dynamic_index_in_dim(block_ids, in_pos * 2 + xh, keepdims=False)
    where = jnp.stack([z, xh, block_id, c]).astype(jnp.int32)
    basis, right, tokens, delta = rotate(
        where, query_ids, jnp.transpose(v_pool, (0, 2, 1)), chunks, block
    )
    parts, score = back(
        where, factor_table, right, tokens, delta, lefts, windows, inverses, n_z, queries
    )
    summed = exchange(parts.reshape(n_z, -1, width), "z")
    owned = exchange(tile_part(summed, basis, 4), QUAD).astype(F32)
    pairs = owned.reshape(2, 2, queries, -1, block)
    tiles = (pairs[:, 0] + pairs[:, 1]).astype(BF)
    tiles = jnp.moveaxis(tiles, 0, 2).reshape(queries, -1, 2 * block)

    score = copies(jnp.sum(score, axis=1)[None], "z").sum(axis=0)
    score = copies(score, PLANE).sum(axis=0)
    return tiles, score.reshape(queries, train)


def solution(mesh):
    split = Mesh(mesh.devices.reshape(8, 2, 2, 4, 2), ("z", "xh", "c", "y", "xl"))
    return jax.shard_map(
        shards,
        mesh=split,
        in_specs=(
            P(IN, OUT),
            P(OUT, IN),
            P(),
            P(),
            P(IN, OUT, None),
            P(),
            P(None, IN, None),
            P(None, IN, None),
            P(),
            P(None, OUT, IN),
            P(None, OUT, None),
        ),
        out_specs=(P(None, OUT, IN), P()),
        check_vma=False,
    )
```

```python
import functools

import jax
import jax.numpy as jnp
from jax import lax
from jax.experimental import pallas as pl
from jax.experimental.pallas import tpu as pltpu
from jax.sharding import Mesh
from jax.sharding import PartitionSpec as P

WIN_ROWS = 16
OUT = ("z", "xh", "c")
IN = ("y", "xl")
QUAD = ("xh", "c")
PLANE = ("xh", "c", "y", "xl")
BF = jnp.bfloat16
F32 = jnp.float32
LANES = 128
MIB = 2**20

VMEM_SPEC = pl.BlockSpec(memory_space=pltpu.VMEM)
SMEM_SPEC = pl.BlockSpec(memory_space=pltpu.SMEM)


def setup(mib, flops, nbytes):
    return {
        "compiler_params": pltpu.CompilerParams(vmem_limit_bytes=mib * MIB),
        "cost_estimate": pl.CostEstimate(flops=flops, bytes_accessed=nbytes, transcendentals=0),
    }


def dot(a, b, ca, cb):
    return lax.dot_general(a, b, (((ca,), (cb,)), ((), ())), preferred_element_type=F32)


def exchange(value, axis):
    return lax.all_to_all(value, axis, split_axis=0, concat_axis=0, tiled=True)


def swap(value, axis, mask=1):
    size = lax.axis_size(axis)
    return lax.ppermute(value, axis, [(i, i ^ mask) for i in range(size)])


def left_body(ids, u0, u1, u2, u3, basis, out):
    left = jnp.concatenate([u[0] for u in (u0, u1, u2, u3)], axis=0)
    n_in, rows, width = out.shape
    part = dot(left, basis[...], 1, 0).astype(BF)
    out[:, : rows - WIN_ROWS, :] = part.reshape(n_in, rows - WIN_ROWS, width)
    out[:, rows - WIN_ROWS :, :] = jnp.broadcast_to(
        basis[:WIN_ROWS, :][None], (n_in, WIN_ROWS, width)
    )


def left_part(query_ids, u_t, basis_out, n_in):
    queries = query_ids.shape[0]
    _, rank, depth = u_t.shape
    eigen = basis_out.shape[1]
    rows = queries * rank // n_in + WIN_ROWS
    tile = 256
    specs = [
        pl.BlockSpec((1, rank, depth), functools.partial(lambda q, n, ids: (ids[q], 0, 0), q))
        for q in range(queries)
    ]
    return pl.pallas_call(
        left_body,
        out_shape=jax.ShapeDtypeStruct((n_in, rows, eigen), BF),
        grid_spec=pltpu.PrefetchScalarGridSpec(
            num_scalar_prefetch=1,
            grid=(eigen // tile,),
            in_specs=[*specs, pl.BlockSpec((depth, tile), lambda n, ids: (0, n))],
            out_specs=pl.BlockSpec((n_in, rows, tile), lambda n, ids: (0, 0, n)),
        ),
        **setup(16, 2 * depth * eigen * rank * queries, 4 * MIB),
        name="left",
    )(query_ids, u_t, u_t, u_t, u_t, basis_out)


def left_sum_body(parts, out, window):
    n_in, rows, _ = parts.shape
    own = rows - WIN_ROWS
    total = parts[0, :own, :].astype(F32)
    for i in range(1, n_in):
        total += parts[i, :own, :].astype(F32)
    total = total.astype(BF)
    for i in range(n_in):
        out[i] = total
        window[i * WIN_ROWS : (i + 1) * WIN_ROWS, :] = parts[i, own:, :]


def left_sum(parts):
    n_in, rows, eigen = parts.shape
    return pl.pallas_call(
        left_sum_body,
        out_shape=(
            jax.ShapeDtypeStruct((n_in, rows - WIN_ROWS, eigen), BF),
            jax.ShapeDtypeStruct((n_in * WIN_ROWS, eigen), BF),
        ),
        in_specs=[VMEM_SPEC],
        out_specs=(VMEM_SPEC, VMEM_SPEC),
        **setup(4, 0, 2 * MIB),
        name="left_sum",
    )(parts)


def inverse_body(where, corrected, *outs):
    for r, out in enumerate(outs):
        half = where[3] ^ r
        skip = corrected.shape[1] - out.shape[1]
        at = pl.multiple_of(half * skip, LANES)
        out[...] = (1.0 / corrected[:, pl.ds(at, out.shape[1])]).astype(BF)


def inverse_halves(where, corrected, block, width, far):
    rows = corrected.shape[0]
    tile = 64
    return pl.pallas_call(
        inverse_body,
        out_shape=tuple(jax.ShapeDtypeStruct((rows, width), BF) for _ in range(2)),
        grid_spec=pltpu.PrefetchScalarGridSpec(
            num_scalar_prefetch=1,
            grid=(rows // tile,),
            in_specs=[pl.BlockSpec((tile, block), lambda n, w: (n, w[1] ^ far))],
            out_specs=tuple(pl.BlockSpec((tile, width), lambda n, w: (n, 0)) for _ in range(2)),
        ),
        **setup(8, 0, 12 * MIB),
        name="inverse",
    )(where, corrected)


def pack_body(where, train_ids, basis, tokens, delta, *outs):
    rows = basis.shape[1]
    train = train_ids.shape[0]
    for r, out in enumerate(outs):
        width = out.shape[1]
        block = basis.shape[2]
        skip = block - width
        blk, half = where[1] ^ (r // 2), where[3] ^ (r % 2)
        out[:rows, :] = basis[blk, :, pl.ds(pl.multiple_of(half * skip, LANES), width)]
        for b in range(train):
            row = train_ids[b]
            first = pl.multiple_of(blk * block, LANES)
            rest = pl.multiple_of(blk * block + width, LANES)
            out[rows + b : rows + b + 1, :] = tokens[row, :, pl.ds(first, width)]
            at = rows + train + b
            out[at : at + 1, :skip] = tokens[row, :, pl.ds(rest, skip)]
            out[at : at + 1, skip:] = delta[row]


def pack(where, train_ids, basis, tokens, delta, width):
    rows = basis.shape[1] + 2 * train_ids.shape[0]
    return pl.pallas_call(
        pack_body,
        out_shape=tuple(jax.ShapeDtypeStruct((rows, width), BF) for _ in range(4)),
        in_specs=[SMEM_SPEC, SMEM_SPEC, VMEM_SPEC, VMEM_SPEC, VMEM_SPEC],
        out_specs=tuple([VMEM_SPEC] * 4),
        **setup(4, 0, 2 * MIB),
        name="pack",
    )(where, train_ids, basis, tokens, delta)


def arrange_body(where, a0, a1, a2, a3, out, *, local, train):
    me = 2 * where[1] + where[3]
    rows = out.shape[0]
    each = local + 2 * train
    to = lax.broadcasted_iota(jnp.int32, (rows, each), 0)
    at = lax.broadcasted_iota(jnp.int32, (rows, each), 1)
    total = None
    for r, part in enumerate((a0, a1, a2, a3)):
        src = me ^ r
        head = src * local + at
        token = 4 * local + src * train + at - local
        other = 4 * local + 4 * train + src * train + at - local - train
        goal = jnp.where(at < local, head, jnp.where(at < local + train, token, other))
        term = dot(jnp.where(goal == to, 1.0, 0.0).astype(BF), part[...], 1, 0)
        total = term if total is None else total + term
    out[...] = total.astype(BF)


def arrange(where, parts, local, train):
    rows, width = parts[0].shape
    return pl.pallas_call(
        functools.partial(arrange_body, local=local, train=train),
        out_shape=jax.ShapeDtypeStruct((4 * rows, width), BF),
        in_specs=[SMEM_SPEC, *([VMEM_SPEC] * 4)],
        out_specs=VMEM_SPEC,
        **setup(8, 0, 2 * MIB),
        name="arrange",
    )(where, *parts)


def rotate_body(where, ids, v0, v1, v2, v3, gathered, basis, right, tokens, delta, *, n_z):
    each = gathered.shape[0] // n_z
    slab = basis.shape[0] // n_z
    extra = (each - slab) // 2
    for k in range(n_z):
        basis[k * slab : (k + 1) * slab, :] = gathered[k * each : k * each + slab, :]
    factors = jnp.concatenate([v[0] for v in (v0, v1, v2, v3)], axis=0)
    whole = basis[...]
    right[...] = dot(factors, whole, 1, 0).astype(BF)
    width = whole.shape[1]
    rest = whole.shape[0] - width
    head, tail = (
        jnp.concatenate(
            [gathered[k * each + a : k * each + a + extra, :] for k in range(n_z)], axis=0
        )
        for a in (slab, slab + extra)
    )
    rotated = dot(head, whole[:width, :], 1, 0) + dot(tail[:, :rest], whole[width:, :], 1, 0)
    tokens[...] = rotated.astype(BF)
    delta[...] = tail[:, rest:]


def rotate(where, query_ids, v_t, gathered, block, n_z):
    queries = query_ids.shape[0]
    rank = v_t.shape[1]
    rows, width = gathered.shape
    extra = (rows - block) // 2
    specs = [
        pl.BlockSpec(
            (1, rank, block), functools.partial(lambda q, n, w, ids: (ids[q], 0, w[1]), q)
        )
        for q in range(queries)
    ]

    def full(shape):
        return pl.BlockSpec(shape, lambda n, w, ids: (0, 0))

    shapes = (
        (block, width),
        (queries * rank, width),
        (extra, width),
        (extra, 2 * width - block),
    )
    return pl.pallas_call(
        functools.partial(rotate_body, n_z=n_z),
        out_shape=tuple(jax.ShapeDtypeStruct(s, BF) for s in shapes),
        grid_spec=pltpu.PrefetchScalarGridSpec(
            num_scalar_prefetch=2,
            grid=(1,),
            in_specs=[*specs, full((rows, width))],
            out_specs=tuple(full(s) for s in shapes),
        ),
        **setup(32, 2 * block * width * (queries * rank + extra), 8 * MIB),
        name="rotate",
    )(where, query_ids, v_t, v_t, v_t, v_t, gathered)


def back_body(where, factors, right, tokens, delta, *refs, queries, train):
    lefts, windows, inverses, out = refs[:4], refs[4:8], refs[8:12], refs[12]
    n_z, rows, width = out.shape
    win = windows[0].shape[0]
    per = win // n_z
    rank = right.shape[0] // queries
    valid = factors.shape[1] // 2
    skip = factors.shape[1] - width
    row = factors[pl.ds(where[2], 1), pl.ds(pl.multiple_of(where[3] * skip, LANES), width)]
    lane = lax.broadcasted_iota(jnp.int32, (1, width), 1)
    first = where[3] * (width - valid)
    mine = jnp.logical_and(lane >= first, lane < first + valid)
    scale = jnp.where(mine, 1.0 / row, 0.0)
    which = lax.rem(
        lax.broadcasted_iota(jnp.int32, (tokens.shape[0], 1), 0), train
    )
    scores = []
    for q in range(queries):
        at = slice(q * rank, (q + 1) * rank)
        total = None
        for left, window, inverse in zip(lefts, windows, inverses):
            product = dot(left[at, :], right[at, :], 0, 0)
            precond = (product * inverse[...].astype(F32)).astype(BF)
            term = dot(window[...], precond, 1, 0)
            total = term if total is None else total + term
        total = (total * scale).astype(BF)
        out[:, q * per : (q + 1) * per, :] = total.reshape(n_z, per, width)
        projected = dot(tokens[...], total, 1, 1) * delta[...].astype(F32)
        scores += [
            jnp.sum(jnp.where(which == b, projected, 0.0), axis=0, keepdims=True)
            for b in range(train)
        ]
    words = []
    for k in range(0, queries * train, 8):
        group = jnp.concatenate(scores[k : k + 8], axis=0)
        high = group.astype(BF)
        words += [high, (group - high.astype(F32)).astype(BF)]
    words.append(jnp.zeros((8, width - len(words) * win), BF))
    extra = jnp.concatenate(words, axis=1)
    for k in range(n_z):
        out[k, queries * per :, :] = extra


def back(where, factors, right, tokens, delta, lefts, windows, inverses, n_z, queries, train):
    width = right.shape[1]
    win, depth = windows[0].shape
    return pl.pallas_call(
        functools.partial(back_body, queries=queries, train=train),
        out_shape=jax.ShapeDtypeStruct((n_z, queries * win // n_z + 8, width), BF),
        in_specs=[SMEM_SPEC, *([VMEM_SPEC] * (4 + 12))],
        out_specs=VMEM_SPEC,
        **setup(32, 16 * depth * width * queries * win, 8 * MIB),
        name="back",
    )(where, factors, right, tokens, delta, *lefts, *windows, *inverses)


def tile_body(where, parts, basis, t0, t1, t2, t3, score, *, queries, train):
    n_z = parts.shape[0]
    me = 2 * where[1] + where[3]
    own = t0.shape[0]
    rows = 4 * own
    per = own // queries
    total = parts[0].astype(F32)
    for k in range(1, n_z):
        total += parts[k].astype(F32)
    to = lax.broadcasted_iota(jnp.int32, (rows, rows), 0)
    at = lax.broadcasted_iota(jnp.int32, (rows, rows), 1)
    query = at // own
    owner = lax.rem(at // per, 4)
    goal = (owner ^ me) * own + query * per + lax.rem(at, per)
    select = jnp.where(goal == to, 1.0, 0.0).astype(BF)
    half = dot(select, total[:rows].astype(BF), 1, 0).astype(BF)
    tiles = dot(half, basis[...], 1, 1).astype(BF)
    for r, out in enumerate((t0, t1, t2, t3)):
        out[...] = tiles[r * own : (r + 1) * own]
    words = total[rows:]
    line = lax.broadcasted_iota(jnp.int32, (8, LANES), 0)
    lane = lax.broadcasted_iota(jnp.int32, (8, LANES), 1)
    table = jnp.zeros((8, LANES), F32)
    for k in range(queries * train // 8):
        at = 2 * k * LANES
        sums = words[:, at : at + LANES] + words[:, at + LANES : at + 2 * LANES]
        sums = jnp.sum(sums, axis=1, keepdims=True)
        for i in range(8):
            q, b = divmod(8 * k + i, train)
            table = jnp.where(jnp.logical_and(line == q, lane == b), sums[i : i + 1], table)
    score[...] = jnp.broadcast_to(table[None], score.shape)


def tile_part(where, parts, basis, plane, queries, train):
    own = (parts.shape[1] - 8) // 4
    block = basis.shape[0]
    return pl.pallas_call(
        functools.partial(tile_body, queries=queries, train=train),
        out_shape=(
            *(jax.ShapeDtypeStruct((own, block), BF) for _ in range(4)),
            jax.ShapeDtypeStruct((plane, 8, LANES), F32),
        ),
        in_specs=[SMEM_SPEC, VMEM_SPEC, VMEM_SPEC],
        out_specs=tuple([VMEM_SPEC] * 5),
        **setup(24, 8 * own * block * basis.shape[1], 5 * MIB),
        name="tile",
    )(where, parts, basis)


def final_body(where, t0, t1, t2, t3, score, tiles, scores):
    queries, per, columns = tiles.shape
    block = columns // 2
    for r, (a, b) in enumerate(((t0, t1), (t2, t3))):
        total = (a[...].astype(F32) + b[...].astype(F32)).astype(BF)
        at = pl.multiple_of((where[1] ^ r) * block, LANES)
        for q in range(queries):
            tiles[q, :, pl.ds(at, block)] = total[q * per : (q + 1) * per]
    scores[...] = jnp.sum(score[...], axis=0)[: scores.shape[0], : scores.shape[1]]


def final(where, parts, score, queries, train):
    own, block = parts[0].shape
    return pl.pallas_call(
        final_body,
        out_shape=(
            jax.ShapeDtypeStruct((queries, own // queries, 2 * block), BF),
            jax.ShapeDtypeStruct((queries, train), F32),
        ),
        in_specs=[SMEM_SPEC, *([VMEM_SPEC] * 5)],
        out_specs=(VMEM_SPEC, VMEM_SPEC),
        **setup(4, 0, 1 * MIB),
        name="final",
    )(where, *parts, score)


def shards(
    basis_out,
    corrected,
    factor_table,
    block_ids,
    basis_in,
    query_ids,
    u_pool,
    v_pool,
    train_ids,
    x_pool,
    delta_pool,
):
    n_z, n_in = lax.axis_size("z"), lax.axis_size(IN)
    xh, c = lax.axis_index("xh"), lax.axis_index("c")
    in_pos = lax.axis_index(IN)
    queries, train = query_ids.shape[0], train_ids.shape[0]
    _, local_rows, block = basis_in.shape
    width = -(-(block // 2) // LANES) * LANES
    block_id = lax.dynamic_index_in_dim(block_ids, in_pos * 2 + xh, keepdims=False)
    where = jnp.stack([in_pos, xh, block_id, c]).astype(jnp.int32)

    packed = pack(where, train_ids, basis_in, x_pool, delta_pool, width)
    parts = (
        packed[0],
        swap(packed[1], "c"),
        swap(packed[2], "xh"),
        swap(packed[3], QUAD, 3),
    )
    own = arrange(where, parts, local_rows, train)
    gathered = lax.all_gather(own, "z", axis=0, tiled=True)

    far = inverse_halves(where, corrected, block, width, 1)
    near = inverse_halves(where, corrected, block, width, 0)
    inverses = (near[0], swap(near[1], "c"), swap(far[0], "xh"), swap(far[1], QUAD, 3))
    left_ids, _ = lax.optimization_barrier((query_ids, far[0]))

    parts = left_part(left_ids, jnp.transpose(u_pool, (0, 2, 1)), basis_out, n_in)
    spread, window = left_sum(exchange(parts, IN))
    left = exchange(spread, IN).reshape(-1, basis_out.shape[1])
    left_x, window_x = swap(left, "xh"), swap(window, "xh")
    lefts = (left, swap(left, "c"), left_x, swap(left_x, "c"))
    windows = (window, swap(window, "c"), window_x, swap(window_x, "c"))

    basis, right, tokens, delta = rotate(
        where, query_ids, jnp.transpose(v_pool, (0, 2, 1)), gathered, block, n_z
    )
    parts = back(
        where,
        factor_table,
        right,
        tokens,
        delta,
        lefts,
        windows,
        inverses,
        n_z,
        queries,
        train,
    )
    *parts, score = tile_part(
        where, exchange(parts, "z"), basis, lax.axis_size(PLANE), queries, train
    )
    parts = (
        parts[0],
        swap(parts[1], "c"),
        swap(parts[2], "xh"),
        swap(parts[3], QUAD, 3),
    )
    return final(where, parts, exchange(score, PLANE), queries, train)


def solution(mesh):
    split = Mesh(mesh.devices.reshape(8, 2, 2, 4, 2), ("z", "xh", "c", "y", "xl"))
    return jax.shard_map(
        shards,
        mesh=split,
        in_specs=(
            P(IN, OUT),
            P(OUT, IN),
            P(),
            P(),
            P(IN, OUT, None),
            P(),
            P(None, IN, None),
            P(None, IN, None),
            P(),
            P(None, OUT, IN),
            P(None, OUT, None),
        ),
        out_specs=(P(None, OUT, IN), P()),
        check_vma=False,
    )
```

```python
import functools

import jax
import jax.numpy as jnp
from jax import lax
from jax.experimental import pallas as pl
from jax.experimental.pallas import tpu as pltpu
from jax.sharding import Mesh
from jax.sharding import PartitionSpec as P

WIN_ROWS = 16
OUT = ("z", "xh", "c")
IN = ("y", "xl")
QUAD = ("xh", "c")
PLANE = ("xh", "c", "y", "xl")
BF = jnp.bfloat16
F32 = jnp.float32
LANES = 128
MIB = 2**20

VMEM_SPEC = pl.BlockSpec(memory_space=pltpu.VMEM)
SMEM_SPEC = pl.BlockSpec(memory_space=pltpu.SMEM)


def params(mib):
    return pltpu.CompilerParams(vmem_limit_bytes=mib * MIB)


def dot(a, b, ca, cb):
    return lax.dot_general(a, b, (((ca,), (cb,)), ((), ())), preferred_element_type=F32)


def exchange(value, axis):
    return lax.all_to_all(value, axis, split_axis=0, concat_axis=0, tiled=True)


def swap(value, axis, mask=1):
    size = lax.axis_size(axis)
    return lax.ppermute(value, axis, [(i, i ^ mask) for i in range(size)])


def shift(value, step):
    size = lax.axis_size("z")
    return lax.ppermute(value, "z", [(i, (i + step) % size) for i in range(size)])


def after(value, *others):
    return lax.optimization_barrier((value, others))[0]


def left_body(ids, u0, u1, u2, u3, basis, out):
    left = jnp.concatenate([u[0] for u in (u0, u1, u2, u3)], axis=0)
    n_in, rows, width = out.shape
    part = dot(left, basis[...], 1, 0).astype(BF)
    out[:, : rows - WIN_ROWS, :] = part.reshape(n_in, rows - WIN_ROWS, width)
    out[:, rows - WIN_ROWS :, :] = jnp.broadcast_to(
        basis[:WIN_ROWS, :][None], (n_in, WIN_ROWS, width)
    )


def left_part(query_ids, u_t, basis_out, n_in):
    queries = query_ids.shape[0]
    _, rank, depth = u_t.shape
    eigen = basis_out.shape[1]
    rows = queries * rank // n_in + WIN_ROWS
    tile = 256
    specs = [
        pl.BlockSpec((1, rank, depth), functools.partial(lambda q, n, ids: (ids[q], 0, 0), q))
        for q in range(queries)
    ]
    return pl.pallas_call(
        left_body,
        out_shape=jax.ShapeDtypeStruct((n_in, rows, eigen), BF),
        grid_spec=pltpu.PrefetchScalarGridSpec(
            num_scalar_prefetch=1,
            grid=(eigen // tile,),
            in_specs=[*specs, pl.BlockSpec((depth, tile), lambda n, ids: (0, n))],
            out_specs=pl.BlockSpec((n_in, rows, tile), lambda n, ids: (0, 0, n)),
        ),
        compiler_params=params(16),
        name="left",
    )(query_ids, u_t, u_t, u_t, u_t, basis_out)


def left_sum_body(parts, out, window):
    n_in, rows, _ = parts.shape
    own = rows - WIN_ROWS
    total = parts[0, :own, :].astype(F32)
    for i in range(1, n_in):
        total += parts[i, :own, :].astype(F32)
    total = total.astype(BF)
    for i in range(n_in):
        out[i] = total
        window[i * WIN_ROWS : (i + 1) * WIN_ROWS, :] = parts[i, own:, :]


def left_sum(parts):
    n_in, rows, eigen = parts.shape
    return pl.pallas_call(
        left_sum_body,
        out_shape=(
            jax.ShapeDtypeStruct((n_in, rows - WIN_ROWS, eigen), BF),
            jax.ShapeDtypeStruct((n_in * WIN_ROWS, eigen), BF),
        ),
        in_specs=[VMEM_SPEC],
        out_specs=(VMEM_SPEC, VMEM_SPEC),
        compiler_params=params(4),
        name="left_sum",
    )(parts)


def inverse_body(where, corrected, out_0, out_1, values, done, *, far, part):
    rows, block = values.shape
    blk = where[1] ^ far
    source = corrected.at[
        pl.ds(part * rows, rows), pl.ds(pl.multiple_of(blk * block, LANES), block)
    ]
    copy = pltpu.make_async_copy(source, values, done)
    copy.start()
    copy.wait()
    for r, out in enumerate((out_0, out_1)):
        skip = block - out.shape[1]
        at = pl.multiple_of((where[3] ^ r) * skip, LANES)
        out[...] = (1.0 / values[:, pl.ds(at, out.shape[1])]).astype(BF)


def inverse_halves(where, corrected, block, width, far, parts=1, part=0):
    rows = corrected.shape[0] // parts
    return pl.pallas_call(
        functools.partial(inverse_body, far=far, part=part),
        out_shape=tuple(jax.ShapeDtypeStruct((rows, width), BF) for _ in range(2)),
        in_specs=[SMEM_SPEC, pl.BlockSpec(memory_space=pltpu.HBM)],
        out_specs=(VMEM_SPEC, VMEM_SPEC),
        scratch_shapes=[pltpu.VMEM((rows, block), F32), pltpu.SemaphoreType.DMA],
        compiler_params=params(12),
        name="inverse",
    )(where, corrected)


def pack_body(where, train_ids, basis, tokens, delta, *outs):
    rows = basis.shape[1]
    train, stored = train_ids.shape[0], tokens.shape[0]
    line = lax.broadcasted_iota(jnp.int32, (stored, stored), 0)
    lane = lax.broadcasted_iota(jnp.int32, (stored, stored), 1)
    chosen = jnp.zeros((stored, stored), jnp.bool_)
    for b in range(train):
        chosen = jnp.logical_or(chosen, jnp.logical_and(line == b, lane == train_ids[b]))
    chosen = jnp.where(chosen, 1.0, 0.0).astype(BF)
    gradients = dot(chosen, delta[...], 1, 0).astype(BF)[:train]
    for r, out in enumerate(outs):
        width = out.shape[1]
        block = basis.shape[2]
        skip = block - width
        blk, half = where[1] ^ (r // 2), where[3] ^ (r % 2)
        out[:rows, :] = basis[blk, :, pl.ds(pl.multiple_of(half * skip, LANES), width)]
        own = tokens[:, pl.ds(pl.multiple_of(blk * block, LANES), block)]
        own = dot(chosen, own, 1, 0).astype(BF)[:train]
        out[rows : rows + train, :] = own[:, :width]
        out[rows + train :, :skip] = own[:, width:]
        out[rows + train :, skip:] = gradients


def pack(where, train_ids, basis, tokens, delta, width):
    rows = basis.shape[1] + 2 * train_ids.shape[0]
    return pl.pallas_call(
        pack_body,
        out_shape=tuple(jax.ShapeDtypeStruct((rows, width), BF) for _ in range(4)),
        in_specs=[SMEM_SPEC, SMEM_SPEC, VMEM_SPEC, VMEM_SPEC, VMEM_SPEC],
        out_specs=tuple([VMEM_SPEC] * 4),
        compiler_params=params(4),
        name="pack",
    )(where, train_ids, basis, tokens, delta)


def arrange_body(where, a0, a1, a2, a3, out, *, local, train):
    me = 2 * where[1] + where[3]
    rows = out.shape[0]
    each = local + 2 * train
    to = lax.broadcasted_iota(jnp.int32, (rows, each), 0)
    at = lax.broadcasted_iota(jnp.int32, (rows, each), 1)
    total = None
    for r, part in enumerate((a0, a1, a2, a3)):
        src = me ^ r
        head = src * local + at
        token = 4 * local + src * train + at - local
        other = 4 * local + 4 * train + src * train + at - local - train
        goal = jnp.where(at < local, head, jnp.where(at < local + train, token, other))
        term = dot(jnp.where(goal == to, 1.0, 0.0).astype(BF), part[...], 1, 0)
        total = term if total is None else total + term
    out[...] = total.astype(BF)


def arrange(where, parts, local, train):
    rows, width = parts[0].shape
    return pl.pallas_call(
        functools.partial(arrange_body, local=local, train=train),
        out_shape=jax.ShapeDtypeStruct((4 * rows, width), BF),
        in_specs=[SMEM_SPEC, *([VMEM_SPEC] * 4)],
        out_specs=VMEM_SPEC,
        compiler_params=params(8),
        name="arrange",
    )(where, *parts)


def rotate_body(where, ids, v0, v1, v2, v3, *refs):
    chunks, (basis, right, tokens, delta) = refs[:-4], refs[-4:]
    n_z = len(chunks)
    slab = basis.shape[0] // n_z
    extra = (chunks[0].shape[0] - slab) // 2
    for k, chunk in enumerate(chunks):
        step = k if k <= n_z // 2 else k - n_z
        at = lax.rem(where[0] - step + n_z, n_z) * slab
        basis[pl.ds(pl.multiple_of(at, 16), slab), :] = chunk[:slab, :]
    factors = jnp.concatenate([v[0] for v in (v0, v1, v2, v3)], axis=0)
    whole = basis[...]
    right[...] = dot(factors, whole, 1, 0).astype(BF)
    width = whole.shape[1]
    rest = whole.shape[0] - width
    head = jnp.concatenate([c[slab : slab + extra, :] for c in chunks], axis=0)
    tail = jnp.concatenate([c[slab + extra :, :] for c in chunks], axis=0)
    rotated = dot(head, whole[:width, :], 1, 0) + dot(tail[:, :rest], whole[width:, :], 1, 0)
    tokens[...] = rotated.astype(BF)
    delta[...] = tail[:, rest:]


def rotate(where, query_ids, v_t, chunks, block):
    queries = query_ids.shape[0]
    rank = v_t.shape[1]
    rows, width = chunks[0].shape
    extra = (rows * len(chunks) - block) // 2
    specs = [
        pl.BlockSpec(
            (1, rank, block), functools.partial(lambda q, n, w, ids: (ids[q], 0, w[1]), q)
        )
        for q in range(queries)
    ]

    def full(shape):
        return pl.BlockSpec(shape, lambda n, w, ids: (0, 0))

    shapes = (
        (block, width),
        (queries * rank, width),
        (extra, width),
        (extra, 2 * width - block),
    )
    return pl.pallas_call(
        rotate_body,
        out_shape=tuple(jax.ShapeDtypeStruct(s, BF) for s in shapes),
        grid_spec=pltpu.PrefetchScalarGridSpec(
            num_scalar_prefetch=2,
            grid=(1,),
            in_specs=[*specs, *(full((rows, width)) for _ in chunks)],
            out_specs=tuple(full(s) for s in shapes),
        ),
        compiler_params=params(32),
        name="rotate",
    )(where, query_ids, v_t, v_t, v_t, v_t, *chunks)


def back_terms(right, lefts, windows, inverses, rank, q):
    at = slice(q * rank, (q + 1) * rank)
    total = None
    pieces = len(inverses) // 2
    for k, (left, window) in enumerate(zip(lefts, windows)):
        inverse = jnp.concatenate(
            [i[...] for i in inverses[k * pieces : (k + 1) * pieces]], axis=0
        )
        product = dot(left[at, :], right[at, :], 0, 0)
        precond = (product * inverse.astype(F32)).astype(BF)
        term = dot(window[...], precond, 1, 0)
        total = term if total is None else total + term
    return total


def back_first_body(right, *refs):
    out = refs[6]
    queries = out.shape[0]
    rank = right.shape[0] // queries
    for q in range(queries):
        out[q] = back_terms(right, refs[:2], refs[2:4], refs[4:6], rank, q)


def back_first(right, lefts, windows, inverses, queries):
    width = right.shape[1]
    win, depth = windows[0].shape
    return pl.pallas_call(
        back_first_body,
        out_shape=jax.ShapeDtypeStruct((queries, win, width), F32),
        in_specs=[VMEM_SPEC] * 7,
        out_specs=VMEM_SPEC,
        compiler_params=params(24),
        name="back_first",
    )(right, *lefts, *windows, *inverses)


def back_body(where, block_ids, so_far, factors, right, tokens, delta, *refs, train):
    out, refs = refs[-1], refs[:-1]
    queries = so_far.shape[0]
    n_z, rows, width = out.shape
    win = so_far.shape[1]
    per = win // n_z
    rank = right.shape[0] // queries
    valid = factors.shape[1] // 2
    skip = factors.shape[1] - width
    chosen = block_ids[2 * where[2] + where[1]]
    row = factors[pl.ds(chosen, 1), pl.ds(pl.multiple_of(where[3] * skip, LANES), width)]
    lane = lax.broadcasted_iota(jnp.int32, (1, width), 1)
    first = where[3] * (width - valid)
    mine = jnp.logical_and(lane >= first, lane < first + valid)
    scale = jnp.where(mine, 1.0 / row, 0.0)
    which = lax.rem(lax.broadcasted_iota(jnp.int32, (tokens.shape[0], 1), 0), train)
    scores = []
    for q in range(queries):
        total = so_far[q] + back_terms(right, refs[:2], refs[2:4], refs[4:], rank, q)
        total = (total * scale).astype(BF)
        out[:, q * per : (q + 1) * per, :] = total.reshape(n_z, per, width)
        projected = dot(tokens[...], total, 1, 1) * delta[...].astype(F32)
        scores += [
            jnp.sum(jnp.where(which == b, projected, 0.0), axis=0, keepdims=True)
            for b in range(train)
        ]
    words = []
    for k in range(0, queries * train, 8):
        group = jnp.concatenate(scores[k : k + 8], axis=0)
        high = group.astype(BF)
        words += [high, (group - high.astype(F32)).astype(BF)]
    words.append(jnp.zeros((8, width - len(words) * win), BF))
    extra = jnp.concatenate(words, axis=1)
    for k in range(n_z):
        out[k, queries * per :, :] = extra


def back(where, block_ids, so_far, factors, right, tokens, delta, near, n_z, train):
    queries, win, width = so_far.shape
    depth = near[0].shape[1]
    return pl.pallas_call(
        functools.partial(back_body, train=train),
        out_shape=jax.ShapeDtypeStruct((n_z, queries * win // n_z + 8, width), BF),
        in_specs=[SMEM_SPEC, SMEM_SPEC, *([VMEM_SPEC] * (5 + len(near)))],
        out_specs=VMEM_SPEC,
        compiler_params=params(24),
        name="back",
    )(where, block_ids, so_far, factors, right, tokens, delta, *near)


def tile_body(where, parts, basis, t0, t1, t2, t3, score, *, queries, train):
    n_z = parts.shape[0]
    me = 2 * where[1] + where[3]
    own = t0.shape[0]
    rows = 4 * own
    per = own // queries
    total = parts[0].astype(F32)
    for k in range(1, n_z):
        total += parts[k].astype(F32)
    to = lax.broadcasted_iota(jnp.int32, (rows, rows), 0)
    at = lax.broadcasted_iota(jnp.int32, (rows, rows), 1)
    query = at // own
    owner = lax.rem(at // per, 4)
    goal = (owner ^ me) * own + query * per + lax.rem(at, per)
    select = jnp.where(goal == to, 1.0, 0.0).astype(BF)
    half = dot(select, total[:rows].astype(BF), 1, 0).astype(BF)
    tiles = dot(half, basis[...], 1, 1).astype(BF)
    for r, out in enumerate((t0, t1, t2, t3)):
        out[...] = tiles[r * own : (r + 1) * own]
    words = total[rows:]
    lane = lax.broadcasted_iota(jnp.int32, (1, LANES), 1)
    table = jnp.zeros((1, LANES), F32)
    for k in range(queries * train // 8):
        at = 2 * k * LANES
        sums = words[:, at : at + LANES] + words[:, at + LANES : at + 2 * LANES]
        sums = jnp.sum(sums, axis=1, keepdims=True)
        for i in range(8):
            table = jnp.where(lane == 8 * k + i, sums[i : i + 1], table)
    score[...] = jnp.broadcast_to(table[None], score.shape)


def tile_part(where, parts, basis, plane, queries, train):
    own = (parts.shape[1] - 8) // 4
    block = basis.shape[0]
    return pl.pallas_call(
        functools.partial(tile_body, queries=queries, train=train),
        out_shape=(
            *(jax.ShapeDtypeStruct((own, block), BF) for _ in range(4)),
            jax.ShapeDtypeStruct((plane, 1, LANES), F32),
        ),
        in_specs=[SMEM_SPEC, VMEM_SPEC, VMEM_SPEC],
        out_specs=tuple([VMEM_SPEC] * 5),
        compiler_params=params(24),
        name="tile",
    )(where, parts, basis)


def final_body(where, t0, t1, t2, t3, score, tiles, scores):
    queries, per, columns = tiles.shape
    block = columns // 2
    for r, (a, b) in enumerate(((t0, t1), (t2, t3))):
        total = (a[...].astype(F32) + b[...].astype(F32)).astype(BF)
        at = pl.multiple_of((where[1] ^ r) * block, LANES)
        for q in range(queries):
            tiles[q, :, pl.ds(at, block)] = total[q * per : (q + 1) * per]
    sums = jnp.sum(score[...], axis=0)
    train = scores.shape[1]
    for q in range(queries):
        scores[q : q + 1, :] = sums[:, q * train : (q + 1) * train]


def final(where, parts, score, queries, train):
    own, block = parts[0].shape
    return pl.pallas_call(
        final_body,
        out_shape=(
            jax.ShapeDtypeStruct((queries, own // queries, 2 * block), BF),
            jax.ShapeDtypeStruct((queries, train), F32),
        ),
        in_specs=[SMEM_SPEC, *([VMEM_SPEC] * 5)],
        out_specs=(VMEM_SPEC, VMEM_SPEC),
        compiler_params=params(4),
        name="final",
    )(where, *parts, score)


def shards(
    basis_out,
    corrected,
    factor_table,
    block_ids,
    basis_in,
    query_ids,
    u_pool,
    v_pool,
    train_ids,
    x_pool,
    delta_pool,
):
    n_z, n_in = lax.axis_size("z"), lax.axis_size(IN)
    z, xh, c = lax.axis_index("z"), lax.axis_index("xh"), lax.axis_index("c")
    in_pos = lax.axis_index(IN)
    queries, train = query_ids.shape[0], train_ids.shape[0]
    _, local_rows, block = basis_in.shape
    width = -(-(block // 2) // LANES) * LANES
    where = jnp.stack([z, xh, in_pos, c]).astype(jnp.int32)

    packed = pack(where, train_ids, basis_in, x_pool[:, 0], delta_pool[:, 0], width)
    parts = (
        packed[0],
        swap(packed[1], "c"),
        swap(packed[2], "xh"),
        swap(packed[3], QUAD, 3),
    )
    pieces = n_z // 2
    far = [inverse_halves(where, corrected, block, width, 1, pieces, k) for k in range(pieces)]
    own = arrange(where, (after(packed[0], far[0][0]), *parts[1:]), local_rows, train)
    far = [(swap(a, "xh"), swap(b, QUAD, 3)) for a, b in far]
    near = inverse_halves(where, corrected, block, width, 0)
    near = (near[0], swap(near[1], "c"))

    partial = left_part(query_ids, jnp.transpose(u_pool, (0, 2, 1)), basis_out, n_in)
    ahead, behind = [shift(own, 1)], [shift(own, -1)]
    up, down = after((ahead[0], behind[0]), far[0], partial)
    ahead.append(shift(up, 1))
    behind.append(shift(down, -1))
    spread, window = left_sum(exchange(partial, IN))
    up, down = after((ahead[1], behind[1]), far[1], spread)
    ahead.append(shift(up, 1))
    behind.append(shift(down, -1))
    left = exchange(spread, IN).reshape(-1, basis_out.shape[1])
    up, left, window = after((ahead[2], left, window), behind[2], far[2])
    ahead.append(shift(up, 1))
    left_x, window_x = swap(left, "xh"), swap(window, "xh")
    lefts = (left, swap(left, "c"))
    windows = (window, swap(window, "c"))
    chunks = (own, *ahead[:3], after(ahead[3], far[3]), *behind[::-1])

    basis, right, tokens, delta = rotate(
        where, query_ids, jnp.transpose(v_pool, (0, 2, 1)), chunks, block
    )
    so_far = back_first(right, lefts, windows, near, queries)
    left_x, window_x = after((left_x, window_x), so_far)
    far = (
        *(left_x, swap(left_x, "c"), window_x, swap(window_x, "c")),
        *(a for a, _ in far),
        *(b for _, b in far),
    )
    parts = back(
        where, block_ids, so_far, factor_table, right, tokens, delta, far, n_z, train
    )
    *parts, score = tile_part(
        where, exchange(parts, "z"), basis, lax.axis_size(PLANE), queries, train
    )
    parts = (
        parts[0],
        swap(parts[1], "c"),
        swap(parts[2], "xh"),
        swap(parts[3], QUAD, 3),
    )
    return final(where, parts, exchange(score, PLANE), queries, train)


def solution(mesh):
    split = Mesh(mesh.devices.reshape(8, 2, 2, 4, 2), ("z", "xh", "c", "y", "xl"))
    return jax.shard_map(
        shards,
        mesh=split,
        in_specs=(
            P(IN, OUT),
            P(OUT, IN),
            P(),
            P(),
            P(IN, OUT, None),
            P(),
            P(None, IN, None),
            P(None, IN, None),
            P(),
            P(None, OUT, IN),
            P(None, OUT, None),
        ),
        out_specs=(P(None, OUT, IN), P()),
        check_vma=False,
    )
```

```python
import functools

import jax
import jax.numpy as jnp
from jax import lax
from jax.experimental import pallas as pl
from jax.experimental.pallas import tpu as pltpu
from jax.sharding import Mesh
from jax.sharding import PartitionSpec as P

WIN_ROWS = 16
OUT = ("z", "xh", "c")
IN = ("y", "xl")
QUAD = ("xh", "c")
PLANE = ("xh", "c", "y", "xl")
BF = jnp.bfloat16
F32 = jnp.float32
LANES = 128
MIB = 2**20

VMEM_SPEC = pl.BlockSpec(memory_space=pltpu.VMEM)
SMEM_SPEC = pl.BlockSpec(memory_space=pltpu.SMEM)


def params(mib):
    return pltpu.CompilerParams(vmem_limit_bytes=mib * MIB)


def dot(a, b, ca, cb):
    return lax.dot_general(a, b, (((ca,), (cb,)), ((), ())), preferred_element_type=F32)


def exchange(value, axis):
    return lax.all_to_all(value, axis, split_axis=0, concat_axis=0, tiled=True)


def swap(value, axis, mask=1):
    size = lax.axis_size(axis)
    return lax.ppermute(value, axis, [(i, i ^ mask) for i in range(size)])


def shift(value, step):
    size = lax.axis_size("z")
    return lax.ppermute(value, "z", [(i, (i + step) % size) for i in range(size)])


def after(value, *others):
    return lax.optimization_barrier((value, others))[0]


def left_body(ids, u0, u1, u2, u3, basis, out):
    left = jnp.concatenate([u[0] for u in (u0, u1, u2, u3)], axis=0)
    n_in, rows, width = out.shape
    part = dot(left, basis[...], 1, 0).astype(BF)
    out[:, : rows - WIN_ROWS, :] = part.reshape(n_in, rows - WIN_ROWS, width)
    out[:, rows - WIN_ROWS :, :] = jnp.broadcast_to(
        basis[:WIN_ROWS, :][None], (n_in, WIN_ROWS, width)
    )


def left_part(query_ids, u_t, basis_out, n_in):
    queries = query_ids.shape[0]
    _, rank, depth = u_t.shape
    eigen = basis_out.shape[1]
    rows = queries * rank // n_in + WIN_ROWS
    tile = 256
    specs = [
        pl.BlockSpec((1, rank, depth), functools.partial(lambda q, n, ids: (ids[q], 0, 0), q))
        for q in range(queries)
    ]
    return pl.pallas_call(
        left_body,
        out_shape=jax.ShapeDtypeStruct((n_in, rows, eigen), BF),
        grid_spec=pltpu.PrefetchScalarGridSpec(
            num_scalar_prefetch=1,
            grid=(eigen // tile,),
            in_specs=[*specs, pl.BlockSpec((depth, tile), lambda n, ids: (0, n))],
            out_specs=pl.BlockSpec((n_in, rows, tile), lambda n, ids: (0, 0, n)),
        ),
        compiler_params=params(16),
        name="left",
    )(query_ids, u_t, u_t, u_t, u_t, basis_out)


def left_sum_body(parts, out, window):
    n_in, rows, _ = parts.shape
    own = rows - WIN_ROWS
    total = parts[0, :own, :].astype(F32)
    for i in range(1, n_in):
        total += parts[i, :own, :].astype(F32)
    total = total.astype(BF)
    for i in range(n_in):
        out[i] = total
        window[i * WIN_ROWS : (i + 1) * WIN_ROWS, :] = parts[i, own:, :]


def left_sum(parts):
    n_in, rows, eigen = parts.shape
    return pl.pallas_call(
        left_sum_body,
        out_shape=(
            jax.ShapeDtypeStruct((n_in, rows - WIN_ROWS, eigen), BF),
            jax.ShapeDtypeStruct((n_in * WIN_ROWS, eigen), BF),
        ),
        in_specs=[VMEM_SPEC],
        out_specs=(VMEM_SPEC, VMEM_SPEC),
        compiler_params=params(4),
        name="left_sum",
    )(parts)


def inverse_body(where, corrected, *outs):
    width = outs[0].shape[1]
    skip = corrected.shape[1] - width
    for r, out in enumerate(outs):
        at = pl.multiple_of((where[3] ^ r) * skip, LANES) if skip else 0
        out[...] = (1.0 / corrected[:, pl.ds(at, width)]).astype(BF)


def inverse_block(where, corrected, block, far, width, count):
    rows = corrected.shape[0]
    tile = 128
    return pl.pallas_call(
        inverse_body,
        out_shape=tuple(jax.ShapeDtypeStruct((rows, width), BF) for _ in range(count)),
        grid_spec=pltpu.PrefetchScalarGridSpec(
            num_scalar_prefetch=1,
            grid=(rows // tile,),
            in_specs=[pl.BlockSpec((tile, block), lambda n, w: (n, w[1] ^ far))],
            out_specs=tuple(
                pl.BlockSpec((tile, width), lambda n, w: (n, 0)) for _ in range(count)
            ),
        ),
        compiler_params=params(58),
        name="inverse",
    )(where, corrected)


def halves_body(where, block, own, other):
    width = own.shape[1]
    skip = block.shape[1] - width
    for r, out in enumerate((own, other)):
        out[...] = block[:, pl.ds(pl.multiple_of((where[3] ^ r) * skip, LANES), width)]


def halves(where, block, width):
    return pl.pallas_call(
        halves_body,
        out_shape=tuple(jax.ShapeDtypeStruct((block.shape[0], width), BF) for _ in range(2)),
        in_specs=[SMEM_SPEC, VMEM_SPEC],
        out_specs=(VMEM_SPEC, VMEM_SPEC),
        compiler_params=params(10),
        name="halves",
    )(where, block)


def pack_body(where, train_ids, basis, tokens, delta, *outs):
    rows = basis.shape[1]
    train, stored = train_ids.shape[0], tokens.shape[0]
    line = lax.broadcasted_iota(jnp.int32, (stored, stored), 0)
    lane = lax.broadcasted_iota(jnp.int32, (stored, stored), 1)
    chosen = jnp.zeros((stored, stored), jnp.bool_)
    for b in range(train):
        chosen = jnp.logical_or(chosen, jnp.logical_and(line == b, lane == train_ids[b]))
    chosen = jnp.where(chosen, 1.0, 0.0).astype(BF)
    gradients = dot(chosen, delta[...], 1, 0).astype(BF)[:train]
    for r, out in enumerate(outs):
        width = out.shape[1]
        block = basis.shape[2]
        skip = block - width
        blk, half = where[1] ^ (r // 2), where[3] ^ (r % 2)
        out[:rows, :] = basis[blk, :, pl.ds(pl.multiple_of(half * skip, LANES), width)]
        own = tokens[:, pl.ds(pl.multiple_of(blk * block, LANES), block)]
        own = dot(chosen, own, 1, 0).astype(BF)[:train]
        out[rows : rows + train, :] = own[:, :width]
        out[rows + train :, :skip] = own[:, width:]
        out[rows + train :, skip:] = gradients


def pack(where, train_ids, basis, tokens, delta, width):
    rows = basis.shape[1] + 2 * train_ids.shape[0]
    return pl.pallas_call(
        pack_body,
        out_shape=tuple(jax.ShapeDtypeStruct((rows, width), BF) for _ in range(4)),
        in_specs=[SMEM_SPEC, SMEM_SPEC, VMEM_SPEC, VMEM_SPEC, VMEM_SPEC],
        out_specs=tuple([VMEM_SPEC] * 4),
        compiler_params=params(4),
        name="pack",
    )(where, train_ids, basis, tokens, delta)


def arrange_body(where, a0, a1, a2, a3, out, *, local, train):
    me = 2 * where[1] + where[3]
    rows = out.shape[0]
    each = local + 2 * train
    to = lax.broadcasted_iota(jnp.int32, (rows, each), 0)
    at = lax.broadcasted_iota(jnp.int32, (rows, each), 1)
    total = None
    for r, part in enumerate((a0, a1, a2, a3)):
        src = me ^ r
        head = src * local + at
        token = 4 * local + src * train + at - local
        other = 4 * local + 4 * train + src * train + at - local - train
        goal = jnp.where(at < local, head, jnp.where(at < local + train, token, other))
        term = dot(jnp.where(goal == to, 1.0, 0.0).astype(BF), part[...], 1, 0)
        total = term if total is None else total + term
    out[...] = total.astype(BF)


def arrange(where, parts, local, train):
    rows, width = parts[0].shape
    return pl.pallas_call(
        functools.partial(arrange_body, local=local, train=train),
        out_shape=jax.ShapeDtypeStruct((4 * rows, width), BF),
        in_specs=[SMEM_SPEC, *([VMEM_SPEC] * 4)],
        out_specs=VMEM_SPEC,
        compiler_params=params(8),
        name="arrange",
    )(where, *parts)


def rotate_body(where, ids, v0, v1, v2, v3, *refs):
    chunks, (basis, right, tokens, delta) = refs[:-4], refs[-4:]
    n_z = len(chunks)
    slab = basis.shape[0] // n_z
    extra = (chunks[0].shape[0] - slab) // 2
    for k, chunk in enumerate(chunks):
        step = k if k <= n_z // 2 else k - n_z
        at = lax.rem(where[0] - step + n_z, n_z) * slab
        basis[pl.ds(pl.multiple_of(at, 16), slab), :] = chunk[:slab, :]
    factors = jnp.concatenate([v[0] for v in (v0, v1, v2, v3)], axis=0)
    whole = basis[...]
    right[...] = dot(factors, whole, 1, 0).astype(BF)
    width = whole.shape[1]
    rest = whole.shape[0] - width
    head = jnp.concatenate([c[slab : slab + extra, :] for c in chunks], axis=0)
    tail = jnp.concatenate([c[slab + extra :, :] for c in chunks], axis=0)
    rotated = dot(head, whole[:width, :], 1, 0) + dot(tail[:, :rest], whole[width:, :], 1, 0)
    tokens[...] = rotated.astype(BF)
    delta[...] = tail[:, rest:]


def rotate(where, query_ids, v_t, chunks, block):
    queries = query_ids.shape[0]
    rank = v_t.shape[1]
    rows, width = chunks[0].shape
    extra = (rows * len(chunks) - block) // 2
    specs = [
        pl.BlockSpec(
            (1, rank, block), functools.partial(lambda q, n, w, ids: (ids[q], 0, w[1]), q)
        )
        for q in range(queries)
    ]

    def full(shape):
        return pl.BlockSpec(shape, lambda n, w, ids: (0, 0))

    shapes = (
        (block, width),
        (queries * rank, width),
        (extra, width),
        (extra, 2 * width - block),
    )
    return pl.pallas_call(
        rotate_body,
        out_shape=tuple(jax.ShapeDtypeStruct(s, BF) for s in shapes),
        grid_spec=pltpu.PrefetchScalarGridSpec(
            num_scalar_prefetch=2,
            grid=(1,),
            in_specs=[*specs, *(full((rows, width)) for _ in chunks)],
            out_specs=tuple(full(s) for s in shapes),
        ),
        compiler_params=params(32),
        name="rotate",
    )(where, query_ids, v_t, v_t, v_t, v_t, *chunks)


def back_terms(right, lefts, windows, inverses, rank, q):
    at = slice(q * rank, (q + 1) * rank)
    total = None
    pieces = len(inverses) // 2
    for k, (left, window) in enumerate(zip(lefts, windows)):
        inverse = jnp.concatenate(
            [i[...] for i in inverses[k * pieces : (k + 1) * pieces]], axis=0
        )
        product = dot(left[at, :], right[at, :], 0, 0)
        precond = (product * inverse.astype(F32)).astype(BF)
        term = dot(window[...], precond, 1, 0)
        total = term if total is None else total + term
    return total


def back_first_body(right, *refs):
    out = refs[6]
    queries = out.shape[0]
    rank = right.shape[0] // queries
    for q in range(queries):
        out[q] = back_terms(right, refs[:2], refs[2:4], refs[4:6], rank, q)


def back_first(right, lefts, windows, inverses, queries):
    width = right.shape[1]
    win, depth = windows[0].shape
    return pl.pallas_call(
        back_first_body,
        out_shape=jax.ShapeDtypeStruct((queries, win, width), F32),
        in_specs=[VMEM_SPEC] * 7,
        out_specs=VMEM_SPEC,
        compiler_params=params(24),
        name="back_first",
    )(right, *lefts, *windows, *inverses)


def back_body(where, block_ids, so_far, factors, right, tokens, delta, *refs, train):
    out, refs = refs[-1], refs[:-1]
    queries = so_far.shape[0]
    n_z, rows, width = out.shape
    win = so_far.shape[1]
    per = win // n_z
    rank = right.shape[0] // queries
    valid = factors.shape[1] // 2
    skip = factors.shape[1] - width
    chosen = block_ids[2 * where[2] + where[1]]
    row = factors[pl.ds(chosen, 1), pl.ds(pl.multiple_of(where[3] * skip, LANES), width)]
    lane = lax.broadcasted_iota(jnp.int32, (1, width), 1)
    first = where[3] * (width - valid)
    mine = jnp.logical_and(lane >= first, lane < first + valid)
    scale = jnp.where(mine, 1.0 / row, 0.0)
    which = lax.rem(lax.broadcasted_iota(jnp.int32, (tokens.shape[0], 1), 0), train)
    scores = []
    for q in range(queries):
        total = so_far[q] + back_terms(right, refs[:2], refs[2:4], refs[4:], rank, q)
        total = (total * scale).astype(BF)
        out[:, q * per : (q + 1) * per, :] = total.reshape(n_z, per, width)
        projected = dot(tokens[...], total, 1, 1) * delta[...].astype(F32)
        scores += [
            jnp.sum(jnp.where(which == b, projected, 0.0), axis=0, keepdims=True)
            for b in range(train)
        ]
    words = []
    for k in range(0, queries * train, 8):
        group = jnp.concatenate(scores[k : k + 8], axis=0)
        high = group.astype(BF)
        words += [high, (group - high.astype(F32)).astype(BF)]
    words.append(jnp.zeros((8, width - len(words) * win), BF))
    extra = jnp.concatenate(words, axis=1)
    for k in range(n_z):
        out[k, queries * per :, :] = extra


def back(where, block_ids, so_far, factors, right, tokens, delta, near, n_z, train):
    queries, win, width = so_far.shape
    depth = near[0].shape[1]
    return pl.pallas_call(
        functools.partial(back_body, train=train),
        out_shape=jax.ShapeDtypeStruct((n_z, queries * win // n_z + 8, width), BF),
        in_specs=[SMEM_SPEC, SMEM_SPEC, *([VMEM_SPEC] * (5 + len(near)))],
        out_specs=VMEM_SPEC,
        compiler_params=params(24),
        name="back",
    )(where, block_ids, so_far, factors, right, tokens, delta, *near)


def tile_body(where, parts, basis, t0, t1, t2, t3, score, *, queries, train):
    n_z = parts.shape[0]
    me = 2 * where[1] + where[3]
    own = t0.shape[0]
    rows = 4 * own
    per = own // queries
    total = parts[0].astype(F32)
    for k in range(1, n_z):
        total += parts[k].astype(F32)
    to = lax.broadcasted_iota(jnp.int32, (rows, rows), 0)
    at = lax.broadcasted_iota(jnp.int32, (rows, rows), 1)
    query = at // own
    owner = lax.rem(at // per, 4)
    goal = (owner ^ me) * own + query * per + lax.rem(at, per)
    select = jnp.where(goal == to, 1.0, 0.0).astype(BF)
    half = dot(select, total[:rows].astype(BF), 1, 0).astype(BF)
    tiles = dot(half, basis[...], 1, 1).astype(BF)
    for r, out in enumerate((t0, t1, t2, t3)):
        out[...] = tiles[r * own : (r + 1) * own]
    words = total[rows:]
    lane = lax.broadcasted_iota(jnp.int32, (1, LANES), 1)
    table = jnp.zeros((1, LANES), F32)
    for k in range(queries * train // 8):
        at = 2 * k * LANES
        sums = words[:, at : at + LANES] + words[:, at + LANES : at + 2 * LANES]
        sums = jnp.sum(sums, axis=1, keepdims=True)
        for i in range(8):
            table = jnp.where(lane == 8 * k + i, sums[i : i + 1], table)
    score[...] = jnp.broadcast_to(table[None], score.shape)


def tile_part(where, parts, basis, plane, queries, train):
    own = (parts.shape[1] - 8) // 4
    block = basis.shape[0]
    return pl.pallas_call(
        functools.partial(tile_body, queries=queries, train=train),
        out_shape=(
            *(jax.ShapeDtypeStruct((own, block), BF) for _ in range(4)),
            jax.ShapeDtypeStruct((plane, 1, LANES), F32),
        ),
        in_specs=[SMEM_SPEC, VMEM_SPEC, VMEM_SPEC],
        out_specs=tuple([VMEM_SPEC] * 5),
        compiler_params=params(24),
        name="tile",
    )(where, parts, basis)


def final_body(where, t0, t1, t2, t3, score, tiles, scores):
    queries, per, columns = tiles.shape
    block = columns // 2
    for r, (a, b) in enumerate(((t0, t1), (t2, t3))):
        total = (a[...].astype(F32) + b[...].astype(F32)).astype(BF)
        at = pl.multiple_of((where[1] ^ r) * block, LANES)
        for q in range(queries):
            tiles[q, :, pl.ds(at, block)] = total[q * per : (q + 1) * per]
    sums = jnp.sum(score[...], axis=0)
    train = scores.shape[1]
    for q in range(queries):
        scores[q : q + 1, :] = sums[:, q * train : (q + 1) * train]


def final(where, parts, score, queries, train):
    own, block = parts[0].shape
    return pl.pallas_call(
        final_body,
        out_shape=(
            jax.ShapeDtypeStruct((queries, own // queries, 2 * block), BF),
            jax.ShapeDtypeStruct((queries, train), F32),
        ),
        in_specs=[SMEM_SPEC, *([VMEM_SPEC] * 5)],
        out_specs=(VMEM_SPEC, VMEM_SPEC),
        compiler_params=params(4),
        name="final",
    )(where, *parts, score)


def shards(
    basis_out,
    corrected,
    factor_table,
    block_ids,
    basis_in,
    query_ids,
    u_pool,
    v_pool,
    train_ids,
    x_pool,
    delta_pool,
):
    n_z, n_in = lax.axis_size("z"), lax.axis_size(IN)
    z, xh, c = lax.axis_index("z"), lax.axis_index("xh"), lax.axis_index("c")
    in_pos = lax.axis_index(IN)
    queries, train = query_ids.shape[0], train_ids.shape[0]
    _, local_rows, block = basis_in.shape
    width = -(-(block // 2) // LANES) * LANES
    where = jnp.stack([z, xh, in_pos, c]).astype(jnp.int32)

    packed = pack(where, train_ids, basis_in, x_pool[:, 0], delta_pool[:, 0], width)
    parts = (
        packed[0],
        swap(packed[1], "c"),
        swap(packed[2], "xh"),
        swap(packed[3], QUAD, 3),
    )
    (far,) = inverse_block(where, corrected, block, 1, block, 1)
    own = arrange(where, (after(packed[0], far), *parts[1:]), local_rows, train)
    far = swap(far, "xh")
    near = inverse_block(where, corrected, block, 0, width, 2)
    near = (near[0], swap(near[1], "c"))

    partial = left_part(query_ids, jnp.transpose(u_pool, (0, 2, 1)), basis_out, n_in)
    ahead, behind = [shift(own, 1)], [shift(own, -1)]
    up, down = after((ahead[0], behind[0]), partial)
    ahead.append(shift(up, 1))
    behind.append(shift(down, -1))
    spread, window = left_sum(exchange(partial, IN))
    up, down = after((ahead[1], behind[1]), spread)
    ahead.append(shift(up, 1))
    behind.append(shift(down, -1))
    left = exchange(spread, IN).reshape(-1, basis_out.shape[1])
    up, left, window = after((ahead[2], left, window), behind[2])
    ahead.append(shift(up, 1))
    left_x, window_x = swap(left, "xh"), swap(window, "xh")
    lefts = (left, swap(left, "c"))
    windows = (window, swap(window, "c"))
    chunks = (own, *ahead, *behind[::-1])

    basis, right, tokens, delta = rotate(
        where, query_ids, jnp.transpose(v_pool, (0, 2, 1)), chunks, block
    )
    so_far = back_first(right, lefts, windows, near, queries)
    left_x, window_x, far = after((left_x, window_x, far), so_far)
    far = halves(where, far, width)
    far = (left_x, swap(left_x, "c"), window_x, swap(window_x, "c"), far[0], swap(far[1], "c"))
    parts = back(
        where, block_ids, so_far, factor_table, right, tokens, delta, far, n_z, train
    )
    *parts, score = tile_part(
        where, exchange(parts, "z"), basis, lax.axis_size(PLANE), queries, train
    )
    parts = (
        parts[0],
        swap(parts[1], "c"),
        swap(parts[2], "xh"),
        swap(parts[3], QUAD, 3),
    )
    return final(where, parts, exchange(score, PLANE), queries, train)


def solution(mesh):
    split = Mesh(mesh.devices.reshape(8, 2, 2, 4, 2), ("z", "xh", "c", "y", "xl"))
    return jax.shard_map(
        shards,
        mesh=split,
        in_specs=(
            P(IN, OUT),
            P(OUT, IN),
            P(),
            P(),
            P(IN, OUT, None),
            P(),
            P(None, IN, None),
            P(None, IN, None),
            P(),
            P(None, OUT, IN),
            P(None, OUT, None),
        ),
        out_specs=(P(None, OUT, IN), P()),
        check_vma=False,
    )
```

```python
import functools

import jax
import jax.numpy as jnp
from jax import lax
from jax.experimental import pallas as pl
from jax.experimental.pallas import tpu as pltpu
from jax.sharding import Mesh
from jax.sharding import PartitionSpec as P

WIN_ROWS = 16
OUT = ("z", "xh", "c")
IN = ("y", "xl")
QUAD = ("xh", "c")
PLANE = ("xh", "c", "y", "xl")
BF = jnp.bfloat16
F32 = jnp.float32
LANES = 128
MIB = 2**20

VMEM_SPEC = pl.BlockSpec(memory_space=pltpu.VMEM)
SMEM_SPEC = pl.BlockSpec(memory_space=pltpu.SMEM)


def params(mib):
    return pltpu.CompilerParams(vmem_limit_bytes=mib * MIB)


def dot(a, b, ca, cb):
    return lax.dot_general(a, b, (((ca,), (cb,)), ((), ())), preferred_element_type=F32)


def exchange(value, axis):
    return lax.all_to_all(value, axis, split_axis=0, concat_axis=0, tiled=True)


def swap(value, axis, mask=1):
    size = lax.axis_size(axis)
    return lax.ppermute(value, axis, [(i, i ^ mask) for i in range(size)])


def shift(value, step):
    size = lax.axis_size("z")
    return lax.ppermute(value, "z", [(i, (i + step) % size) for i in range(size)])


def after(value, *others):
    return lax.optimization_barrier((value, others))[0]


def left_body(ids, u0, u1, u2, u3, basis, out):
    left = jnp.concatenate([u[0] for u in (u0, u1, u2, u3)], axis=0)
    n_in, rows, width = out.shape
    part = dot(left, basis[...], 1, 0).astype(BF)
    out[:, : rows - WIN_ROWS, :] = part.reshape(n_in, rows - WIN_ROWS, width)
    out[:, rows - WIN_ROWS :, :] = jnp.broadcast_to(
        basis[:WIN_ROWS, :][None], (n_in, WIN_ROWS, width)
    )


def left_part(query_ids, u_t, basis_out, n_in):
    queries = query_ids.shape[0]
    _, rank, depth = u_t.shape
    eigen = basis_out.shape[1]
    rows = queries * rank // n_in + WIN_ROWS
    tile = 256
    specs = [
        pl.BlockSpec((1, rank, depth), functools.partial(lambda q, n, ids: (ids[q], 0, 0), q))
        for q in range(queries)
    ]
    return pl.pallas_call(
        left_body,
        out_shape=jax.ShapeDtypeStruct((n_in, rows, eigen), BF),
        grid_spec=pltpu.PrefetchScalarGridSpec(
            num_scalar_prefetch=1,
            grid=(eigen // tile,),
            in_specs=[*specs, pl.BlockSpec((depth, tile), lambda n, ids: (0, n))],
            out_specs=pl.BlockSpec((n_in, rows, tile), lambda n, ids: (0, 0, n)),
        ),
        compiler_params=params(16),
        name="left",
    )(query_ids, u_t, u_t, u_t, u_t, basis_out)


def left_sum_body(parts, out, window):
    n_in, rows, _ = parts.shape
    own = rows - WIN_ROWS
    total = parts[0, :own, :].astype(F32)
    for i in range(1, n_in):
        total += parts[i, :own, :].astype(F32)
    total = total.astype(BF)
    for i in range(n_in):
        out[i] = total
        window[i * WIN_ROWS : (i + 1) * WIN_ROWS, :] = parts[i, own:, :]


def left_sum(parts):
    n_in, rows, eigen = parts.shape
    return pl.pallas_call(
        left_sum_body,
        out_shape=(
            jax.ShapeDtypeStruct((n_in, rows - WIN_ROWS, eigen), BF),
            jax.ShapeDtypeStruct((n_in * WIN_ROWS, eigen), BF),
        ),
        in_specs=[VMEM_SPEC],
        out_specs=(VMEM_SPEC, VMEM_SPEC),
        compiler_params=params(4),
        name="left_sum",
    )(parts)


def inverse_body(where, corrected, *outs):
    width = outs[0].shape[1]
    skip = corrected.shape[1] - width
    for r, out in enumerate(outs):
        at = pl.multiple_of((where[3] ^ r) * skip, LANES) if skip else 0
        out[...] = (1.0 / corrected[:, pl.ds(at, width)]).astype(BF)


def inverse_block(where, corrected, block, far, width, count, start=0, stop=None):
    tile = 64
    first = start // tile
    rows = (stop or corrected.shape[0]) - start
    return pl.pallas_call(
        inverse_body,
        out_shape=tuple(jax.ShapeDtypeStruct((rows, width), BF) for _ in range(count)),
        grid_spec=pltpu.PrefetchScalarGridSpec(
            num_scalar_prefetch=1,
            grid=(rows // tile,),
            in_specs=[pl.BlockSpec((tile, block), lambda n, w: (first + n, w[1] ^ far))],
            out_specs=tuple(
                pl.BlockSpec((tile, width), lambda n, w: (n, 0)) for _ in range(count)
            ),
        ),
        compiler_params=params(58),
        name="inverse",
    )(where, corrected)


def halves_body(where, *refs):
    pieces, (own, other) = refs[:-2], refs[-2:]
    width = own.shape[1]
    first = 0
    for piece in pieces:
        rows, block = piece.shape
        for r, out in enumerate((own, other)):
            at = pl.multiple_of((where[3] ^ r) * (block - width), LANES)
            out[first : first + rows, :] = piece[:, pl.ds(at, width)]
        first += rows


def halves(where, pieces, width):
    rows = sum(p.shape[0] for p in pieces)
    return pl.pallas_call(
        halves_body,
        out_shape=tuple(jax.ShapeDtypeStruct((rows, width), BF) for _ in range(2)),
        in_specs=[SMEM_SPEC, *([VMEM_SPEC] * len(pieces))],
        out_specs=(VMEM_SPEC, VMEM_SPEC),
        compiler_params=params(10),
        name="halves",
    )(where, *pieces)


def pack_body(where, train_ids, basis, tokens, delta, *outs):
    rows = basis.shape[1]
    train, stored = train_ids.shape[0], tokens.shape[0]
    line = lax.broadcasted_iota(jnp.int32, (stored, stored), 0)
    lane = lax.broadcasted_iota(jnp.int32, (stored, stored), 1)
    chosen = jnp.zeros((stored, stored), jnp.bool_)
    for b in range(train):
        chosen = jnp.logical_or(chosen, jnp.logical_and(line == b, lane == train_ids[b]))
    chosen = jnp.where(chosen, 1.0, 0.0).astype(BF)
    gradients = dot(chosen, delta[...], 1, 0).astype(BF)[:train]
    for r, out in enumerate(outs):
        width = out.shape[1]
        block = basis.shape[2]
        skip = block - width
        blk, half = where[1] ^ (r // 2), where[3] ^ (r % 2)
        out[:rows, :] = basis[blk, :, pl.ds(pl.multiple_of(half * skip, LANES), width)]
        own = tokens[:, pl.ds(pl.multiple_of(blk * block, LANES), block)]
        own = dot(chosen, own, 1, 0).astype(BF)[:train]
        out[rows : rows + train, :] = own[:, :width]
        out[rows + train :, :skip] = own[:, width:]
        out[rows + train :, skip:] = gradients


def pack(where, train_ids, basis, tokens, delta, width):
    rows = basis.shape[1] + 2 * train_ids.shape[0]
    return pl.pallas_call(
        pack_body,
        out_shape=tuple(jax.ShapeDtypeStruct((rows, width), BF) for _ in range(4)),
        in_specs=[SMEM_SPEC, SMEM_SPEC, VMEM_SPEC, VMEM_SPEC, VMEM_SPEC],
        out_specs=tuple([VMEM_SPEC] * 4),
        compiler_params=params(4),
        name="pack",
    )(where, train_ids, basis, tokens, delta)


def arrange_body(where, a0, a1, a2, a3, out, *, local, train):
    me = 2 * where[1] + where[3]
    rows = out.shape[0]
    each = local + 2 * train
    to = lax.broadcasted_iota(jnp.int32, (rows, each), 0)
    at = lax.broadcasted_iota(jnp.int32, (rows, each), 1)
    total = None
    for r, part in enumerate((a0, a1, a2, a3)):
        src = me ^ r
        head = src * local + at
        token = 4 * local + src * train + at - local
        other = 4 * local + 4 * train + src * train + at - local - train
        goal = jnp.where(at < local, head, jnp.where(at < local + train, token, other))
        term = dot(jnp.where(goal == to, 1.0, 0.0).astype(BF), part[...], 1, 0)
        total = term if total is None else total + term
    out[...] = total.astype(BF)


def arrange(where, parts, local, train):
    rows, width = parts[0].shape
    return pl.pallas_call(
        functools.partial(arrange_body, local=local, train=train),
        out_shape=jax.ShapeDtypeStruct((4 * rows, width), BF),
        in_specs=[SMEM_SPEC, *([VMEM_SPEC] * 4)],
        out_specs=VMEM_SPEC,
        compiler_params=params(8),
        name="arrange",
    )(where, *parts)


def rotate_body(where, ids, v0, v1, v2, v3, *refs):
    chunks, (basis, right, tokens, delta) = refs[:-4], refs[-4:]
    n_z = len(chunks)
    slab = basis.shape[0] // n_z
    extra = (chunks[0].shape[0] - slab) // 2
    for k, chunk in enumerate(chunks):
        step = k if k <= n_z // 2 else k - n_z
        at = lax.rem(where[0] - step + n_z, n_z) * slab
        basis[pl.ds(pl.multiple_of(at, 16), slab), :] = chunk[:slab, :]
    factors = jnp.concatenate([v[0] for v in (v0, v1, v2, v3)], axis=0)
    whole = basis[...]
    right[...] = dot(factors, whole, 1, 0).astype(BF)
    width = whole.shape[1]
    rest = whole.shape[0] - width
    head = jnp.concatenate([c[slab : slab + extra, :] for c in chunks], axis=0)
    tail = jnp.concatenate([c[slab + extra :, :] for c in chunks], axis=0)
    rotated = dot(head, whole[:width, :], 1, 0) + dot(tail[:, :rest], whole[width:, :], 1, 0)
    tokens[...] = rotated.astype(BF)
    delta[...] = tail[:, rest:]


def rotate(where, query_ids, v_t, chunks, block):
    queries = query_ids.shape[0]
    rank = v_t.shape[1]
    rows, width = chunks[0].shape
    extra = (rows * len(chunks) - block) // 2
    specs = [
        pl.BlockSpec(
            (1, rank, block), functools.partial(lambda q, n, w, ids: (ids[q], 0, w[1]), q)
        )
        for q in range(queries)
    ]

    def full(shape):
        return pl.BlockSpec(shape, lambda n, w, ids: (0, 0))

    shapes = (
        (block, width),
        (queries * rank, width),
        (extra, width),
        (extra, 2 * width - block),
    )
    return pl.pallas_call(
        rotate_body,
        out_shape=tuple(jax.ShapeDtypeStruct(s, BF) for s in shapes),
        grid_spec=pltpu.PrefetchScalarGridSpec(
            num_scalar_prefetch=2,
            grid=(1,),
            in_specs=[*specs, *(full((rows, width)) for _ in chunks)],
            out_specs=tuple(full(s) for s in shapes),
        ),
        compiler_params=params(32),
        name="rotate",
    )(where, query_ids, v_t, v_t, v_t, v_t, *chunks)


def back_terms(right, lefts, windows, inverses, rank, q):
    at = slice(q * rank, (q + 1) * rank)
    total = None
    pieces = len(inverses) // 2
    for k, (left, window) in enumerate(zip(lefts, windows)):
        inverse = jnp.concatenate(
            [i[...] for i in inverses[k * pieces : (k + 1) * pieces]], axis=0
        )
        product = dot(left[at, :], right[at, :], 0, 0)
        precond = (product * inverse.astype(F32)).astype(BF)
        term = dot(window[...], precond, 1, 0)
        total = term if total is None else total + term
    return total


def back_first_body(right, *refs):
    out = refs[6]
    queries = out.shape[0]
    rank = right.shape[0] // queries
    for q in range(queries):
        out[q] = back_terms(right, refs[:2], refs[2:4], refs[4:6], rank, q)


def back_first(right, lefts, windows, inverses, queries):
    width = right.shape[1]
    win, depth = windows[0].shape
    return pl.pallas_call(
        back_first_body,
        out_shape=jax.ShapeDtypeStruct((queries, win, width), F32),
        in_specs=[VMEM_SPEC] * 7,
        out_specs=VMEM_SPEC,
        compiler_params=params(24),
        name="back_first",
    )(right, *lefts, *windows, *inverses)


def back_body(where, block_ids, so_far, factors, right, tokens, delta, *refs, train):
    out, refs = refs[-1], refs[:-1]
    queries = so_far.shape[0]
    n_z, rows, width = out.shape
    win = so_far.shape[1]
    per = win // n_z
    rank = right.shape[0] // queries
    valid = factors.shape[1] // 2
    skip = factors.shape[1] - width
    chosen = block_ids[2 * where[2] + where[1]]
    row = factors[pl.ds(chosen, 1), pl.ds(pl.multiple_of(where[3] * skip, LANES), width)]
    lane = lax.broadcasted_iota(jnp.int32, (1, width), 1)
    first = where[3] * (width - valid)
    mine = jnp.logical_and(lane >= first, lane < first + valid)
    scale = jnp.where(mine, 1.0 / row, 0.0)
    which = lax.rem(lax.broadcasted_iota(jnp.int32, (tokens.shape[0], 1), 0), train)
    scores = []
    for q in range(queries):
        total = so_far[q] + back_terms(right, refs[:2], refs[2:4], refs[4:], rank, q)
        total = (total * scale).astype(BF)
        out[:, q * per : (q + 1) * per, :] = total.reshape(n_z, per, width)
        projected = dot(tokens[...], total, 1, 1) * delta[...].astype(F32)
        scores += [
            jnp.sum(jnp.where(which == b, projected, 0.0), axis=0, keepdims=True)
            for b in range(train)
        ]
    words = []
    for k in range(0, queries * train, 8):
        group = jnp.concatenate(scores[k : k + 8], axis=0)
        high = group.astype(BF)
        words += [high, (group - high.astype(F32)).astype(BF)]
    words.append(jnp.zeros((8, width - len(words) * win), BF))
    extra = jnp.concatenate(words, axis=1)
    for k in range(n_z):
        out[k, queries * per :, :] = extra


def back(where, block_ids, so_far, factors, right, tokens, delta, near, n_z, train):
    queries, win, width = so_far.shape
    depth = near[0].shape[1]
    return pl.pallas_call(
        functools.partial(back_body, train=train),
        out_shape=jax.ShapeDtypeStruct((n_z, queries * win // n_z + 8, width), BF),
        in_specs=[SMEM_SPEC, SMEM_SPEC, *([VMEM_SPEC] * (5 + len(near)))],
        out_specs=VMEM_SPEC,
        compiler_params=params(24),
        name="back",
    )(where, block_ids, so_far, factors, right, tokens, delta, *near)


def tile_body(where, parts, basis, t0, t1, t2, t3, score, *, queries, train):
    n_z = parts.shape[0]
    me = 2 * where[1] + where[3]
    own = t0.shape[0]
    rows = 4 * own
    per = own // queries
    total = parts[0].astype(F32)
    for k in range(1, n_z):
        total += parts[k].astype(F32)
    to = lax.broadcasted_iota(jnp.int32, (rows, rows), 0)
    at = lax.broadcasted_iota(jnp.int32, (rows, rows), 1)
    query = at // own
    owner = lax.rem(at // per, 4)
    goal = (owner ^ me) * own + query * per + lax.rem(at, per)
    select = jnp.where(goal == to, 1.0, 0.0).astype(BF)
    half = dot(select, total[:rows].astype(BF), 1, 0).astype(BF)
    tiles = dot(half, basis[...], 1, 1).astype(BF)
    for r, out in enumerate((t0, t1, t2, t3)):
        out[...] = tiles[r * own : (r + 1) * own]
    words = total[rows:]
    lane = lax.broadcasted_iota(jnp.int32, (1, LANES), 1)
    table = jnp.zeros((1, LANES), F32)
    for k in range(queries * train // 8):
        at = 2 * k * LANES
        sums = words[:, at : at + LANES] + words[:, at + LANES : at + 2 * LANES]
        sums = jnp.sum(sums, axis=1, keepdims=True)
        for i in range(8):
            table = jnp.where(lane == 8 * k + i, sums[i : i + 1], table)
    score[...] = jnp.broadcast_to(table[None], score.shape)


def tile_part(where, parts, basis, plane, queries, train):
    own = (parts.shape[1] - 8) // 4
    block = basis.shape[0]
    return pl.pallas_call(
        functools.partial(tile_body, queries=queries, train=train),
        out_shape=(
            *(jax.ShapeDtypeStruct((own, block), BF) for _ in range(4)),
            jax.ShapeDtypeStruct((plane, 1, LANES), F32),
        ),
        in_specs=[SMEM_SPEC, VMEM_SPEC, VMEM_SPEC],
        out_specs=tuple([VMEM_SPEC] * 5),
        compiler_params=params(24),
        name="tile",
    )(where, parts, basis)


def final_body(where, t0, t1, t2, t3, score, tiles, scores):
    queries, per, columns = tiles.shape
    block = columns // 2
    for r, (a, b) in enumerate(((t0, t1), (t2, t3))):
        total = (a[...].astype(F32) + b[...].astype(F32)).astype(BF)
        at = pl.multiple_of((where[1] ^ r) * block, LANES)
        for q in range(queries):
            tiles[q, :, pl.ds(at, block)] = total[q * per : (q + 1) * per]
    sums = jnp.sum(score[...], axis=0)
    train = scores.shape[1]
    for q in range(queries):
        scores[q : q + 1, :] = sums[:, q * train : (q + 1) * train]


def final(where, parts, score, queries, train):
    own, block = parts[0].shape
    return pl.pallas_call(
        final_body,
        out_shape=(
            jax.ShapeDtypeStruct((queries, own // queries, 2 * block), BF),
            jax.ShapeDtypeStruct((queries, train), F32),
        ),
        in_specs=[SMEM_SPEC, *([VMEM_SPEC] * 5)],
        out_specs=(VMEM_SPEC, VMEM_SPEC),
        compiler_params=params(4),
        name="final",
    )(where, *parts, score)


def shards(
    basis_out,
    corrected,
    factor_table,
    block_ids,
    basis_in,
    query_ids,
    u_pool,
    v_pool,
    train_ids,
    x_pool,
    delta_pool,
):
    n_z, n_in = lax.axis_size("z"), lax.axis_size(IN)
    z, xh, c = lax.axis_index("z"), lax.axis_index("xh"), lax.axis_index("c")
    in_pos = lax.axis_index(IN)
    queries, train = query_ids.shape[0], train_ids.shape[0]
    _, local_rows, block = basis_in.shape
    width = -(-(block // 2) // LANES) * LANES
    where = jnp.stack([z, xh, in_pos, c]).astype(jnp.int32)

    packed = pack(where, train_ids, basis_in, x_pool[:, 0], delta_pool[:, 0], width)
    parts = (
        packed[0],
        swap(packed[1], "c"),
        swap(packed[2], "xh"),
        swap(packed[3], QUAD, 3),
    )
    rows = corrected.shape[0]
    ends = (0, 3 * rows // 8, 3 * rows // 4, rows)
    far = [
        inverse_block(where, corrected, block, 1, block, 1, a, b)[0]
        for a, b in zip(ends[:-1], ends[1:])
    ]
    partial = left_part(query_ids, jnp.transpose(u_pool, (0, 2, 1)), basis_out, n_in)
    own = arrange(where, (after(packed[0], far[0], partial), *parts[1:]), local_rows, train)
    near = inverse_block(where, corrected, block, 0, width, 2)
    near = (near[0], swap(near[1], "c"))

    ahead, behind = [shift(own, 1)], [shift(own, -1)]
    far[0] = swap(far[0], "xh")
    spread, window = left_sum(exchange(partial, IN))
    up, down = after((ahead[0], behind[0]), spread)
    far[1] = swap(after(far[1], ahead[0], spread), "xh")
    ahead.append(shift(up, 1))
    behind.append(shift(down, -1))
    left = exchange(spread, IN).reshape(-1, basis_out.shape[1])
    up, down, left = after((ahead[1], behind[1], left), far[0])
    ahead.append(shift(up, 1))
    behind.append(shift(down, -1))
    up = after(ahead[2], behind[2], far[1])
    ahead.append(shift(up, 1))
    far[2] = swap(after(far[2], left), "xh")
    left_x, window_x = swap(left, "xh"), swap(window, "xh")
    lefts = (left, swap(left, "c"))
    windows = (window, swap(window, "c"))
    chunks = (own, *ahead, *behind[::-1])

    basis, right, tokens, delta = rotate(
        where, query_ids, jnp.transpose(v_pool, (0, 2, 1)), chunks, block
    )
    so_far = back_first(right, lefts, windows, near, queries)
    left_x, window_x, *far = after((left_x, window_x, *far), so_far)
    far = halves(where, far, width)
    far = (left_x, swap(left_x, "c"), window_x, swap(window_x, "c"), far[0], swap(far[1], "c"))
    parts = back(
        where, block_ids, so_far, factor_table, right, tokens, delta, far, n_z, train
    )
    *parts, score = tile_part(
        where, exchange(parts, "z"), basis, lax.axis_size(PLANE), queries, train
    )
    parts = (
        parts[0],
        swap(parts[1], "c"),
        swap(parts[2], "xh"),
        swap(parts[3], QUAD, 3),
    )
    return final(where, parts, exchange(score, PLANE), queries, train)


def solution(mesh):
    split = Mesh(mesh.devices.reshape(8, 2, 2, 4, 2), ("z", "xh", "c", "y", "xl"))
    return jax.shard_map(
        shards,
        mesh=split,
        in_specs=(
            P(IN, OUT),
            P(OUT, IN),
            P(),
            P(),
            P(IN, OUT, None),
            P(),
            P(None, IN, None),
            P(None, IN, None),
            P(),
            P(None, OUT, IN),
            P(None, OUT, None),
        ),
        out_specs=(P(None, OUT, IN), P()),
        check_vma=False,
    )
```

```python
import functools

import jax
import jax.numpy as jnp
from jax import lax
from jax.experimental import pallas as pl
from jax.experimental.pallas import tpu as pltpu
from jax.sharding import Mesh
from jax.sharding import PartitionSpec as P

WIN_ROWS = 16
OUT = ("z", "xh", "c")
IN = ("y", "xl")
QUAD = ("xh", "c")
BF = jnp.bfloat16
F32 = jnp.float32
LANES = 128
MIB = 2**20

VMEM_SPEC = pl.BlockSpec(memory_space=pltpu.VMEM)
SMEM_SPEC = pl.BlockSpec(memory_space=pltpu.SMEM)


def params(mib):
    return pltpu.CompilerParams(vmem_limit_bytes=mib * MIB)


def dot(a, b, ca, cb):
    return lax.dot_general(a, b, (((ca,), (cb,)), ((), ())), preferred_element_type=F32)


def exchange(value, axis):
    return lax.all_to_all(value, axis, split_axis=0, concat_axis=0, tiled=True)


def swap(value, axis, mask=1):
    size = lax.axis_size(axis)
    return lax.ppermute(value, axis, [(i, i ^ mask) for i in range(size)])


def shift(value, step):
    size = lax.axis_size("z")
    return lax.ppermute(value, "z", [(i, (i + step) % size) for i in range(size)])


def after(value, *others):
    return lax.optimization_barrier((value, others))[0]


def left_body(ids, u0, u1, u2, u3, basis, out):
    left = jnp.concatenate([u[0] for u in (u0, u1, u2, u3)], axis=0)
    rows = left.shape[0]
    out[:rows, :] = dot(left, basis[...], 1, 0).astype(BF)
    out[rows:, :] = basis[:WIN_ROWS, :]


def left_part(query_ids, u_t, basis_out):
    queries = query_ids.shape[0]
    _, rank, depth = u_t.shape
    eigen = basis_out.shape[1]
    rows = queries * rank + WIN_ROWS
    tile = 256
    specs = [
        pl.BlockSpec((1, rank, depth), functools.partial(lambda q, n, ids: (ids[q], 0, 0), q))
        for q in range(queries)
    ]
    return pl.pallas_call(
        left_body,
        out_shape=jax.ShapeDtypeStruct((rows, eigen), BF),
        grid_spec=pltpu.PrefetchScalarGridSpec(
            num_scalar_prefetch=1,
            grid=(eigen // tile,),
            in_specs=[*specs, pl.BlockSpec((depth, tile), lambda n, ids: (0, n))],
            out_specs=pl.BlockSpec((rows, tile), lambda n, ids: (0, n)),
        ),
        compiler_params=params(10),
        name="left",
    )(query_ids, u_t, u_t, u_t, u_t, basis_out)


def left_pair_body(where, own, other, out):
    n_y, rows, _ = out.shape
    each = rows - 2 * WIN_ROWS
    near = lax.rem(where[2], 2)
    last = n_y * each
    for k in range(n_y):
        at = slice(k * each, (k + 1) * each)
        out[k, :each, :] = (own[at, :].astype(F32) + other[at, :].astype(F32)).astype(BF)
        for part, place in ((own, near), (other, 1 - near)):
            first = pl.multiple_of(each + place * WIN_ROWS, WIN_ROWS)
            out[k, pl.ds(first, WIN_ROWS), :] = part[last:, :]


def left_pair(where, own, other, n_y):
    rows, eigen = own.shape
    return pl.pallas_call(
        left_pair_body,
        out_shape=jax.ShapeDtypeStruct(
            (n_y, (rows - WIN_ROWS) // n_y + 2 * WIN_ROWS, eigen), BF
        ),
        in_specs=[SMEM_SPEC, VMEM_SPEC, VMEM_SPEC],
        out_specs=VMEM_SPEC,
        compiler_params=params(3),
        name="left_pair",
    )(where, own, other)


def left_sum_body(parts, out, window):
    n_y, rows, _ = parts.shape
    wins = 2 * WIN_ROWS
    own = rows - wins
    total = parts[0, :own, :].astype(F32)
    for i in range(1, n_y):
        total += parts[i, :own, :].astype(F32)
    total = total.astype(BF)
    for i in range(n_y):
        out[i] = total
        window[i * wins : (i + 1) * wins, :] = parts[i, own:, :]


def left_sum(parts):
    n_y, rows, eigen = parts.shape
    wins = 2 * WIN_ROWS
    return pl.pallas_call(
        left_sum_body,
        out_shape=(
            jax.ShapeDtypeStruct((n_y, rows - wins, eigen), BF),
            jax.ShapeDtypeStruct((n_y * wins, eigen), BF),
        ),
        in_specs=[VMEM_SPEC],
        out_specs=(VMEM_SPEC, VMEM_SPEC),
        compiler_params=params(3),
        name="left_sum",
    )(parts)


def inverse_body(where, corrected, *outs):
    width = outs[0].shape[1]
    skip = corrected.shape[1] - width
    for r, out in enumerate(outs):
        at = pl.multiple_of((where[3] ^ r) * skip, LANES) if skip else 0
        out[...] = (1.0 / corrected[:, pl.ds(at, width)]).astype(BF)


def inverse_block(where, corrected, block, far, width, count, start=0, stop=None):
    rows = (stop or corrected.shape[0]) - start
    tile = min(rows, 256)
    while start % tile or rows % tile:
        tile -= 64
    first = start // tile
    return pl.pallas_call(
        inverse_body,
        out_shape=tuple(jax.ShapeDtypeStruct((rows, width), BF) for _ in range(count)),
        grid_spec=pltpu.PrefetchScalarGridSpec(
            num_scalar_prefetch=1,
            grid=(rows // tile,),
            in_specs=[pl.BlockSpec((tile, block), lambda n, w: (first + n, w[1] ^ far))],
            out_specs=tuple(
                pl.BlockSpec((tile, width), lambda n, w: (n, 0)) for _ in range(count)
            ),
        ),
        compiler_params=params(58),
        name="inverse",
    )(where, corrected)


def halves_body(where, *refs):
    pieces, (own, other) = refs[:-2], refs[-2:]
    width = own.shape[1]
    first = 0
    for piece in pieces:
        rows, block = piece.shape
        for r, out in enumerate((own, other)):
            at = pl.multiple_of((where[3] ^ r) * (block - width), LANES)
            out[first : first + rows, :] = piece[:, pl.ds(at, width)]
        first += rows


def halves(where, pieces, width):
    rows = sum(p.shape[0] for p in pieces)
    return pl.pallas_call(
        halves_body,
        out_shape=tuple(jax.ShapeDtypeStruct((rows, width), BF) for _ in range(2)),
        in_specs=[SMEM_SPEC, *([VMEM_SPEC] * len(pieces))],
        out_specs=(VMEM_SPEC, VMEM_SPEC),
        compiler_params=params(6),
        name="halves",
    )(where, *pieces)


def pack_body(where, train_ids, basis, tokens, delta, *outs):
    rows = basis.shape[1]
    train, stored = train_ids.shape[0], tokens.shape[0]
    line = lax.broadcasted_iota(jnp.int32, (stored, stored), 0)
    lane = lax.broadcasted_iota(jnp.int32, (stored, stored), 1)
    chosen = jnp.zeros((stored, stored), jnp.bool_)
    for b in range(train):
        chosen = jnp.logical_or(chosen, jnp.logical_and(line == b, lane == train_ids[b]))
    chosen = jnp.where(chosen, 1.0, 0.0).astype(BF)
    gradients = dot(chosen, delta[...], 1, 0).astype(BF)[:train]
    for r, out in enumerate(outs):
        width = out.shape[1]
        block = basis.shape[2]
        skip = block - width
        blk, half = where[1] ^ (r // 2), where[3] ^ (r % 2)
        out[:rows, :] = basis[blk, :, pl.ds(pl.multiple_of(half * skip, LANES), width)]
        own = tokens[:, pl.ds(pl.multiple_of(blk * block, LANES), block)]
        own = dot(chosen, own, 1, 0).astype(BF)[:train]
        out[rows : rows + train, :] = own[:, :width]
        out[rows + train :, :skip] = own[:, width:]
        out[rows + train :, skip:] = gradients


def pack(where, train_ids, basis, tokens, delta, width):
    rows = basis.shape[1] + 2 * train_ids.shape[0]
    return pl.pallas_call(
        pack_body,
        out_shape=tuple(jax.ShapeDtypeStruct((rows, width), BF) for _ in range(4)),
        in_specs=[SMEM_SPEC, SMEM_SPEC, VMEM_SPEC, VMEM_SPEC, VMEM_SPEC],
        out_specs=tuple([VMEM_SPEC] * 4),
        compiler_params=params(4),
        name="pack",
    )(where, train_ids, basis, tokens, delta)


def arrange_body(where, a0, a1, a2, a3, out, *, local, train):
    me = 2 * where[1] + where[3]
    rows = out.shape[0]
    each = local + 2 * train
    to = lax.broadcasted_iota(jnp.int32, (rows, each), 0)
    at = lax.broadcasted_iota(jnp.int32, (rows, each), 1)
    total = None
    for r, part in enumerate((a0, a1, a2, a3)):
        src = me ^ r
        head = src * local + at
        token = 4 * local + src * train + at - local
        other = 4 * local + 4 * train + src * train + at - local - train
        goal = jnp.where(at < local, head, jnp.where(at < local + train, token, other))
        term = dot(jnp.where(goal == to, 1.0, 0.0).astype(BF), part[...], 1, 0)
        total = term if total is None else total + term
    out[...] = total.astype(BF)


def arrange(where, parts, local, train):
    rows, width = parts[0].shape
    return pl.pallas_call(
        functools.partial(arrange_body, local=local, train=train),
        out_shape=jax.ShapeDtypeStruct((4 * rows, width), BF),
        in_specs=[SMEM_SPEC, *([VMEM_SPEC] * 4)],
        out_specs=VMEM_SPEC,
        compiler_params=params(3),
        name="arrange",
    )(where, *parts)


def rotate_body(where, ids, v0, v1, v2, v3, *refs):
    chunks, (basis, right, tokens, delta) = refs[:-4], refs[-4:]
    n_z = len(chunks)
    slab = basis.shape[0] // n_z
    extra = (chunks[0].shape[0] - slab) // 2
    for k, chunk in enumerate(chunks):
        step = k if k <= n_z // 2 else k - n_z
        at = lax.rem(where[0] - step + n_z, n_z) * slab
        basis[pl.ds(pl.multiple_of(at, 16), slab), :] = chunk[:slab, :]
    factors = jnp.concatenate([v[0] for v in (v0, v1, v2, v3)], axis=0)
    whole = basis[...]
    right[...] = dot(factors, whole, 1, 0).astype(BF)
    width = whole.shape[1]
    rest = whole.shape[0] - width
    head = jnp.concatenate([c[slab : slab + extra, :] for c in chunks], axis=0)
    tail = jnp.concatenate([c[slab + extra :, :] for c in chunks], axis=0)
    rotated = dot(head, whole[:width, :], 1, 0) + dot(tail[:, :rest], whole[width:, :], 1, 0)
    tokens[...] = rotated.astype(BF)
    delta[...] = tail[:, rest:]


def rotate(where, query_ids, v_t, chunks, block):
    queries = query_ids.shape[0]
    rank = v_t.shape[1]
    rows, width = chunks[0].shape
    extra = (rows * len(chunks) - block) // 2
    specs = [
        pl.BlockSpec(
            (1, rank, block), functools.partial(lambda q, n, w, ids: (ids[q], 0, w[1]), q)
        )
        for q in range(queries)
    ]

    def full(shape):
        return pl.BlockSpec(shape, lambda n, w, ids: (0, 0))

    shapes = (
        (block, width),
        (queries * rank, width),
        (extra, width),
        (extra, 2 * width - block),
    )
    return pl.pallas_call(
        rotate_body,
        out_shape=tuple(jax.ShapeDtypeStruct(s, BF) for s in shapes),
        grid_spec=pltpu.PrefetchScalarGridSpec(
            num_scalar_prefetch=2,
            grid=(1,),
            in_specs=[*specs, *(full((rows, width)) for _ in chunks)],
            out_specs=tuple(full(s) for s in shapes),
        ),
        compiler_params=params(20),
        name="rotate",
    )(where, query_ids, v_t, v_t, v_t, v_t, *chunks)


def back_terms(right, lefts, windows, inverses, rank, q):
    at = slice(q * rank, (q + 1) * rank)
    total = None
    pieces = len(inverses) // 2
    for k, (left, window) in enumerate(zip(lefts, windows)):
        inverse = jnp.concatenate(
            [i[...] for i in inverses[k * pieces : (k + 1) * pieces]], axis=0
        )
        product = dot(left[at, :], right[at, :], 0, 0)
        precond = (product * inverse.astype(F32)).astype(BF)
        term = dot(window[...], precond, 1, 0)
        total = term if total is None else total + term
    return total


def back_first_body(right, *refs):
    out = refs[6]
    queries = out.shape[0]
    rank = right.shape[0] // queries
    for q in range(queries):
        out[q] = back_terms(right, refs[:2], refs[2:4], refs[4:6], rank, q)


def back_first(right, lefts, windows, inverses, queries):
    width = right.shape[1]
    win, depth = windows[0].shape
    return pl.pallas_call(
        back_first_body,
        out_shape=jax.ShapeDtypeStruct((queries, win, width), F32),
        in_specs=[VMEM_SPEC] * 7,
        out_specs=VMEM_SPEC,
        compiler_params=params(10),
        name="back_first",
    )(right, *lefts, *windows, *inverses)


def back_body(where, block_ids, so_far, factors, right, tokens, delta, *refs, train):
    refs, (out, score) = refs[:-2], refs[-2:]
    queries = so_far.shape[0]
    n_z, rows, width = out.shape
    per = rows // queries
    rank = right.shape[0] // queries
    valid = factors.shape[1] // 2
    skip = factors.shape[1] - width
    chosen = block_ids[2 * where[2] + where[1]]
    row = factors[pl.ds(chosen, 1), pl.ds(pl.multiple_of(where[3] * skip, LANES), width)]
    lane = lax.broadcasted_iota(jnp.int32, (1, width), 1)
    first = where[3] * (width - valid)
    mine = jnp.logical_and(lane >= first, lane < first + valid)
    scale = jnp.where(mine, 1.0 / row, 0.0)
    which = lax.rem(lax.broadcasted_iota(jnp.int32, (tokens.shape[0], 1), 0), train)
    place = lax.broadcasted_iota(jnp.int32, (1, LANES), 1)
    table = jnp.zeros((1, LANES), F32)
    for q in range(queries):
        total = so_far[q] + back_terms(right, refs[:2], refs[2:4], refs[4:], rank, q)
        total = (total * scale).astype(BF)
        out[:, q * per : (q + 1) * per, :] = total.reshape(n_z, per, width)
        projected = dot(tokens[...], total, 1, 1) * delta[...].astype(F32)
        for b in range(train):
            part = jnp.sum(jnp.where(which == b, projected, 0.0), axis=0, keepdims=True)
            part = jnp.sum(part, axis=1, keepdims=True)
            table = jnp.where(place == q * train + b, part, table)
    score[...] = table


def back(where, block_ids, so_far, factors, right, tokens, delta, far, n_z, train):
    queries, win, width = so_far.shape
    return pl.pallas_call(
        functools.partial(back_body, train=train),
        out_shape=(
            jax.ShapeDtypeStruct((n_z, queries * win // n_z, width), BF),
            jax.ShapeDtypeStruct((1, LANES), F32),
        ),
        in_specs=[SMEM_SPEC, SMEM_SPEC, *([VMEM_SPEC] * (5 + len(far)))],
        out_specs=(VMEM_SPEC, VMEM_SPEC),
        compiler_params=params(12),
        name="back",
    )(where, block_ids, so_far, factors, right, tokens, delta, *far)


def tile_body(where, parts, basis, *outs, queries):
    n_z, rows, _ = parts.shape
    me = 2 * where[1] + where[3]
    own = rows // 4
    per = own // queries
    total = parts[0].astype(F32)
    for k in range(1, n_z):
        total += parts[k].astype(F32)
    to = lax.broadcasted_iota(jnp.int32, (rows, rows), 0)
    at = lax.broadcasted_iota(jnp.int32, (rows, rows), 1)
    query = at // own
    owner = lax.rem(at // per, 4)
    goal = (owner ^ me) * own + query * per + lax.rem(at, per)
    select = jnp.where(goal == to, 1.0, 0.0).astype(BF)
    half = dot(select, total.astype(BF), 1, 0).astype(BF)
    tiles = dot(half, basis[...], 1, 1).astype(BF)
    for r, out in enumerate(outs):
        out[...] = tiles[r * own : (r + 1) * own]


def tile_part(where, parts, basis, queries):
    own = parts.shape[1] // 4
    return pl.pallas_call(
        functools.partial(tile_body, queries=queries),
        out_shape=tuple(jax.ShapeDtypeStruct((own, basis.shape[0]), BF) for _ in range(4)),
        in_specs=[SMEM_SPEC, VMEM_SPEC, VMEM_SPEC],
        out_specs=tuple([VMEM_SPEC] * 4),
        compiler_params=params(8),
        name="tile",
    )(where, parts, basis)


def final_body(where, t0, t1, t2, t3, score, tiles, scores):
    queries, per, columns = tiles.shape
    block = columns // 2
    for r, (a, b) in enumerate(((t0, t1), (t2, t3))):
        total = (a[...].astype(F32) + b[...].astype(F32)).astype(BF)
        at = pl.multiple_of((where[1] ^ r) * block, LANES)
        for q in range(queries):
            tiles[q, :, pl.ds(at, block)] = total[q * per : (q + 1) * per]
    sums = jnp.sum(score[...], axis=0)
    train = scores.shape[1]
    for q in range(queries):
        scores[q : q + 1, :] = sums[:, q * train : (q + 1) * train]


def final(where, parts, score, queries, train):
    own, block = parts[0].shape
    return pl.pallas_call(
        final_body,
        out_shape=(
            jax.ShapeDtypeStruct((queries, own // queries, 2 * block), BF),
            jax.ShapeDtypeStruct((queries, train), F32),
        ),
        in_specs=[SMEM_SPEC, *([VMEM_SPEC] * 5)],
        out_specs=(VMEM_SPEC, VMEM_SPEC),
        compiler_params=params(3),
        name="final",
    )(where, *parts, score)


def shards(
    basis_out,
    corrected,
    factor_table,
    block_ids,
    basis_in,
    query_ids,
    u_pool,
    v_pool,
    train_ids,
    x_pool,
    delta_pool,
):
    n_z = lax.axis_size("z")
    z, xh, c = lax.axis_index("z"), lax.axis_index("xh"), lax.axis_index("c")
    in_pos = lax.axis_index(IN)
    queries, train = query_ids.shape[0], train_ids.shape[0]
    _, local_rows, block = basis_in.shape
    width = -(-(block // 2) // LANES) * LANES
    where = jnp.stack([z, xh, in_pos, c]).astype(jnp.int32)

    packed = pack(where, train_ids, basis_in, x_pool[:, 0], delta_pool[:, 0], width)
    parts = (
        packed[0],
        swap(packed[1], "c"),
        swap(packed[2], "xh"),
        swap(packed[3], QUAD, 3),
    )
    partial = left_part(
        after(query_ids, packed[0]), jnp.transpose(u_pool, (0, 2, 1)), basis_out
    )
    other = swap(partial, "xl")
    rows = corrected.shape[0]
    ends = (0, 3 * rows // 8, 3 * rows // 4, rows)
    far = [
        inverse_block(after(where, partial), corrected, block, 1, block, 1, a, b)[0]
        for a, b in zip(ends[:-1], ends[1:])
    ]
    own = arrange(where, (after(packed[0], far[0]), *parts[1:]), local_rows, train)
    near = inverse_block(where, corrected, block, 0, width, 2)
    near = (near[0], swap(near[1], "c"))

    partial = left_pair(where, partial, other, lax.axis_size("y"))
    ahead, behind = [shift(own, 1)], [shift(own, -1)]
    far[0] = swap(after(far[0], other), "xh")
    up, down = after((ahead[0], behind[0]), far[0])
    spread, window = left_sum(exchange(partial, "y"))
    far[1] = swap(after(far[1], ahead[0]), "xh")
    ahead.append(shift(up, 1))
    behind.append(shift(down, -1))
    left = exchange(spread, "y").reshape(-1, basis_out.shape[1])
    up, down, left = after((ahead[1], behind[1], left), far[1])
    ahead.append(shift(up, 1))
    behind.append(shift(down, -1))
    far[2] = swap(after(far[2], left), "xh")
    left_x, window_x = swap(left, "xh"), swap(window, "xh")
    lefts = (left, swap(left, "c"))
    windows = (window, swap(window, "c"))
    up, left_x, window_x = after((ahead[2], left_x, window_x), behind[2])
    ahead.append(shift(up, 1))
    far = halves(where, far, width)
    last, *far = after((ahead[3], *far))
    chunks = (own, *ahead[:3], last, *behind[::-1])

    basis, right, tokens, delta = rotate(
        where, query_ids, jnp.transpose(v_pool, (0, 2, 1)), chunks, block
    )
    left_x, window_x, right_x = after((left_x, window_x, right))
    left_d, window_d = swap(left_x, "c"), swap(window_x, "c")
    so_far = back_first(right_x, lefts, windows, near, queries)
    far = (left_x, left_d, window_x, window_d, far[0], swap(far[1], "c"))
    parts, score = back(
        where, block_ids, so_far, factor_table, right, tokens, delta, far, n_z, train
    )
    for axis, mask in (("c", 1), ("xl", 1), ("y", 1), ("y", 2), ("xh", 1)):
        score = score + swap(score, axis, mask)
    parts, score = after((exchange(parts, "z"), score))
    parts = tile_part(where, parts, basis, queries)
    score = exchange(jnp.broadcast_to(score, (n_z, *score.shape)), "z")
    parts = (
        parts[0],
        swap(parts[1], "c"),
        swap(parts[2], "xh"),
        swap(parts[3], QUAD, 3),
    )
    return final(where, parts, score, queries, train)


def solution(mesh):
    split = Mesh(mesh.devices.reshape(8, 2, 2, 4, 2), ("z", "xh", "c", "y", "xl"))
    return jax.shard_map(
        shards,
        mesh=split,
        in_specs=(
            P(IN, OUT),
            P(OUT, IN),
            P(),
            P(),
            P(IN, OUT, None),
            P(),
            P(None, IN, None),
            P(None, IN, None),
            P(),
            P(None, OUT, IN),
            P(None, OUT, None),
        ),
        out_specs=(P(None, OUT, IN), P()),
        check_vma=False,
    )
```

```python
import functools

import jax
import jax.numpy as jnp
from jax import lax
from jax.experimental import pallas as pl
from jax.experimental.pallas import tpu as pltpu
from jax.sharding import Mesh
from jax.sharding import PartitionSpec as P

WIN_ROWS = 16
OUT = ("z", "xh", "c")
IN = ("y", "xl")
QUAD = ("xh", "c")
PLANE = ("xh", "c", "y", "xl")
BF = jnp.bfloat16
F32 = jnp.float32
LANES = 128
MIB = 2**20

VMEM_SPEC = pl.BlockSpec(memory_space=pltpu.VMEM)
SMEM_SPEC = pl.BlockSpec(memory_space=pltpu.SMEM)


def params(mib):
    return pltpu.CompilerParams(vmem_limit_bytes=mib * MIB)


def dot(a, b, ca, cb):
    return lax.dot_general(a, b, (((ca,), (cb,)), ((), ())), preferred_element_type=F32)


def exchange(value, axis):
    return lax.all_to_all(value, axis, split_axis=0, concat_axis=0, tiled=True)


def swap(value, axis, mask=1):
    size = lax.axis_size(axis)
    return lax.ppermute(value, axis, [(i, i ^ mask) for i in range(size)])


def shift(value, step):
    size = lax.axis_size("z")
    return lax.ppermute(value, "z", [(i, (i + step) % size) for i in range(size)])


def after(value, *others):
    return lax.optimization_barrier((value, others))[0]


def left_body(ids, u0, u1, u2, u3, basis, out):
    left = jnp.concatenate([u[0] for u in (u0, u1, u2, u3)], axis=0)
    n_in, rows, width = out.shape
    part = dot(left, basis[...], 1, 0).astype(BF)
    out[:, : rows - WIN_ROWS, :] = part.reshape(n_in, rows - WIN_ROWS, width)
    out[:, rows - WIN_ROWS :, :] = jnp.broadcast_to(
        basis[:WIN_ROWS, :][None], (n_in, WIN_ROWS, width)
    )


def left_part(query_ids, u_t, basis_out, n_in):
    queries = query_ids.shape[0]
    _, rank, depth = u_t.shape
    eigen = basis_out.shape[1]
    rows = queries * rank // n_in + WIN_ROWS
    tile = 256
    specs = [
        pl.BlockSpec((1, rank, depth), functools.partial(lambda q, n, ids: (ids[q], 0, 0), q))
        for q in range(queries)
    ]
    return pl.pallas_call(
        left_body,
        out_shape=jax.ShapeDtypeStruct((n_in, rows, eigen), BF),
        grid_spec=pltpu.PrefetchScalarGridSpec(
            num_scalar_prefetch=1,
            grid=(eigen // tile,),
            in_specs=[*specs, pl.BlockSpec((depth, tile), lambda n, ids: (0, n))],
            out_specs=pl.BlockSpec((n_in, rows, tile), lambda n, ids: (0, 0, n)),
        ),
        compiler_params=params(16),
        name="left",
    )(query_ids, u_t, u_t, u_t, u_t, basis_out)


def left_sum_body(parts, out, window):
    n_in, rows, _ = parts.shape
    own = rows - WIN_ROWS
    total = parts[0, :own, :].astype(F32)
    for i in range(1, n_in):
        total += parts[i, :own, :].astype(F32)
    total = total.astype(BF)
    for i in range(n_in):
        out[i] = total
        window[i * WIN_ROWS : (i + 1) * WIN_ROWS, :] = parts[i, own:, :]


def left_sum(parts):
    n_in, rows, eigen = parts.shape
    return pl.pallas_call(
        left_sum_body,
        out_shape=(
            jax.ShapeDtypeStruct((n_in, rows - WIN_ROWS, eigen), BF),
            jax.ShapeDtypeStruct((n_in * WIN_ROWS, eigen), BF),
        ),
        in_specs=[VMEM_SPEC],
        out_specs=(VMEM_SPEC, VMEM_SPEC),
        compiler_params=params(4),
        name="left_sum",
    )(parts)


def inverse_body(where, corrected, *outs):
    width = outs[0].shape[1]
    skip = corrected.shape[1] - width
    for r, out in enumerate(outs):
        at = pl.multiple_of((where[3] ^ r) * skip, LANES) if skip else 0
        out[...] = (1.0 / corrected[:, pl.ds(at, width)]).astype(BF)


def inverse_block(where, corrected, block, far, width, count, start=0, stop=None):
    rows = (stop or corrected.shape[0]) - start
    tile = min(rows, 256)
    while start % tile or rows % tile:
        tile -= 64
    first = start // tile
    return pl.pallas_call(
        inverse_body,
        out_shape=tuple(jax.ShapeDtypeStruct((rows, width), BF) for _ in range(count)),
        grid_spec=pltpu.PrefetchScalarGridSpec(
            num_scalar_prefetch=1,
            grid=(rows // tile,),
            in_specs=[pl.BlockSpec((tile, block), lambda n, w: (first + n, w[1] ^ far))],
            out_specs=tuple(
                pl.BlockSpec((tile, width), lambda n, w: (n, 0)) for _ in range(count)
            ),
        ),
        compiler_params=params(58),
        name="inverse",
    )(where, corrected)


def halves_body(where, *refs):
    pieces, (own, other) = refs[:-2], refs[-2:]
    width = own.shape[1]
    first = 0
    for piece in pieces:
        rows, block = piece.shape
        for r, out in enumerate((own, other)):
            at = pl.multiple_of((where[3] ^ r) * (block - width), LANES)
            out[first : first + rows, :] = piece[:, pl.ds(at, width)]
        first += rows


def halves(where, pieces, width):
    rows = sum(p.shape[0] for p in pieces)
    return pl.pallas_call(
        halves_body,
        out_shape=tuple(jax.ShapeDtypeStruct((rows, width), BF) for _ in range(2)),
        in_specs=[SMEM_SPEC, *([VMEM_SPEC] * len(pieces))],
        out_specs=(VMEM_SPEC, VMEM_SPEC),
        compiler_params=params(6),
        name="halves",
    )(where, *pieces)


def pack_body(where, train_ids, basis, tokens, delta, *outs):
    rows = basis.shape[1]
    train, stored = train_ids.shape[0], tokens.shape[0]
    line = lax.broadcasted_iota(jnp.int32, (stored, stored), 0)
    lane = lax.broadcasted_iota(jnp.int32, (stored, stored), 1)
    chosen = jnp.zeros((stored, stored), jnp.bool_)
    for b in range(train):
        chosen = jnp.logical_or(chosen, jnp.logical_and(line == b, lane == train_ids[b]))
    chosen = jnp.where(chosen, 1.0, 0.0).astype(BF)
    gradients = dot(chosen, delta[...], 1, 0).astype(BF)[:train]
    for r, out in enumerate(outs):
        width = out.shape[1]
        block = basis.shape[2]
        skip = block - width
        blk, half = where[1] ^ (r // 2), where[3] ^ (r % 2)
        out[:rows, :] = basis[blk, :, pl.ds(pl.multiple_of(half * skip, LANES), width)]
        own = tokens[:, pl.ds(pl.multiple_of(blk * block, LANES), block)]
        own = dot(chosen, own, 1, 0).astype(BF)[:train]
        out[rows : rows + train, :] = own[:, :width]
        out[rows + train :, :skip] = own[:, width:]
        out[rows + train :, skip:] = gradients


def pack(where, train_ids, basis, tokens, delta, width):
    rows = basis.shape[1] + 2 * train_ids.shape[0]
    return pl.pallas_call(
        pack_body,
        out_shape=tuple(jax.ShapeDtypeStruct((rows, width), BF) for _ in range(4)),
        in_specs=[SMEM_SPEC, SMEM_SPEC, VMEM_SPEC, VMEM_SPEC, VMEM_SPEC],
        out_specs=tuple([VMEM_SPEC] * 4),
        compiler_params=params(4),
        name="pack",
    )(where, train_ids, basis, tokens, delta)


def arrange_body(where, a0, a1, a2, a3, out, *, local, train):
    me = 2 * where[1] + where[3]
    rows = out.shape[0]
    each = local + 2 * train
    to = lax.broadcasted_iota(jnp.int32, (rows, each), 0)
    at = lax.broadcasted_iota(jnp.int32, (rows, each), 1)
    total = None
    for r, part in enumerate((a0, a1, a2, a3)):
        src = me ^ r
        head = src * local + at
        token = 4 * local + src * train + at - local
        other = 4 * local + 4 * train + src * train + at - local - train
        goal = jnp.where(at < local, head, jnp.where(at < local + train, token, other))
        term = dot(jnp.where(goal == to, 1.0, 0.0).astype(BF), part[...], 1, 0)
        total = term if total is None else total + term
    out[...] = total.astype(BF)


def arrange(where, parts, local, train):
    rows, width = parts[0].shape
    return pl.pallas_call(
        functools.partial(arrange_body, local=local, train=train),
        out_shape=jax.ShapeDtypeStruct((4 * rows, width), BF),
        in_specs=[SMEM_SPEC, *([VMEM_SPEC] * 4)],
        out_specs=VMEM_SPEC,
        compiler_params=params(3),
        name="arrange",
    )(where, *parts)


def rotate_body(where, ids, v0, v1, v2, v3, *refs):
    chunks, (basis, right, tokens, delta) = refs[:-4], refs[-4:]
    n_z = len(chunks)
    slab = basis.shape[0] // n_z
    extra = (chunks[0].shape[0] - slab) // 2
    for k, chunk in enumerate(chunks):
        step = k if k <= n_z // 2 else k - n_z
        at = lax.rem(where[0] - step + n_z, n_z) * slab
        basis[pl.ds(pl.multiple_of(at, 16), slab), :] = chunk[:slab, :]
    factors = jnp.concatenate([v[0] for v in (v0, v1, v2, v3)], axis=0)
    whole = basis[...]
    right[...] = dot(factors, whole, 1, 0).astype(BF)
    width = whole.shape[1]
    rest = whole.shape[0] - width
    head = jnp.concatenate([c[slab : slab + extra, :] for c in chunks], axis=0)
    tail = jnp.concatenate([c[slab + extra :, :] for c in chunks], axis=0)
    rotated = dot(head, whole[:width, :], 1, 0) + dot(tail[:, :rest], whole[width:, :], 1, 0)
    tokens[...] = rotated.astype(BF)
    delta[...] = tail[:, rest:]


def rotate(where, query_ids, v_t, chunks, block):
    queries = query_ids.shape[0]
    rank = v_t.shape[1]
    rows, width = chunks[0].shape
    extra = (rows * len(chunks) - block) // 2
    specs = [
        pl.BlockSpec(
            (1, rank, block), functools.partial(lambda q, n, w, ids: (ids[q], 0, w[1]), q)
        )
        for q in range(queries)
    ]

    def full(shape):
        return pl.BlockSpec(shape, lambda n, w, ids: (0, 0))

    shapes = (
        (block, width),
        (queries * rank, width),
        (extra, width),
        (extra, 2 * width - block),
    )
    return pl.pallas_call(
        rotate_body,
        out_shape=tuple(jax.ShapeDtypeStruct(s, BF) for s in shapes),
        grid_spec=pltpu.PrefetchScalarGridSpec(
            num_scalar_prefetch=2,
            grid=(1,),
            in_specs=[*specs, *(full((rows, width)) for _ in chunks)],
            out_specs=tuple(full(s) for s in shapes),
        ),
        compiler_params=params(20),
        name="rotate",
    )(where, query_ids, v_t, v_t, v_t, v_t, *chunks)


def back_terms(right, lefts, windows, inverses, rank, q):
    at = slice(q * rank, (q + 1) * rank)
    total = None
    pieces = len(inverses) // 2
    for k, (left, window) in enumerate(zip(lefts, windows)):
        inverse = jnp.concatenate(
            [i[...] for i in inverses[k * pieces : (k + 1) * pieces]], axis=0
        )
        product = dot(left[at, :], right[at, :], 0, 0)
        precond = (product * inverse.astype(F32)).astype(BF)
        term = dot(window[...], precond, 1, 0)
        total = term if total is None else total + term
    return total


def back_first_body(right, *refs):
    out = refs[6]
    queries = out.shape[0]
    rank = right.shape[0] // queries
    for q in range(queries):
        out[q] = back_terms(right, refs[:2], refs[2:4], refs[4:6], rank, q)


def back_first(right, lefts, windows, inverses, queries):
    width = right.shape[1]
    win, depth = windows[0].shape
    return pl.pallas_call(
        back_first_body,
        out_shape=jax.ShapeDtypeStruct((queries, win, width), F32),
        in_specs=[VMEM_SPEC] * 7,
        out_specs=VMEM_SPEC,
        compiler_params=params(10),
        name="back_first",
    )(right, *lefts, *windows, *inverses)


def back_body(where, block_ids, so_far, factors, right, tokens, delta, *refs, train):
    refs, (out, score) = refs[:-2], refs[-2:]
    queries = so_far.shape[0]
    n_z, rows, width = out.shape
    per = rows // queries
    rank = right.shape[0] // queries
    valid = factors.shape[1] // 2
    skip = factors.shape[1] - width
    chosen = block_ids[2 * where[2] + where[1]]
    row = factors[pl.ds(chosen, 1), pl.ds(pl.multiple_of(where[3] * skip, LANES), width)]
    lane = lax.broadcasted_iota(jnp.int32, (1, width), 1)
    first = where[3] * (width - valid)
    mine = jnp.logical_and(lane >= first, lane < first + valid)
    scale = jnp.where(mine, 1.0 / row, 0.0)
    which = lax.rem(lax.broadcasted_iota(jnp.int32, (tokens.shape[0], 1), 0), train)
    place = lax.broadcasted_iota(jnp.int32, (1, LANES), 1)
    table = jnp.zeros((1, LANES), F32)
    for q in range(queries):
        total = so_far[q] + back_terms(right, refs[:2], refs[2:4], refs[4:], rank, q)
        total = (total * scale).astype(BF)
        out[:, q * per : (q + 1) * per, :] = total.reshape(n_z, per, width)
        projected = dot(tokens[...], total, 1, 1) * delta[...].astype(F32)
        for b in range(train):
            part = jnp.sum(jnp.where(which == b, projected, 0.0), axis=0, keepdims=True)
            part = jnp.sum(part, axis=1, keepdims=True)
            table = jnp.where(place == q * train + b, part, table)
    score[...] = table


def back(where, block_ids, so_far, factors, right, tokens, delta, far, n_z, train):
    queries, win, width = so_far.shape
    return pl.pallas_call(
        functools.partial(back_body, train=train),
        out_shape=(
            jax.ShapeDtypeStruct((n_z, queries * win // n_z, width), BF),
            jax.ShapeDtypeStruct((1, LANES), F32),
        ),
        in_specs=[SMEM_SPEC, SMEM_SPEC, *([VMEM_SPEC] * (5 + len(far)))],
        out_specs=(VMEM_SPEC, VMEM_SPEC),
        compiler_params=params(12),
        name="back",
    )(where, block_ids, so_far, factors, right, tokens, delta, *far)


def tile_body(where, parts, basis, *outs, queries):
    n_z, rows, _ = parts.shape
    me = 2 * where[1] + where[3]
    own = rows // 4
    per = own // queries
    total = parts[0].astype(F32)
    for k in range(1, n_z):
        total += parts[k].astype(F32)
    to = lax.broadcasted_iota(jnp.int32, (rows, rows), 0)
    at = lax.broadcasted_iota(jnp.int32, (rows, rows), 1)
    query = at // own
    owner = lax.rem(at // per, 4)
    goal = (owner ^ me) * own + query * per + lax.rem(at, per)
    select = jnp.where(goal == to, 1.0, 0.0).astype(BF)
    half = dot(select, total.astype(BF), 1, 0).astype(BF)
    tiles = dot(half, basis[...], 1, 1).astype(BF)
    for r, out in enumerate(outs):
        out[...] = tiles[r * own : (r + 1) * own]


def tile_part(where, parts, basis, queries):
    own = parts.shape[1] // 4
    return pl.pallas_call(
        functools.partial(tile_body, queries=queries),
        out_shape=tuple(jax.ShapeDtypeStruct((own, basis.shape[0]), BF) for _ in range(4)),
        in_specs=[SMEM_SPEC, VMEM_SPEC, VMEM_SPEC],
        out_specs=tuple([VMEM_SPEC] * 4),
        compiler_params=params(8),
        name="tile",
    )(where, parts, basis)


def final_body(where, t0, t1, t2, t3, score, tiles, scores):
    queries, per, columns = tiles.shape
    block = columns // 2
    for r, (a, b) in enumerate(((t0, t1), (t2, t3))):
        total = (a[...].astype(F32) + b[...].astype(F32)).astype(BF)
        at = pl.multiple_of((where[1] ^ r) * block, LANES)
        for q in range(queries):
            tiles[q, :, pl.ds(at, block)] = total[q * per : (q + 1) * per]
    sums = jnp.sum(score[...], axis=0)
    train = scores.shape[1]
    for q in range(queries):
        scores[q : q + 1, :] = sums[:, q * train : (q + 1) * train]


def final(where, parts, score, queries, train):
    own, block = parts[0].shape
    return pl.pallas_call(
        final_body,
        out_shape=(
            jax.ShapeDtypeStruct((queries, own // queries, 2 * block), BF),
            jax.ShapeDtypeStruct((queries, train), F32),
        ),
        in_specs=[SMEM_SPEC, *([VMEM_SPEC] * 5)],
        out_specs=(VMEM_SPEC, VMEM_SPEC),
        compiler_params=params(3),
        name="final",
    )(where, *parts, score)


def shards(
    basis_out,
    corrected,
    factor_table,
    block_ids,
    basis_in,
    query_ids,
    u_pool,
    v_pool,
    train_ids,
    x_pool,
    delta_pool,
):
    n_z, n_in = lax.axis_size("z"), lax.axis_size(IN)
    z, xh, c = lax.axis_index("z"), lax.axis_index("xh"), lax.axis_index("c")
    in_pos = lax.axis_index(IN)
    queries, train = query_ids.shape[0], train_ids.shape[0]
    _, local_rows, block = basis_in.shape
    width = -(-(block // 2) // LANES) * LANES
    where = jnp.stack([z, xh, in_pos, c]).astype(jnp.int32)

    packed = pack(where, train_ids, basis_in, x_pool[:, 0], delta_pool[:, 0], width)
    parts = (
        packed[0],
        swap(packed[1], "c"),
        swap(packed[2], "xh"),
        swap(packed[3], QUAD, 3),
    )
    rows = corrected.shape[0]
    ends = (0, 3 * rows // 8, 3 * rows // 4, rows)
    far = [
        inverse_block(where, corrected, block, 1, block, 1, a, b)[0]
        for a, b in zip(ends[:-1], ends[1:])
    ]
    partial = left_part(query_ids, jnp.transpose(u_pool, (0, 2, 1)), basis_out, n_in)
    own = arrange(where, (after(packed[0], far[0], partial), *parts[1:]), local_rows, train)

    ahead, behind = [shift(own, 1)], [shift(own, -1)]
    far[0] = swap(after(far[0], *parts[1:], partial), "xh")
    spread, window = left_sum(after(exchange(partial, IN), far[1]))
    near = inverse_block(after(where, spread), corrected, block, 0, width, 2)
    far[1] = swap(after(far[1], ahead[0], near[0]), "xh")
    near = (near[0], swap(near[1], "c"))
    up, down = after((ahead[0], behind[0]), spread, far[0])
    ahead.append(shift(up, 1))
    behind.append(shift(down, -1))
    left = exchange(spread, IN).reshape(-1, basis_out.shape[1])
    up, down, left = after((ahead[1], behind[1], left), far[2])
    ahead.append(shift(up, 1))
    behind.append(shift(down, -1))
    far[2] = swap(after(far[2], ahead[1]), "xh")
    left_x, window_x = swap(left, "xh"), swap(window, "xh")
    lefts = (left, swap(left, "c"))
    windows = (window, swap(window, "c"))
    up = after(ahead[2], behind[2], far[1])
    ahead.append(shift(up, 1))
    far = halves(where, far, width)
    last, *far = after((ahead[3], *far))
    chunks = (own, *ahead[:3], last, *behind[::-1])

    basis, right, tokens, delta = rotate(
        where, query_ids, jnp.transpose(v_pool, (0, 2, 1)), chunks, block
    )
    so_far = back_first(right, lefts, windows, near, queries)
    left_x, window_x = after((left_x, window_x), so_far)
    far = (left_x, swap(left_x, "c"), window_x, swap(window_x, "c"), far[0], swap(far[1], "c"))
    parts, score = back(
        where, block_ids, so_far, factor_table, right, tokens, delta, far, n_z, train
    )
    for axis, mask in (("c", 1), ("xl", 1), ("y", 1), ("y", 2), ("xh", 1)):
        score = score + swap(score, axis, mask)
    parts, score = after((exchange(parts, "z"), score))
    parts = tile_part(where, parts, basis, queries)
    score = exchange(jnp.broadcast_to(score, (n_z, *score.shape)), "z")
    parts = (
        parts[0],
        swap(parts[1], "c"),
        swap(parts[2], "xh"),
        swap(parts[3], QUAD, 3),
    )
    return final(where, parts, score, queries, train)


def solution(mesh):
    split = Mesh(mesh.devices.reshape(8, 2, 2, 4, 2), ("z", "xh", "c", "y", "xl"))
    return jax.shard_map(
        shards,
        mesh=split,
        in_specs=(
            P(IN, OUT),
            P(OUT, IN),
            P(),
            P(),
            P(IN, OUT, None),
            P(),
            P(None, IN, None),
            P(None, IN, None),
            P(),
            P(None, OUT, IN),
            P(None, OUT, None),
        ),
        out_specs=(P(None, OUT, IN), P()),
        check_vma=False,
    )
```

```python
import functools

import jax
import jax.numpy as jnp
from jax import lax
from jax.experimental import pallas as pl
from jax.experimental.pallas import tpu as pltpu
from jax.sharding import Mesh
from jax.sharding import PartitionSpec as P

WIN_ROWS = 16
OUT = ("z", "xh", "c")
IN = ("y", "xl")
QUAD = ("xh", "c")
PLANE = ("xh", "c", "y", "xl")
BF = jnp.bfloat16
F32 = jnp.float32
LANES = 128
MIB = 2**20

VMEM_SPEC = pl.BlockSpec(memory_space=pltpu.VMEM)
SMEM_SPEC = pl.BlockSpec(memory_space=pltpu.SMEM)


def params(mib):
    return pltpu.CompilerParams(vmem_limit_bytes=mib * MIB)


def dot(a, b, ca, cb):
    return lax.dot_general(a, b, (((ca,), (cb,)), ((), ())), preferred_element_type=F32)


def exchange(value, axis):
    return lax.all_to_all(value, axis, split_axis=0, concat_axis=0, tiled=True)


def swap(value, axis, mask=1):
    size = lax.axis_size(axis)
    return lax.ppermute(value, axis, [(i, i ^ mask) for i in range(size)])


def shift(value, step):
    size = lax.axis_size("z")
    return lax.ppermute(value, "z", [(i, (i + step) % size) for i in range(size)])


def after(value, *others):
    return lax.optimization_barrier((value, others))[0]


def left_body(ids, u0, u1, u2, u3, basis, out):
    left = jnp.concatenate([u[0] for u in (u0, u1, u2, u3)], axis=0)
    n_in, rows, width = out.shape
    part = dot(left, basis[...], 1, 0).astype(BF)
    out[:, : rows - WIN_ROWS, :] = part.reshape(n_in, rows - WIN_ROWS, width)
    out[:, rows - WIN_ROWS :, :] = jnp.broadcast_to(
        basis[:WIN_ROWS, :][None], (n_in, WIN_ROWS, width)
    )


def left_part(query_ids, u_t, basis_out, n_in):
    queries = query_ids.shape[0]
    _, rank, depth = u_t.shape
    eigen = basis_out.shape[1]
    rows = queries * rank // n_in + WIN_ROWS
    tile = 256
    specs = [
        pl.BlockSpec((1, rank, depth), functools.partial(lambda q, n, ids: (ids[q], 0, 0), q))
        for q in range(queries)
    ]
    return pl.pallas_call(
        left_body,
        out_shape=jax.ShapeDtypeStruct((n_in, rows, eigen), BF),
        grid_spec=pltpu.PrefetchScalarGridSpec(
            num_scalar_prefetch=1,
            grid=(eigen // tile,),
            in_specs=[*specs, pl.BlockSpec((depth, tile), lambda n, ids: (0, n))],
            out_specs=pl.BlockSpec((n_in, rows, tile), lambda n, ids: (0, 0, n)),
        ),
        compiler_params=params(16),
        name="left",
    )(query_ids, u_t, u_t, u_t, u_t, basis_out)


def left_sum_body(parts, out, window):
    n_in, rows, _ = parts.shape
    own = rows - WIN_ROWS
    total = parts[0, :own, :].astype(F32)
    for i in range(1, n_in):
        total += parts[i, :own, :].astype(F32)
    total = total.astype(BF)
    for i in range(n_in):
        out[i] = total
        window[i * WIN_ROWS : (i + 1) * WIN_ROWS, :] = parts[i, own:, :]


def left_sum(parts):
    n_in, rows, eigen = parts.shape
    return pl.pallas_call(
        left_sum_body,
        out_shape=(
            jax.ShapeDtypeStruct((n_in, rows - WIN_ROWS, eigen), BF),
            jax.ShapeDtypeStruct((n_in * WIN_ROWS, eigen), BF),
        ),
        in_specs=[VMEM_SPEC],
        out_specs=(VMEM_SPEC, VMEM_SPEC),
        compiler_params=params(4),
        name="left_sum",
    )(parts)


def inverse_body(where, corrected, *outs):
    width = outs[0].shape[1]
    skip = corrected.shape[1] - width
    for r, out in enumerate(outs):
        at = pl.multiple_of((where[3] ^ r) * skip, LANES) if skip else 0
        out[...] = (1.0 / corrected[:, pl.ds(at, width)]).astype(BF)


def inverse_block(where, corrected, block, far, width, count, start=0, stop=None):
    rows = (stop or corrected.shape[0]) - start
    tile = min(rows, 256)
    while start % tile or rows % tile:
        tile -= 64
    first = start // tile
    return pl.pallas_call(
        inverse_body,
        out_shape=tuple(jax.ShapeDtypeStruct((rows, width), BF) for _ in range(count)),
        grid_spec=pltpu.PrefetchScalarGridSpec(
            num_scalar_prefetch=1,
            grid=(rows // tile,),
            in_specs=[pl.BlockSpec((tile, block), lambda n, w: (first + n, w[1] ^ far))],
            out_specs=tuple(
                pl.BlockSpec((tile, width), lambda n, w: (n, 0)) for _ in range(count)
            ),
        ),
        compiler_params=params(58),
        name="inverse",
    )(where, corrected)


def halves_body(where, *refs):
    pieces, (own, other) = refs[:-2], refs[-2:]
    width = own.shape[1]
    first = 0
    for piece in pieces:
        rows, block = piece.shape
        for r, out in enumerate((own, other)):
            at = pl.multiple_of((where[3] ^ r) * (block - width), LANES)
            out[first : first + rows, :] = piece[:, pl.ds(at, width)]
        first += rows


def halves(where, pieces, width):
    rows = sum(p.shape[0] for p in pieces)
    return pl.pallas_call(
        halves_body,
        out_shape=tuple(jax.ShapeDtypeStruct((rows, width), BF) for _ in range(2)),
        in_specs=[SMEM_SPEC, *([VMEM_SPEC] * len(pieces))],
        out_specs=(VMEM_SPEC, VMEM_SPEC),
        compiler_params=params(6),
        name="halves",
    )(where, *pieces)


def pack_body(where, train_ids, basis, tokens, delta, *outs):
    rows = basis.shape[1]
    train, stored = train_ids.shape[0], tokens.shape[0]
    line = lax.broadcasted_iota(jnp.int32, (stored, stored), 0)
    lane = lax.broadcasted_iota(jnp.int32, (stored, stored), 1)
    chosen = jnp.zeros((stored, stored), jnp.bool_)
    for b in range(train):
        chosen = jnp.logical_or(chosen, jnp.logical_and(line == b, lane == train_ids[b]))
    chosen = jnp.where(chosen, 1.0, 0.0).astype(BF)
    gradients = dot(chosen, delta[...], 1, 0).astype(BF)[:train]
    for r, out in enumerate(outs):
        width = out.shape[1]
        block = basis.shape[2]
        skip = block - width
        blk, half = where[1] ^ (r // 2), where[3] ^ (r % 2)
        out[:rows, :] = basis[blk, :, pl.ds(pl.multiple_of(half * skip, LANES), width)]
        own = tokens[:, pl.ds(pl.multiple_of(blk * block, LANES), block)]
        own = dot(chosen, own, 1, 0).astype(BF)[:train]
        out[rows : rows + train, :] = own[:, :width]
        out[rows + train :, :skip] = own[:, width:]
        out[rows + train :, skip:] = gradients


def pack(where, train_ids, basis, tokens, delta, width):
    rows = basis.shape[1] + 2 * train_ids.shape[0]
    return pl.pallas_call(
        pack_body,
        out_shape=tuple(jax.ShapeDtypeStruct((rows, width), BF) for _ in range(4)),
        in_specs=[SMEM_SPEC, SMEM_SPEC, VMEM_SPEC, VMEM_SPEC, VMEM_SPEC],
        out_specs=tuple([VMEM_SPEC] * 4),
        compiler_params=params(4),
        name="pack",
    )(where, train_ids, basis, tokens, delta)


def arrange_body(where, a0, a1, a2, a3, out, *, local, train):
    me = 2 * where[1] + where[3]
    rows = out.shape[0]
    each = local + 2 * train
    to = lax.broadcasted_iota(jnp.int32, (rows, each), 0)
    at = lax.broadcasted_iota(jnp.int32, (rows, each), 1)
    total = None
    for r, part in enumerate((a0, a1, a2, a3)):
        src = me ^ r
        head = src * local + at
        token = 4 * local + src * train + at - local
        other = 4 * local + 4 * train + src * train + at - local - train
        goal = jnp.where(at < local, head, jnp.where(at < local + train, token, other))
        term = dot(jnp.where(goal == to, 1.0, 0.0).astype(BF), part[...], 1, 0)
        total = term if total is None else total + term
    out[...] = total.astype(BF)


def arrange(where, parts, local, train):
    rows, width = parts[0].shape
    return pl.pallas_call(
        functools.partial(arrange_body, local=local, train=train),
        out_shape=jax.ShapeDtypeStruct((4 * rows, width), BF),
        in_specs=[SMEM_SPEC, *([VMEM_SPEC] * 4)],
        out_specs=VMEM_SPEC,
        compiler_params=params(3),
        name="arrange",
    )(where, *parts)


def rotate_body(where, ids, v0, v1, v2, v3, *refs):
    chunks, (basis, right, tokens, delta) = refs[:-4], refs[-4:]
    n_z = len(chunks)
    slab = basis.shape[0] // n_z
    extra = (chunks[0].shape[0] - slab) // 2
    for k, chunk in enumerate(chunks):
        step = k if k <= n_z // 2 else k - n_z
        at = lax.rem(where[0] - step + n_z, n_z) * slab
        basis[pl.ds(pl.multiple_of(at, 16), slab), :] = chunk[:slab, :]
    factors = jnp.concatenate([v[0] for v in (v0, v1, v2, v3)], axis=0)
    whole = basis[...]
    right[...] = dot(factors, whole, 1, 0).astype(BF)
    width = whole.shape[1]
    rest = whole.shape[0] - width
    head = jnp.concatenate([c[slab : slab + extra, :] for c in chunks], axis=0)
    tail = jnp.concatenate([c[slab + extra :, :] for c in chunks], axis=0)
    rotated = dot(head, whole[:width, :], 1, 0) + dot(tail[:, :rest], whole[width:, :], 1, 0)
    tokens[...] = rotated.astype(BF)
    delta[...] = tail[:, rest:]


def rotate(where, query_ids, v_t, chunks, block):
    queries = query_ids.shape[0]
    rank = v_t.shape[1]
    rows, width = chunks[0].shape
    extra = (rows * len(chunks) - block) // 2
    specs = [
        pl.BlockSpec(
            (1, rank, block), functools.partial(lambda q, n, w, ids: (ids[q], 0, w[1]), q)
        )
        for q in range(queries)
    ]

    def full(shape):
        return pl.BlockSpec(shape, lambda n, w, ids: (0, 0))

    shapes = (
        (block, width),
        (queries * rank, width),
        (extra, width),
        (extra, 2 * width - block),
    )
    return pl.pallas_call(
        rotate_body,
        out_shape=tuple(jax.ShapeDtypeStruct(s, BF) for s in shapes),
        grid_spec=pltpu.PrefetchScalarGridSpec(
            num_scalar_prefetch=2,
            grid=(1,),
            in_specs=[*specs, *(full((rows, width)) for _ in chunks)],
            out_specs=tuple(full(s) for s in shapes),
        ),
        compiler_params=params(20),
        name="rotate",
    )(where, query_ids, v_t, v_t, v_t, v_t, *chunks)


def back_terms(right, lefts, windows, inverses, rank, q):
    at = slice(q * rank, (q + 1) * rank)
    total = None
    pieces = len(inverses) // 2
    for k, (left, window) in enumerate(zip(lefts, windows)):
        inverse = jnp.concatenate(
            [i[...] for i in inverses[k * pieces : (k + 1) * pieces]], axis=0
        )
        product = dot(left[at, :], right[at, :], 0, 0)
        precond = (product * inverse.astype(F32)).astype(BF)
        term = dot(window[...], precond, 1, 0)
        total = term if total is None else total + term
    return total


def back_first_body(right, *refs):
    out = refs[6]
    queries = out.shape[0]
    rank = right.shape[0] // queries
    for q in range(queries):
        out[q] = back_terms(right, refs[:2], refs[2:4], refs[4:6], rank, q)


def back_first(right, lefts, windows, inverses, queries):
    width = right.shape[1]
    win, depth = windows[0].shape
    return pl.pallas_call(
        back_first_body,
        out_shape=jax.ShapeDtypeStruct((queries, win, width), F32),
        in_specs=[VMEM_SPEC] * 7,
        out_specs=VMEM_SPEC,
        compiler_params=params(10),
        name="back_first",
    )(right, *lefts, *windows, *inverses)


def back_body(where, block_ids, so_far, factors, right, tokens, delta, *refs, train):
    refs, (out, score) = refs[:-2], refs[-2:]
    queries = so_far.shape[0]
    n_z, rows, width = out.shape
    per = rows // queries
    rank = right.shape[0] // queries
    valid = factors.shape[1] // 2
    skip = factors.shape[1] - width
    chosen = block_ids[2 * where[2] + where[1]]
    row = factors[pl.ds(chosen, 1), pl.ds(pl.multiple_of(where[3] * skip, LANES), width)]
    lane = lax.broadcasted_iota(jnp.int32, (1, width), 1)
    first = where[3] * (width - valid)
    mine = jnp.logical_and(lane >= first, lane < first + valid)
    scale = jnp.where(mine, 1.0 / row, 0.0)
    which = lax.rem(lax.broadcasted_iota(jnp.int32, (tokens.shape[0], 1), 0), train)
    place = lax.broadcasted_iota(jnp.int32, (1, LANES), 1)
    table = jnp.zeros((1, LANES), F32)
    for q in range(queries):
        total = so_far[q] + back_terms(right, refs[:2], refs[2:4], refs[4:], rank, q)
        total = (total * scale).astype(BF)
        out[:, q * per : (q + 1) * per, :] = total.reshape(n_z, per, width)
        projected = dot(tokens[...], total, 1, 1) * delta[...].astype(F32)
        for b in range(train):
            part = jnp.sum(jnp.where(which == b, projected, 0.0), axis=0, keepdims=True)
            part = jnp.sum(part, axis=1, keepdims=True)
            table = jnp.where(place == q * train + b, part, table)
    score[...] = table


def back(where, block_ids, so_far, factors, right, tokens, delta, far, n_z, train):
    queries, win, width = so_far.shape
    return pl.pallas_call(
        functools.partial(back_body, train=train),
        out_shape=(
            jax.ShapeDtypeStruct((n_z, queries * win // n_z, width), BF),
            jax.ShapeDtypeStruct((1, LANES), F32),
        ),
        in_specs=[SMEM_SPEC, SMEM_SPEC, *([VMEM_SPEC] * (5 + len(far)))],
        out_specs=(VMEM_SPEC, VMEM_SPEC),
        compiler_params=params(12),
        name="back",
    )(where, block_ids, so_far, factors, right, tokens, delta, *far)


def tile_body(where, parts, basis, *outs, queries):
    n_z, rows, _ = parts.shape
    me = 2 * where[1] + where[3]
    own = rows // 4
    per = own // queries
    total = parts[0].astype(F32)
    for k in range(1, n_z):
        total += parts[k].astype(F32)
    to = lax.broadcasted_iota(jnp.int32, (rows, rows), 0)
    at = lax.broadcasted_iota(jnp.int32, (rows, rows), 1)
    query = at // own
    owner = lax.rem(at // per, 4)
    goal = (owner ^ me) * own + query * per + lax.rem(at, per)
    select = jnp.where(goal == to, 1.0, 0.0).astype(BF)
    half = dot(select, total.astype(BF), 1, 0).astype(BF)
    tiles = dot(half, basis[...], 1, 1).astype(BF)
    for r, out in enumerate(outs):
        out[...] = tiles[r * own : (r + 1) * own]


def tile_part(where, parts, basis, queries):
    own = parts.shape[1] // 4
    return pl.pallas_call(
        functools.partial(tile_body, queries=queries),
        out_shape=tuple(jax.ShapeDtypeStruct((own, basis.shape[0]), BF) for _ in range(4)),
        in_specs=[SMEM_SPEC, VMEM_SPEC, VMEM_SPEC],
        out_specs=tuple([VMEM_SPEC] * 4),
        compiler_params=params(8),
        name="tile",
    )(where, parts, basis)


def final_body(where, t0, t1, t2, t3, score, tiles, scores):
    queries, per, columns = tiles.shape
    block = columns // 2
    for r, (a, b) in enumerate(((t0, t1), (t2, t3))):
        total = (a[...].astype(F32) + b[...].astype(F32)).astype(BF)
        at = pl.multiple_of((where[1] ^ r) * block, LANES)
        for q in range(queries):
            tiles[q, :, pl.ds(at, block)] = total[q * per : (q + 1) * per]
    sums = jnp.sum(score[...], axis=0)
    train = scores.shape[1]
    for q in range(queries):
        scores[q : q + 1, :] = sums[:, q * train : (q + 1) * train]


def final(where, parts, score, queries, train):
    own, block = parts[0].shape
    return pl.pallas_call(
        final_body,
        out_shape=(
            jax.ShapeDtypeStruct((queries, own // queries, 2 * block), BF),
            jax.ShapeDtypeStruct((queries, train), F32),
        ),
        in_specs=[SMEM_SPEC, *([VMEM_SPEC] * 5)],
        out_specs=(VMEM_SPEC, VMEM_SPEC),
        compiler_params=params(3),
        name="final",
    )(where, *parts, score)


def shards(
    basis_out,
    corrected,
    factor_table,
    block_ids,
    basis_in,
    query_ids,
    u_pool,
    v_pool,
    train_ids,
    x_pool,
    delta_pool,
):
    n_z, n_in = lax.axis_size("z"), lax.axis_size(IN)
    z, xh, c = lax.axis_index("z"), lax.axis_index("xh"), lax.axis_index("c")
    in_pos = lax.axis_index(IN)
    queries, train = query_ids.shape[0], train_ids.shape[0]
    _, local_rows, block = basis_in.shape
    width = -(-(block // 2) // LANES) * LANES
    where = jnp.stack([z, xh, in_pos, c]).astype(jnp.int32)

    packed = pack(where, train_ids, basis_in, x_pool[:, 0], delta_pool[:, 0], width)
    parts = (
        packed[0],
        swap(packed[1], "c"),
        swap(packed[2], "xh"),
        swap(packed[3], QUAD, 3),
    )
    rows = corrected.shape[0]
    ends = (0, 3 * rows // 8, 3 * rows // 4, rows)
    far = [
        inverse_block(where, corrected, block, 1, block, 1, a, b)[0]
        for a, b in zip(ends[:-1], ends[1:])
    ]
    partial = left_part(query_ids, jnp.transpose(u_pool, (0, 2, 1)), basis_out, n_in)
    own = arrange(where, (after(packed[0], far[0], partial), *parts[1:]), local_rows, train)
    near = inverse_block(where, corrected, block, 0, width, 2)
    near = (near[0], swap(near[1], "c"))

    ahead, behind = [shift(own, 1)], [shift(own, -1)]
    far[0] = swap(far[0], "xh")
    spread, window = left_sum(exchange(partial, IN))
    up, down = after((ahead[0], behind[0]), spread)
    far[1] = swap(after(far[1], ahead[0], spread), "xh")
    ahead.append(shift(up, 1))
    behind.append(shift(down, -1))
    left = exchange(spread, IN).reshape(-1, basis_out.shape[1])
    up, down, left = after((ahead[1], behind[1], left), far[0])
    ahead.append(shift(up, 1))
    behind.append(shift(down, -1))
    up = after(ahead[2], behind[2], far[1])
    ahead.append(shift(up, 1))
    far[2] = swap(after(far[2], left), "xh")
    left_x, window_x = swap(left, "xh"), swap(window, "xh")
    lefts = (left, swap(left, "c"))
    windows = (window, swap(window, "c"))
    chunks = (own, *ahead, *behind[::-1])

    basis, right, tokens, delta = rotate(
        where, query_ids, jnp.transpose(v_pool, (0, 2, 1)), chunks, block
    )
    so_far = back_first(right, lefts, windows, near, queries)
    left_x, window_x, *far = after((left_x, window_x, *far), so_far)
    far = halves(where, far, width)
    far = (left_x, swap(left_x, "c"), window_x, swap(window_x, "c"), far[0], swap(far[1], "c"))
    parts, score = back(
        where, block_ids, so_far, factor_table, right, tokens, delta, far, n_z, train
    )
    for axis, mask in (("c", 1), ("xl", 1), ("y", 1), ("y", 2), ("xh", 1)):
        score = score + swap(score, axis, mask)
    parts, score = after((exchange(parts, "z"), score))
    parts = tile_part(where, parts, basis, queries)
    score = exchange(jnp.broadcast_to(score, (n_z, *score.shape)), "z")
    parts = (
        parts[0],
        swap(parts[1], "c"),
        swap(parts[2], "xh"),
        swap(parts[3], QUAD, 3),
    )
    return final(where, parts, score, queries, train)


def solution(mesh):
    split = Mesh(mesh.devices.reshape(8, 2, 2, 4, 2), ("z", "xh", "c", "y", "xl"))
    return jax.shard_map(
        shards,
        mesh=split,
        in_specs=(
            P(IN, OUT),
            P(OUT, IN),
            P(),
            P(),
            P(IN, OUT, None),
            P(),
            P(None, IN, None),
            P(None, IN, None),
            P(),
            P(None, OUT, IN),
            P(None, OUT, None),
        ),
        out_specs=(P(None, OUT, IN), P()),
        check_vma=False,
    )
```

```python
import functools

import jax
import jax.numpy as jnp
from jax import lax
from jax.experimental import pallas as pl
from jax.experimental.pallas import tpu as pltpu
from jax.sharding import Mesh
from jax.sharding import PartitionSpec as P

WIN_ROWS = 16
OUT = ("z", "xh", "c")
IN = ("y", "xl")
QUAD = ("xh", "c")
PLANE = ("xh", "c", "y", "xl")
BF = jnp.bfloat16
F32 = jnp.float32
LANES = 128
MIB = 2**20

VMEM_SPEC = pl.BlockSpec(memory_space=pltpu.VMEM)
SMEM_SPEC = pl.BlockSpec(memory_space=pltpu.SMEM)


def params(mib):
    return pltpu.CompilerParams(vmem_limit_bytes=mib * MIB)


def dot(a, b, ca, cb):
    return lax.dot_general(a, b, (((ca,), (cb,)), ((), ())), preferred_element_type=F32)


def exchange(value, axis):
    return lax.all_to_all(value, axis, split_axis=0, concat_axis=0, tiled=True)


def swap(value, axis, mask=1):
    size = lax.axis_size(axis)
    return lax.ppermute(value, axis, [(i, i ^ mask) for i in range(size)])


def shift(value, step):
    size = lax.axis_size("z")
    return lax.ppermute(value, "z", [(i, (i + step) % size) for i in range(size)])


def after(value, *others):
    return lax.optimization_barrier((value, others))[0]


def left_body(ids, u0, u1, u2, u3, basis, out):
    left = jnp.concatenate([u[0] for u in (u0, u1, u2, u3)], axis=0)
    n_in, rows, width = out.shape
    part = dot(left, basis[...], 1, 0).astype(BF)
    out[:, : rows - WIN_ROWS, :] = part.reshape(n_in, rows - WIN_ROWS, width)
    out[:, rows - WIN_ROWS :, :] = jnp.broadcast_to(
        basis[:WIN_ROWS, :][None], (n_in, WIN_ROWS, width)
    )


def left_part(query_ids, u_t, basis_out, n_in):
    queries = query_ids.shape[0]
    _, rank, depth = u_t.shape
    eigen = basis_out.shape[1]
    rows = queries * rank // n_in + WIN_ROWS
    tile = 256
    specs = [
        pl.BlockSpec((1, rank, depth), functools.partial(lambda q, n, ids: (ids[q], 0, 0), q))
        for q in range(queries)
    ]
    return pl.pallas_call(
        left_body,
        out_shape=jax.ShapeDtypeStruct((n_in, rows, eigen), BF),
        grid_spec=pltpu.PrefetchScalarGridSpec(
            num_scalar_prefetch=1,
            grid=(eigen // tile,),
            in_specs=[*specs, pl.BlockSpec((depth, tile), lambda n, ids: (0, n))],
            out_specs=pl.BlockSpec((n_in, rows, tile), lambda n, ids: (0, 0, n)),
        ),
        compiler_params=params(16),
        name="left",
    )(query_ids, u_t, u_t, u_t, u_t, basis_out)


def left_sum_body(parts, out, window):
    n_in, rows, _ = parts.shape
    own = rows - WIN_ROWS
    total = parts[0, :own, :].astype(F32)
    for i in range(1, n_in):
        total += parts[i, :own, :].astype(F32)
    total = total.astype(BF)
    for i in range(n_in):
        out[i] = total
        window[i * WIN_ROWS : (i + 1) * WIN_ROWS, :] = parts[i, own:, :]


def left_sum(parts):
    n_in, rows, eigen = parts.shape
    return pl.pallas_call(
        left_sum_body,
        out_shape=(
            jax.ShapeDtypeStruct((n_in, rows - WIN_ROWS, eigen), BF),
            jax.ShapeDtypeStruct((n_in * WIN_ROWS, eigen), BF),
        ),
        in_specs=[VMEM_SPEC],
        out_specs=(VMEM_SPEC, VMEM_SPEC),
        compiler_params=params(4),
        name="left_sum",
    )(parts)


def inverse_body(where, corrected, *outs):
    width = outs[0].shape[1]
    skip = corrected.shape[1] - width
    for r, out in enumerate(outs):
        at = pl.multiple_of((where[3] ^ r) * skip, LANES) if skip else 0
        out[...] = (1.0 / corrected[:, pl.ds(at, width)]).astype(BF)


def inverse_block(where, corrected, block, far, width, count, start=0, stop=None):
    rows = (stop or corrected.shape[0]) - start
    tile = min(rows, 256)
    while start % tile or rows % tile:
        tile -= 64
    first = start // tile
    return pl.pallas_call(
        inverse_body,
        out_shape=tuple(jax.ShapeDtypeStruct((rows, width), BF) for _ in range(count)),
        grid_spec=pltpu.PrefetchScalarGridSpec(
            num_scalar_prefetch=1,
            grid=(rows // tile,),
            in_specs=[pl.BlockSpec((tile, block), lambda n, w: (first + n, w[1] ^ far))],
            out_specs=tuple(
                pl.BlockSpec((tile, width), lambda n, w: (n, 0)) for _ in range(count)
            ),
        ),
        compiler_params=params(58),
        name="inverse",
    )(where, corrected)


def halves_body(where, *refs):
    pieces, (own, other) = refs[:-2], refs[-2:]
    width = own.shape[1]
    first = 0
    for piece in pieces:
        rows, block = piece.shape
        for r, out in enumerate((own, other)):
            at = pl.multiple_of((where[3] ^ r) * (block - width), LANES)
            out[first : first + rows, :] = piece[:, pl.ds(at, width)]
        first += rows


def halves(where, pieces, width):
    rows = sum(p.shape[0] for p in pieces)
    return pl.pallas_call(
        halves_body,
        out_shape=tuple(jax.ShapeDtypeStruct((rows, width), BF) for _ in range(2)),
        in_specs=[SMEM_SPEC, *([VMEM_SPEC] * len(pieces))],
        out_specs=(VMEM_SPEC, VMEM_SPEC),
        compiler_params=params(6),
        name="halves",
    )(where, *pieces)


def pack_body(where, train_ids, basis, tokens, delta, *outs):
    rows = basis.shape[1]
    train, stored = train_ids.shape[0], tokens.shape[0]
    line = lax.broadcasted_iota(jnp.int32, (stored, stored), 0)
    lane = lax.broadcasted_iota(jnp.int32, (stored, stored), 1)
    chosen = jnp.zeros((stored, stored), jnp.bool_)
    for b in range(train):
        chosen = jnp.logical_or(chosen, jnp.logical_and(line == b, lane == train_ids[b]))
    chosen = jnp.where(chosen, 1.0, 0.0).astype(BF)
    gradients = dot(chosen, delta[...], 1, 0).astype(BF)[:train]
    for r, out in enumerate(outs):
        width = out.shape[1]
        block = basis.shape[2]
        skip = block - width
        blk, half = where[1] ^ (r // 2), where[3] ^ (r % 2)
        out[:rows, :] = basis[blk, :, pl.ds(pl.multiple_of(half * skip, LANES), width)]
        own = tokens[:, pl.ds(pl.multiple_of(blk * block, LANES), block)]
        own = dot(chosen, own, 1, 0).astype(BF)[:train]
        out[rows : rows + train, :] = own[:, :width]
        out[rows + train :, :skip] = own[:, width:]
        out[rows + train :, skip:] = gradients


def pack(where, train_ids, basis, tokens, delta, width):
    rows = basis.shape[1] + 2 * train_ids.shape[0]
    return pl.pallas_call(
        pack_body,
        out_shape=tuple(jax.ShapeDtypeStruct((rows, width), BF) for _ in range(4)),
        in_specs=[SMEM_SPEC, SMEM_SPEC, VMEM_SPEC, VMEM_SPEC, VMEM_SPEC],
        out_specs=tuple([VMEM_SPEC] * 4),
        compiler_params=params(4),
        name="pack",
    )(where, train_ids, basis, tokens, delta)


def arrange_body(where, a0, a1, a2, a3, out, *, local, train):
    me = 2 * where[1] + where[3]
    rows = out.shape[0]
    each = local + 2 * train
    to = lax.broadcasted_iota(jnp.int32, (rows, each), 0)
    at = lax.broadcasted_iota(jnp.int32, (rows, each), 1)
    total = None
    for r, part in enumerate((a0, a1, a2, a3)):
        src = me ^ r
        head = src * local + at
        token = 4 * local + src * train + at - local
        other = 4 * local + 4 * train + src * train + at - local - train
        goal = jnp.where(at < local, head, jnp.where(at < local + train, token, other))
        term = dot(jnp.where(goal == to, 1.0, 0.0).astype(BF), part[...], 1, 0)
        total = term if total is None else total + term
    out[...] = total.astype(BF)


def arrange(where, parts, local, train):
    rows, width = parts[0].shape
    return pl.pallas_call(
        functools.partial(arrange_body, local=local, train=train),
        out_shape=jax.ShapeDtypeStruct((4 * rows, width), BF),
        in_specs=[SMEM_SPEC, *([VMEM_SPEC] * 4)],
        out_specs=VMEM_SPEC,
        compiler_params=params(3),
        name="arrange",
    )(where, *parts)


def rotate_body(where, ids, v0, v1, v2, v3, *refs):
    chunks, (basis, right, tokens, delta) = refs[:-4], refs[-4:]
    n_z = len(chunks)
    slab = basis.shape[0] // n_z
    extra = (chunks[0].shape[0] - slab) // 2
    for k, chunk in enumerate(chunks):
        step = k if k <= n_z // 2 else k - n_z
        at = lax.rem(where[0] - step + n_z, n_z) * slab
        basis[pl.ds(pl.multiple_of(at, 16), slab), :] = chunk[:slab, :]
    factors = jnp.concatenate([v[0] for v in (v0, v1, v2, v3)], axis=0)
    whole = basis[...]
    right[...] = dot(factors, whole, 1, 0).astype(BF)
    width = whole.shape[1]
    rest = whole.shape[0] - width
    head = jnp.concatenate([c[slab : slab + extra, :] for c in chunks], axis=0)
    tail = jnp.concatenate([c[slab + extra :, :] for c in chunks], axis=0)
    rotated = dot(head, whole[:width, :], 1, 0) + dot(tail[:, :rest], whole[width:, :], 1, 0)
    tokens[...] = rotated.astype(BF)
    delta[...] = tail[:, rest:]


def rotate(where, query_ids, v_t, chunks, block):
    queries = query_ids.shape[0]
    rank = v_t.shape[1]
    rows, width = chunks[0].shape
    extra = (rows * len(chunks) - block) // 2
    specs = [
        pl.BlockSpec(
            (1, rank, block), functools.partial(lambda q, n, w, ids: (ids[q], 0, w[1]), q)
        )
        for q in range(queries)
    ]

    def full(shape):
        return pl.BlockSpec(shape, lambda n, w, ids: (0, 0))

    shapes = (
        (block, width),
        (queries * rank, width),
        (extra, width),
        (extra, 2 * width - block),
    )
    return pl.pallas_call(
        rotate_body,
        out_shape=tuple(jax.ShapeDtypeStruct(s, BF) for s in shapes),
        grid_spec=pltpu.PrefetchScalarGridSpec(
            num_scalar_prefetch=2,
            grid=(1,),
            in_specs=[*specs, *(full((rows, width)) for _ in chunks)],
            out_specs=tuple(full(s) for s in shapes),
        ),
        compiler_params=params(20),
        name="rotate",
    )(where, query_ids, v_t, v_t, v_t, v_t, *chunks)


def back_terms(right, lefts, windows, inverses, rank, q):
    at = slice(q * rank, (q + 1) * rank)
    total = None
    pieces = len(inverses) // 2
    for k, (left, window) in enumerate(zip(lefts, windows)):
        inverse = jnp.concatenate(
            [i[...] for i in inverses[k * pieces : (k + 1) * pieces]], axis=0
        )
        product = dot(left[at, :], right[at, :], 0, 0)
        precond = (product * inverse.astype(F32)).astype(BF)
        term = dot(window[...], precond, 1, 0)
        total = term if total is None else total + term
    return total


def back_first_body(right, *refs):
    out = refs[6]
    queries = out.shape[0]
    rank = right.shape[0] // queries
    for q in range(queries):
        out[q] = back_terms(right, refs[:2], refs[2:4], refs[4:6], rank, q)


def back_first(right, lefts, windows, inverses, queries):
    width = right.shape[1]
    win, depth = windows[0].shape
    return pl.pallas_call(
        back_first_body,
        out_shape=jax.ShapeDtypeStruct((queries, win, width), F32),
        in_specs=[VMEM_SPEC] * 7,
        out_specs=VMEM_SPEC,
        compiler_params=params(10),
        name="back_first",
    )(right, *lefts, *windows, *inverses)


def back_body(where, block_ids, so_far, factors, right, *refs):
    refs, out = refs[:-1], refs[-1]
    queries = so_far.shape[0]
    n_z, rows, width = out.shape
    per = rows // queries
    rank = right.shape[0] // queries
    valid = factors.shape[1] // 2
    skip = factors.shape[1] - width
    chosen = block_ids[2 * where[2] + where[1]]
    row = factors[pl.ds(chosen, 1), pl.ds(pl.multiple_of(where[3] * skip, LANES), width)]
    lane = lax.broadcasted_iota(jnp.int32, (1, width), 1)
    first = where[3] * (width - valid)
    mine = jnp.logical_and(lane >= first, lane < first + valid)
    scale = jnp.where(mine, 1.0 / row, 0.0)
    for q in range(queries):
        total = so_far[q] + back_terms(right, refs[:2], refs[2:4], refs[4:], rank, q)
        total = (total * scale).astype(BF)
        out[:, q * per : (q + 1) * per, :] = total.reshape(n_z, per, width)


def back(where, block_ids, so_far, factors, right, far, n_z):
    queries, win, width = so_far.shape
    return pl.pallas_call(
        back_body,
        out_shape=jax.ShapeDtypeStruct((n_z, queries * win // n_z, width), BF),
        in_specs=[SMEM_SPEC, SMEM_SPEC, *([VMEM_SPEC] * (3 + len(far)))],
        out_specs=VMEM_SPEC,
        compiler_params=params(12),
        name="back",
    )(where, block_ids, so_far, factors, right, *far)


def score_body(parts, tokens, delta, score, *, queries, train):
    n_z, rows, width = parts.shape
    per = rows // queries
    which = lax.rem(lax.broadcasted_iota(jnp.int32, (tokens.shape[0], 1), 0), train)
    place = lax.broadcasted_iota(jnp.int32, (1, LANES), 1)
    table = jnp.zeros((1, LANES), F32)
    for q in range(queries):
        part = parts[:, q * per : (q + 1) * per, :].reshape(n_z * per, width)
        projected = dot(tokens[...], part, 1, 1) * delta[...].astype(F32)
        for b in range(train):
            line = jnp.sum(jnp.where(which == b, projected, 0.0), axis=0, keepdims=True)
            value = jnp.sum(line, axis=1, keepdims=True)
            table = jnp.where(place == q * train + b, value, table)
    score[...] = table


def score_part(parts, tokens, delta, queries, train):
    return pl.pallas_call(
        functools.partial(score_body, queries=queries, train=train),
        out_shape=jax.ShapeDtypeStruct((1, LANES), F32),
        in_specs=[VMEM_SPEC] * 3,
        out_specs=VMEM_SPEC,
        compiler_params=params(4),
        name="score",
    )(parts, tokens, delta)


def tile_body(where, parts, basis, *outs, queries):
    n_z, rows, _ = parts.shape
    me = 2 * where[1] + where[3]
    own = rows // 4
    per = own // queries
    total = parts[0].astype(F32)
    for k in range(1, n_z):
        total += parts[k].astype(F32)
    to = lax.broadcasted_iota(jnp.int32, (rows, rows), 0)
    at = lax.broadcasted_iota(jnp.int32, (rows, rows), 1)
    query = at // own
    owner = lax.rem(at // per, 4)
    goal = (owner ^ me) * own + query * per + lax.rem(at, per)
    select = jnp.where(goal == to, 1.0, 0.0).astype(BF)
    half = dot(select, total.astype(BF), 1, 0).astype(BF)
    tiles = dot(half, basis[...], 1, 1).astype(BF)
    for r, out in enumerate(outs):
        out[...] = tiles[r * own : (r + 1) * own]


def tile_part(where, parts, basis, queries):
    own = parts.shape[1] // 4
    return pl.pallas_call(
        functools.partial(tile_body, queries=queries),
        out_shape=tuple(jax.ShapeDtypeStruct((own, basis.shape[0]), BF) for _ in range(4)),
        in_specs=[SMEM_SPEC, VMEM_SPEC, VMEM_SPEC],
        out_specs=tuple([VMEM_SPEC] * 4),
        compiler_params=params(8),
        name="tile",
    )(where, parts, basis)


def final_body(where, t0, t1, t2, t3, score, tiles, scores):
    queries, per, columns = tiles.shape
    block = columns // 2
    for r, (a, b) in enumerate(((t0, t1), (t2, t3))):
        total = (a[...].astype(F32) + b[...].astype(F32)).astype(BF)
        at = pl.multiple_of((where[1] ^ r) * block, LANES)
        for q in range(queries):
            tiles[q, :, pl.ds(at, block)] = total[q * per : (q + 1) * per]
    sums = jnp.sum(score[:, :1, :], axis=0)
    train = scores.shape[1]
    for q in range(queries):
        scores[q : q + 1, :] = sums[:, q * train : (q + 1) * train]


def final(where, parts, score, queries, train):
    own, block = parts[0].shape
    return pl.pallas_call(
        final_body,
        out_shape=(
            jax.ShapeDtypeStruct((queries, own // queries, 2 * block), BF),
            jax.ShapeDtypeStruct((queries, train), F32),
        ),
        in_specs=[SMEM_SPEC, *([VMEM_SPEC] * 5)],
        out_specs=(VMEM_SPEC, VMEM_SPEC),
        compiler_params=params(3),
        name="final",
    )(where, *parts, score)


def shards(
    basis_out,
    corrected,
    factor_table,
    block_ids,
    basis_in,
    query_ids,
    u_pool,
    v_pool,
    train_ids,
    x_pool,
    delta_pool,
):
    n_z, n_in = lax.axis_size("z"), lax.axis_size(IN)
    z, xh, c = lax.axis_index("z"), lax.axis_index("xh"), lax.axis_index("c")
    in_pos = lax.axis_index(IN)
    queries, train = query_ids.shape[0], train_ids.shape[0]
    _, local_rows, block = basis_in.shape
    width = -(-(block // 2) // LANES) * LANES
    where = jnp.stack([z, xh, in_pos, c]).astype(jnp.int32)

    packed = pack(where, train_ids, basis_in, x_pool[:, 0], delta_pool[:, 0], width)
    parts = (
        packed[0],
        swap(packed[1], "c"),
        swap(packed[2], "xh"),
        swap(packed[3], QUAD, 3),
    )
    rows = corrected.shape[0]
    ends = (0, 3 * rows // 8, 3 * rows // 4, rows)
    far = [
        inverse_block(where, corrected, block, 1, block, 1, a, b)[0]
        for a, b in zip(ends[:-1], ends[1:])
    ]
    partial = left_part(query_ids, jnp.transpose(u_pool, (0, 2, 1)), basis_out, n_in)
    own = arrange(where, (after(packed[0], far[0], partial), *parts[1:]), local_rows, train)
    near = inverse_block(where, corrected, block, 0, width, 2)
    near = (near[0], swap(near[1], "c"))

    ahead, behind = [shift(own, 1)], [shift(own, -1)]
    far[0] = swap(far[0], "xh")
    spread, window = left_sum(exchange(partial, IN))
    up, down = after((ahead[0], behind[0]), spread)
    far[1] = swap(after(far[1], ahead[0], spread), "xh")
    ahead.append(shift(up, 1))
    behind.append(shift(down, -1))
    left = exchange(spread, IN).reshape(-1, basis_out.shape[1])
    up, down, left = after((ahead[1], behind[1], left), far[0])
    ahead.append(shift(up, 1))
    behind.append(shift(down, -1))
    up = after(ahead[2], behind[2], far[1])
    ahead.append(shift(up, 1))
    far[2] = swap(after(far[2], left), "xh")
    left_x, window_x = swap(left, "xh"), swap(window, "xh")
    lefts = (left, swap(left, "c"))
    windows = (window, swap(window, "c"))
    chunks = (own, *ahead, *behind[::-1])

    basis, right, tokens, delta = rotate(
        where, query_ids, jnp.transpose(v_pool, (0, 2, 1)), chunks, block
    )
    so_far = back_first(right, lefts, windows, near, queries)
    left_x, window_x, *far = after((left_x, window_x, *far), so_far)
    far = halves(where, far, width)
    far = (left_x, swap(left_x, "c"), window_x, swap(window_x, "c"), far[0], swap(far[1], "c"))
    parts = back(where, block_ids, so_far, factor_table, right, far, n_z)
    score = score_part(parts, tokens, delta, queries, train)
    for axis, mask in (("c", 1), ("xl", 1), ("y", 1), ("y", 2), ("xh", 1)):
        score = score + swap(score, axis, mask)
    parts, score = after((exchange(parts, "z"), score))
    parts = tile_part(where, parts, basis, queries)
    score = exchange(jnp.broadcast_to(score, (n_z, 8, LANES)), "z")
    parts = (
        parts[0],
        swap(parts[1], "c"),
        swap(parts[2], "xh"),
        swap(parts[3], QUAD, 3),
    )
    return final(where, parts, score, queries, train)


def solution(mesh):
    split = Mesh(mesh.devices.reshape(8, 2, 2, 4, 2), ("z", "xh", "c", "y", "xl"))
    return jax.shard_map(
        shards,
        mesh=split,
        in_specs=(
            P(IN, OUT),
            P(OUT, IN),
            P(),
            P(),
            P(IN, OUT, None),
            P(),
            P(None, IN, None),
            P(None, IN, None),
            P(),
            P(None, OUT, IN),
            P(None, OUT, None),
        ),
        out_specs=(P(None, OUT, IN), P()),
        check_vma=False,
    )
```

```python
import functools

import jax
import jax.numpy as jnp
from jax import lax
from jax.experimental import pallas as pl
from jax.experimental.pallas import tpu as pltpu
from jax.sharding import Mesh
from jax.sharding import PartitionSpec as P

WIN_ROWS = 16
OUT = ("z", "xh", "c")
IN = ("y", "xl")
QUAD = ("xh", "c")
PLANE = ("xh", "c", "y", "xl")
BF = jnp.bfloat16
F32 = jnp.float32
LANES = 128
MIB = 2**20

VMEM_SPEC = pl.BlockSpec(memory_space=pltpu.VMEM)
SMEM_SPEC = pl.BlockSpec(memory_space=pltpu.SMEM)


def params(mib):
    return pltpu.CompilerParams(vmem_limit_bytes=mib * MIB)


def dot(a, b, ca, cb):
    return lax.dot_general(a, b, (((ca,), (cb,)), ((), ())), preferred_element_type=F32)


def exchange(value, axis):
    return lax.all_to_all(value, axis, split_axis=0, concat_axis=0, tiled=True)


def swap(value, axis, mask=1):
    size = lax.axis_size(axis)
    return lax.ppermute(value, axis, [(i, i ^ mask) for i in range(size)])


def shift(value, step):
    size = lax.axis_size("z")
    return lax.ppermute(value, "z", [(i, (i + step) % size) for i in range(size)])


def after(value, *others):
    return lax.optimization_barrier((value, others))[0]


def left_body(ids, u0, u1, u2, u3, basis, out):
    left = jnp.concatenate([u[0] for u in (u0, u1, u2, u3)], axis=0)
    n_in, rows, width = out.shape
    part = dot(left, basis[...], 1, 0).astype(BF)
    out[:, : rows - WIN_ROWS, :] = part.reshape(n_in, rows - WIN_ROWS, width)
    out[:, rows - WIN_ROWS :, :] = jnp.broadcast_to(
        basis[:WIN_ROWS, :][None], (n_in, WIN_ROWS, width)
    )


def left_part(query_ids, u_t, basis_out, n_in):
    queries = query_ids.shape[0]
    _, rank, depth = u_t.shape
    eigen = basis_out.shape[1]
    rows = queries * rank // n_in + WIN_ROWS
    tile = 256
    specs = [
        pl.BlockSpec((1, rank, depth), functools.partial(lambda q, n, ids: (ids[q], 0, 0), q))
        for q in range(queries)
    ]
    return pl.pallas_call(
        left_body,
        out_shape=jax.ShapeDtypeStruct((n_in, rows, eigen), BF),
        grid_spec=pltpu.PrefetchScalarGridSpec(
            num_scalar_prefetch=1,
            grid=(eigen // tile,),
            in_specs=[*specs, pl.BlockSpec((depth, tile), lambda n, ids: (0, n))],
            out_specs=pl.BlockSpec((n_in, rows, tile), lambda n, ids: (0, 0, n)),
        ),
        compiler_params=params(16),
        name="left",
    )(query_ids, u_t, u_t, u_t, u_t, basis_out)


def left_sum_body(parts, out, window):
    n_in, rows, _ = parts.shape
    own = rows - WIN_ROWS
    total = parts[0, :own, :].astype(F32)
    for i in range(1, n_in):
        total += parts[i, :own, :].astype(F32)
    total = total.astype(BF)
    for i in range(n_in):
        out[i] = total
        window[i * WIN_ROWS : (i + 1) * WIN_ROWS, :] = parts[i, own:, :]


def left_sum(parts):
    n_in, rows, eigen = parts.shape
    return pl.pallas_call(
        left_sum_body,
        out_shape=(
            jax.ShapeDtypeStruct((n_in, rows - WIN_ROWS, eigen), BF),
            jax.ShapeDtypeStruct((n_in * WIN_ROWS, eigen), BF),
        ),
        in_specs=[VMEM_SPEC],
        out_specs=(VMEM_SPEC, VMEM_SPEC),
        compiler_params=params(4),
        name="left_sum",
    )(parts)


def inverse_body(where, corrected, *outs):
    width = outs[0].shape[1]
    skip = corrected.shape[1] - width
    for r, out in enumerate(outs):
        at = pl.multiple_of((where[3] ^ r) * skip, LANES) if skip else 0
        out[...] = (1.0 / corrected[:, pl.ds(at, width)]).astype(BF)


def inverse_block(where, corrected, block, far, width, count, start=0, stop=None):
    rows = (stop or corrected.shape[0]) - start
    tile = min(rows, 256)
    while start % tile or rows % tile:
        tile -= 64
    first = start // tile
    return pl.pallas_call(
        inverse_body,
        out_shape=tuple(jax.ShapeDtypeStruct((rows, width), BF) for _ in range(count)),
        grid_spec=pltpu.PrefetchScalarGridSpec(
            num_scalar_prefetch=1,
            grid=(rows // tile,),
            in_specs=[pl.BlockSpec((tile, block), lambda n, w: (first + n, w[1] ^ far))],
            out_specs=tuple(
                pl.BlockSpec((tile, width), lambda n, w: (n, 0)) for _ in range(count)
            ),
        ),
        compiler_params=params(58),
        name="inverse",
    )(where, corrected)


def halves_body(where, *refs):
    pieces, (own, other) = refs[:-2], refs[-2:]
    width = own.shape[1]
    first = 0
    for piece in pieces:
        rows, block = piece.shape
        for r, out in enumerate((own, other)):
            at = pl.multiple_of((where[3] ^ r) * (block - width), LANES)
            out[first : first + rows, :] = piece[:, pl.ds(at, width)]
        first += rows


def halves(where, pieces, width):
    rows = sum(p.shape[0] for p in pieces)
    return pl.pallas_call(
        halves_body,
        out_shape=tuple(jax.ShapeDtypeStruct((rows, width), BF) for _ in range(2)),
        in_specs=[SMEM_SPEC, *([VMEM_SPEC] * len(pieces))],
        out_specs=(VMEM_SPEC, VMEM_SPEC),
        compiler_params=params(6),
        name="halves",
    )(where, *pieces)


def pack_body(where, train_ids, basis, tokens, delta, *outs):
    rows = basis.shape[1]
    train, stored = train_ids.shape[0], tokens.shape[0]
    line = lax.broadcasted_iota(jnp.int32, (stored, stored), 0)
    lane = lax.broadcasted_iota(jnp.int32, (stored, stored), 1)
    chosen = jnp.zeros((stored, stored), jnp.bool_)
    for b in range(train):
        chosen = jnp.logical_or(chosen, jnp.logical_and(line == b, lane == train_ids[b]))
    chosen = jnp.where(chosen, 1.0, 0.0).astype(BF)
    gradients = dot(chosen, delta[...], 1, 0).astype(BF)[:train]
    for r, out in enumerate(outs):
        width = out.shape[1]
        block = basis.shape[2]
        skip = block - width
        blk, half = where[1] ^ (r // 2), where[3] ^ (r % 2)
        out[:rows, :] = basis[blk, :, pl.ds(pl.multiple_of(half * skip, LANES), width)]
        own = tokens[:, pl.ds(pl.multiple_of(blk * block, LANES), block)]
        own = dot(chosen, own, 1, 0).astype(BF)[:train]
        out[rows : rows + train, :] = own[:, :width]
        out[rows + train :, :skip] = own[:, width:]
        out[rows + train :, skip:] = gradients


def pack(where, train_ids, basis, tokens, delta, width):
    rows = basis.shape[1] + 2 * train_ids.shape[0]
    return pl.pallas_call(
        pack_body,
        out_shape=tuple(jax.ShapeDtypeStruct((rows, width), BF) for _ in range(4)),
        in_specs=[SMEM_SPEC, SMEM_SPEC, VMEM_SPEC, VMEM_SPEC, VMEM_SPEC],
        out_specs=tuple([VMEM_SPEC] * 4),
        compiler_params=params(4),
        name="pack",
    )(where, train_ids, basis, tokens, delta)


def arrange_body(where, a0, a1, a2, a3, out, *, local, train):
    me = 2 * where[1] + where[3]
    rows = out.shape[0]
    each = local + 2 * train
    to = lax.broadcasted_iota(jnp.int32, (rows, each), 0)
    at = lax.broadcasted_iota(jnp.int32, (rows, each), 1)
    total = None
    for r, part in enumerate((a0, a1, a2, a3)):
        src = me ^ r
        head = src * local + at
        token = 4 * local + src * train + at - local
        other = 4 * local + 4 * train + src * train + at - local - train
        goal = jnp.where(at < local, head, jnp.where(at < local + train, token, other))
        term = dot(jnp.where(goal == to, 1.0, 0.0).astype(BF), part[...], 1, 0)
        total = term if total is None else total + term
    out[...] = total.astype(BF)


def arrange(where, parts, local, train):
    rows, width = parts[0].shape
    return pl.pallas_call(
        functools.partial(arrange_body, local=local, train=train),
        out_shape=jax.ShapeDtypeStruct((4 * rows, width), BF),
        in_specs=[SMEM_SPEC, *([VMEM_SPEC] * 4)],
        out_specs=VMEM_SPEC,
        compiler_params=params(3),
        name="arrange",
    )(where, *parts)


def rotate_body(where, ids, v0, v1, v2, v3, *refs):
    chunks, (basis, right, tokens, delta) = refs[:-4], refs[-4:]
    n_z = len(chunks)
    slab = basis.shape[0] // n_z
    extra = (chunks[0].shape[0] - slab) // 2
    for k, chunk in enumerate(chunks):
        step = k if k <= n_z // 2 else k - n_z
        at = lax.rem(where[0] - step + n_z, n_z) * slab
        basis[pl.ds(pl.multiple_of(at, 16), slab), :] = chunk[:slab, :]
    factors = jnp.concatenate([v[0] for v in (v0, v1, v2, v3)], axis=0)
    whole = basis[...]
    right[...] = dot(factors, whole, 1, 0).astype(BF)
    width = whole.shape[1]
    rest = whole.shape[0] - width
    head = jnp.concatenate([c[slab : slab + extra, :] for c in chunks], axis=0)
    tail = jnp.concatenate([c[slab + extra :, :] for c in chunks], axis=0)
    rotated = dot(head, whole[:width, :], 1, 0) + dot(tail[:, :rest], whole[width:, :], 1, 0)
    tokens[...] = rotated.astype(BF)
    delta[...] = tail[:, rest:]


def rotate(where, query_ids, v_t, chunks, block):
    queries = query_ids.shape[0]
    rank = v_t.shape[1]
    rows, width = chunks[0].shape
    extra = (rows * len(chunks) - block) // 2
    specs = [
        pl.BlockSpec(
            (1, rank, block), functools.partial(lambda q, n, w, ids: (ids[q], 0, w[1]), q)
        )
        for q in range(queries)
    ]

    def full(shape):
        return pl.BlockSpec(shape, lambda n, w, ids: (0, 0))

    shapes = (
        (block, width),
        (queries * rank, width),
        (extra, width),
        (extra, 2 * width - block),
    )
    return pl.pallas_call(
        rotate_body,
        out_shape=tuple(jax.ShapeDtypeStruct(s, BF) for s in shapes),
        grid_spec=pltpu.PrefetchScalarGridSpec(
            num_scalar_prefetch=2,
            grid=(1,),
            in_specs=[*specs, *(full((rows, width)) for _ in chunks)],
            out_specs=tuple(full(s) for s in shapes),
        ),
        compiler_params=params(20),
        name="rotate",
    )(where, query_ids, v_t, v_t, v_t, v_t, *chunks)


def back_terms(right, lefts, windows, inverses, rank, q):
    at = slice(q * rank, (q + 1) * rank)
    total = None
    pieces = len(inverses) // 2
    for k, (left, window) in enumerate(zip(lefts, windows)):
        inverse = jnp.concatenate(
            [i[...] for i in inverses[k * pieces : (k + 1) * pieces]], axis=0
        )
        product = dot(left[at, :], right[at, :], 0, 0)
        precond = (product * inverse.astype(F32)).astype(BF)
        term = dot(window[...], precond, 1, 0)
        total = term if total is None else total + term
    return total


def back_first_body(right, *refs):
    out = refs[6]
    queries = out.shape[0]
    rank = right.shape[0] // queries
    for q in range(queries):
        out[q] = back_terms(right, refs[:2], refs[2:4], refs[4:6], rank, q)


def back_first(right, lefts, windows, inverses, queries):
    width = right.shape[1]
    win, depth = windows[0].shape
    return pl.pallas_call(
        back_first_body,
        out_shape=jax.ShapeDtypeStruct((queries, win, width), F32),
        in_specs=[VMEM_SPEC] * 7,
        out_specs=VMEM_SPEC,
        compiler_params=params(10),
        name="back_first",
    )(right, *lefts, *windows, *inverses)


def back_body(where, block_ids, so_far, factors, right, *refs):
    refs, out = refs[:-1], refs[-1]
    queries = so_far.shape[0]
    n_z, rows, width = out.shape
    per = rows // queries
    rank = right.shape[0] // queries
    valid = factors.shape[1] // 2
    skip = factors.shape[1] - width
    chosen = block_ids[2 * where[2] + where[1]]
    row = factors[pl.ds(chosen, 1), pl.ds(pl.multiple_of(where[3] * skip, LANES), width)]
    lane = lax.broadcasted_iota(jnp.int32, (1, width), 1)
    first = where[3] * (width - valid)
    mine = jnp.logical_and(lane >= first, lane < first + valid)
    scale = jnp.where(mine, 1.0 / row, 0.0)
    for q in range(queries):
        total = so_far[q] + back_terms(right, refs[:2], refs[2:4], refs[4:], rank, q)
        total = (total * scale).astype(BF)
        out[:, q * per : (q + 1) * per, :] = total.reshape(n_z, per, width)


def back(where, block_ids, so_far, factors, right, far, n_z):
    queries, win, width = so_far.shape
    return pl.pallas_call(
        back_body,
        out_shape=jax.ShapeDtypeStruct((n_z, queries * win // n_z, width), BF),
        in_specs=[SMEM_SPEC, SMEM_SPEC, *([VMEM_SPEC] * (3 + len(far)))],
        out_specs=VMEM_SPEC,
        compiler_params=params(12),
        name="back",
    )(where, block_ids, so_far, factors, right, *far)


def score_body(parts, tokens, delta, score, *, queries, train):
    n_z, rows, width = parts.shape
    per = rows // queries
    which = lax.rem(lax.broadcasted_iota(jnp.int32, (tokens.shape[0], 1), 0), train)
    place = lax.broadcasted_iota(jnp.int32, (1, LANES), 1)
    table = jnp.zeros((1, LANES), F32)
    for q in range(queries):
        part = parts[:, q * per : (q + 1) * per, :].reshape(n_z * per, width)
        projected = dot(tokens[...], part, 1, 1) * delta[...].astype(F32)
        for b in range(train):
            line = jnp.sum(jnp.where(which == b, projected, 0.0), axis=0, keepdims=True)
            value = jnp.sum(line, axis=1, keepdims=True)
            table = jnp.where(place == q * train + b, value, table)
    score[...] = table


def score_part(parts, tokens, delta, queries, train):
    return pl.pallas_call(
        functools.partial(score_body, queries=queries, train=train),
        out_shape=jax.ShapeDtypeStruct((1, LANES), F32),
        in_specs=[VMEM_SPEC] * 3,
        out_specs=VMEM_SPEC,
        compiler_params=params(4),
        name="score",
    )(parts, tokens, delta)


def tile_body(where, parts, basis, *outs, queries):
    n_z, rows, _ = parts.shape
    me = 2 * where[1] + where[3]
    own = rows // 4
    per = own // queries
    total = parts[0].astype(F32)
    for k in range(1, n_z):
        total += parts[k].astype(F32)
    to = lax.broadcasted_iota(jnp.int32, (rows, rows), 0)
    at = lax.broadcasted_iota(jnp.int32, (rows, rows), 1)
    query = at // own
    owner = lax.rem(at // per, 4)
    goal = (owner ^ me) * own + query * per + lax.rem(at, per)
    select = jnp.where(goal == to, 1.0, 0.0).astype(BF)
    half = dot(select, total.astype(BF), 1, 0).astype(BF)
    tiles = dot(half, basis[...], 1, 1).astype(BF)
    for r, out in enumerate(outs):
        out[...] = tiles[r * own : (r + 1) * own]


def tile_part(where, parts, basis, queries):
    own = parts.shape[1] // 4
    return pl.pallas_call(
        functools.partial(tile_body, queries=queries),
        out_shape=tuple(jax.ShapeDtypeStruct((own, basis.shape[0]), BF) for _ in range(4)),
        in_specs=[SMEM_SPEC, VMEM_SPEC, VMEM_SPEC],
        out_specs=tuple([VMEM_SPEC] * 4),
        compiler_params=params(8),
        name="tile",
    )(where, parts, basis)


def stage_body(score, basis, out):
    out[...] = basis[...]


def stage(score, basis):
    return pl.pallas_call(
        stage_body,
        out_shape=jax.ShapeDtypeStruct(basis.shape, basis.dtype),
        in_specs=[VMEM_SPEC, VMEM_SPEC],
        out_specs=VMEM_SPEC,
        compiler_params=params(8),
        name="stage",
    )(score, basis)


def final_body(where, t0, t1, t2, t3, score, tiles, scores):
    queries, per, columns = tiles.shape
    block = columns // 2
    for r, (a, b) in enumerate(((t0, t1), (t2, t3))):
        total = (a[...].astype(F32) + b[...].astype(F32)).astype(BF)
        at = pl.multiple_of((where[1] ^ r) * block, LANES)
        for q in range(queries):
            tiles[q, :, pl.ds(at, block)] = total[q * per : (q + 1) * per]
    sums = jnp.sum(score[:, :1, :], axis=0)
    train = scores.shape[1]
    for q in range(queries):
        scores[q : q + 1, :] = sums[:, q * train : (q + 1) * train]


def final(where, parts, score, queries, train):
    own, block = parts[0].shape
    return pl.pallas_call(
        final_body,
        out_shape=(
            jax.ShapeDtypeStruct((queries, own // queries, 2 * block), BF),
            jax.ShapeDtypeStruct((queries, train), F32),
        ),
        in_specs=[SMEM_SPEC, *([VMEM_SPEC] * 5)],
        out_specs=(VMEM_SPEC, VMEM_SPEC),
        compiler_params=params(3),
        name="final",
    )(where, *parts, score)


def shards(
    basis_out,
    corrected,
    factor_table,
    block_ids,
    basis_in,
    query_ids,
    u_pool,
    v_pool,
    train_ids,
    x_pool,
    delta_pool,
):
    n_z, n_in = lax.axis_size("z"), lax.axis_size(IN)
    z, xh, c = lax.axis_index("z"), lax.axis_index("xh"), lax.axis_index("c")
    in_pos = lax.axis_index(IN)
    queries, train = query_ids.shape[0], train_ids.shape[0]
    _, local_rows, block = basis_in.shape
    width = -(-(block // 2) // LANES) * LANES
    where = jnp.stack([z, xh, in_pos, c]).astype(jnp.int32)

    packed = pack(where, train_ids, basis_in, x_pool[:, 0], delta_pool[:, 0], width)
    parts = (
        packed[0],
        swap(packed[1], "c"),
        swap(packed[2], "xh"),
        swap(packed[3], QUAD, 3),
    )
    rows = corrected.shape[0]
    ends = (0, 3 * rows // 8, 3 * rows // 4, rows)
    far = [
        inverse_block(where, corrected, block, 1, block, 1, a, b)[0]
        for a, b in zip(ends[:-1], ends[1:])
    ]
    partial = left_part(query_ids, jnp.transpose(u_pool, (0, 2, 1)), basis_out, n_in)
    own = arrange(where, (after(packed[0], far[0], partial), *parts[1:]), local_rows, train)
    near = inverse_block(where, corrected, block, 0, width, 2)
    near = (near[0], swap(near[1], "c"))

    ahead, behind = [shift(own, 1)], [shift(own, -1)]
    far[0] = swap(far[0], "xh")
    spread, window = left_sum(exchange(partial, IN))
    up, down = after((ahead[0], behind[0]), spread)
    far[1] = swap(after(far[1], ahead[0], spread), "xh")
    ahead.append(shift(up, 1))
    behind.append(shift(down, -1))
    left = exchange(spread, IN).reshape(-1, basis_out.shape[1])
    up, down, left = after((ahead[1], behind[1], left), far[0])
    ahead.append(shift(up, 1))
    behind.append(shift(down, -1))
    up = after(ahead[2], behind[2], far[1])
    ahead.append(shift(up, 1))
    far[2] = swap(after(far[2], left), "xh")
    left_x, window_x = swap(left, "xh"), swap(window, "xh")
    lefts = (left, swap(left, "c"))
    windows = (window, swap(window, "c"))
    chunks = (own, *ahead, *behind[::-1])

    basis, right, tokens, delta = rotate(
        where, query_ids, jnp.transpose(v_pool, (0, 2, 1)), chunks, block
    )
    so_far = back_first(right, lefts, windows, near, queries)
    left_x, window_x, *far = after((left_x, window_x, *far), so_far)
    far = halves(where, far, width)
    far = (left_x, swap(left_x, "c"), window_x, swap(window_x, "c"), far[0], swap(far[1], "c"))
    parts = back(where, block_ids, so_far, factor_table, right, far, n_z)
    score = score_part(parts, tokens, delta, queries, train)
    for axis, mask in (("c", 1), ("xl", 1), ("y", 1), ("y", 2), ("xh", 1)):
        score = score + swap(score, axis, mask)
    score = jnp.broadcast_to(score, (n_z, 8, LANES))
    parts, score, basis = after((exchange(parts, "z"), score, stage(score, basis)))
    parts = tile_part(where, parts, basis, queries)
    score = exchange(score, "z")
    parts = (
        parts[0],
        swap(parts[1], "c"),
        swap(parts[2], "xh"),
        swap(parts[3], QUAD, 3),
    )
    return final(where, parts, score, queries, train)


def solution(mesh):
    split = Mesh(mesh.devices.reshape(8, 2, 2, 4, 2), ("z", "xh", "c", "y", "xl"))
    return jax.shard_map(
        shards,
        mesh=split,
        in_specs=(
            P(IN, OUT),
            P(OUT, IN),
            P(),
            P(),
            P(IN, OUT, None),
            P(),
            P(None, IN, None),
            P(None, IN, None),
            P(),
            P(None, OUT, IN),
            P(None, OUT, None),
        ),
        out_specs=(P(None, OUT, IN), P()),
        check_vma=False,
    )
```
